256 devices in a mesh: seq: 64 (over x, y, z_lo), head: 4 (over z_hi, core).
Axes of the slice: x: 4, y: 4, z: 8 (z_hi: 2, z_lo: 4; z = z_hi * 4 + z_lo), core: 2. Of those that a mesh axis runs over, the one named last changes fastest.
Arguments:
- normed_input: bfloat16 [8192, 2304], P('seq'), may hold values from -16 to 16
- stored_queries: bfloat16 [8192, 2048], P('seq', 'head'), may hold values from -50 to 50
- stored_keys: bfloat16 [8192, 1024], P('seq', 'head'), may hold values from -4 to 4
- stored_values: bfloat16 [8192, 1024], P('seq', 'head'), may hold values from -6 to 6
- query_weight: bfloat16 [2304, 2048], P(None, 'head'), may hold values from -0.125 to 0.125
- key_matrix: bfloat16 [2304, 1024], P(None, 'head'), may hold values from -0.125 to 0.125
- value_matrix: bfloat16 [2304, 1024], P(None, 'head'), may hold values from -0.125 to 0.125
- output_weight: bfloat16 [2048, 2304], P('head'), may hold values from -0.125 to 0.125
- out_cotangent: bfloat16 [8192, 2304], P('seq'), may hold values from -128 to 128
Outputs:
- grad_input: bfloat16 [8192, 2304], P('seq', 'head')
- grad_wvalue: float32 [2304, 1024], P('seq', 'head')
- grad_woutput: float32 [2048, 2304], P('head', 'seq')
The draws below stay inside these ranges and needn't reach their ends.
All inputs are finite; a program needn't handle non-finite values.
Results may differ from the reference program's by a relative error of at most 0.033.
Values may be sent and summed in bfloat16 or wider, within the bound.
A program may use at most 128 MiB of HBM per device.

```python
import jax
import jax.numpy as jnp
from jax import lax

MODEL_DIMENSION = 2304
QUERY_HEADS = 16
KEY_VALUE_HEADS = 8
HEAD_SIZE = 128
WINDOW_LENGTH = 4096
BLOCK_TOKENS = 128
QUERIES_PER_KEY = 2
SEQUENCE_TOKENS = 8192


def paired_fields(key):
    query_key, key_random_seed = jax.random.split(jax.random.fold_in(key, 11))
    key_base_offset = jnp.clip(jax.random.normal(key_random_seed, (SEQUENCE_TOKENS, KEY_VALUE_HEADS * HEAD_SIZE), jnp.float32), -4.0, 4.0)
    query_base = jnp.clip(jax.random.normal(query_key, (SEQUENCE_TOKENS, QUERY_HEADS * HEAD_SIZE), jnp.float32), -4.0, 4.0)
    return (query_base, key_base_offset)


def draw_stored_queries(key, part):
    return paired_fields(key)[0].astype(jnp.bfloat16)


def draw_stored_keys(key, part):
    return paired_fields(key)[1].astype(jnp.bfloat16)


def with_spikes(result, own_key, source, target, shards_of, factor):
    def block_of(dim):
        return (jnp.arange(result.shape[dim]) // (result.shape[dim] // shards_of)).reshape((-1,) + (1,) * (result.ndim - 1 - dim))

    one_side = jax.random.permutation(own_key, shards_of)[block_of(target)]
    far = (block_of(target) + shards_of // 2) % shards_of
    return jnp.where((block_of(source) == one_side) | (block_of(source) == far), factor * result, result)


def shard_levels(own_key, extent, cuts, least, top_value):
    def one(dim, shards_of):
        steps = jax.random.uniform(jax.random.fold_in(jax.random.fold_in(own_key, 6), dim), (shards_of,), jnp.float32, least / len(cuts), top_value / len(cuts))
        return jnp.repeat(jnp.exp(steps), extent[dim] // shards_of).reshape((-1,) + (1,) * (len(extent) - dim - 1))

    level = one(*cuts[0])
    for cut in cuts[1:]:
        level = level * one(*cut)
    return level


def gaussian(rng, extent, scale, most, cuts=(), held_as=jnp.bfloat16):
    array = scale * jax.random.normal(rng, extent, jnp.float32)
    if cuts:
        array = array * shard_levels(rng, extent, cuts, -0.22, 0.18)
    return jnp.clip(array, -most, most).astype(held_as)


def noise_with(key, dims, deviation, reach, shards, heavy, kind=jnp.bfloat16):
    result = deviation * jax.random.normal(key, dims, jnp.float32)
    if shards:
        result = result * shard_levels(key, dims, shards, -0.22, 0.18)
    return jnp.clip(with_spikes(result, jax.random.fold_in(key, 3), *heavy), -reach, reach).astype(kind)


def setup_inputs(seed: int = 0) -> dict:
    keys = jax.random.split(jax.random.key(seed), 10)
    normed_input = noise_with(keys[0], (SEQUENCE_TOKENS, MODEL_DIMENSION), 1.0, 16.0, ((0, 64),), (0, 1, 64, 4.0))
    stored_queries = draw_stored_queries(jax.random.fold_in(keys[9], 71), 0)
    stored_keys = draw_stored_keys(jax.random.fold_in(keys[9], 71), 0)
    stored_values = gaussian(keys[3], (SEQUENCE_TOKENS, KEY_VALUE_HEADS * HEAD_SIZE), 1.0, 6.0, ((0, 64), (1, 4)))
    query_weight = gaussian(keys[4], (MODEL_DIMENSION, QUERY_HEADS * HEAD_SIZE), MODEL_DIMENSION ** -0.5, 0.125, ((1, 4),))
    key_matrix = gaussian(keys[5], (MODEL_DIMENSION, KEY_VALUE_HEADS * HEAD_SIZE), MODEL_DIMENSION ** -0.5, 0.125, ((1, 4),))
    value_matrix = gaussian(keys[6], (MODEL_DIMENSION, KEY_VALUE_HEADS * HEAD_SIZE), MODEL_DIMENSION ** -0.5, 0.125, ((1, 4),))
    output_weight = gaussian(keys[7], (QUERY_HEADS * HEAD_SIZE, MODEL_DIMENSION), MODEL_DIMENSION ** -0.5, 0.125, ((0, 4),))
    out_cotangent = noise_with(keys[8], (SEQUENCE_TOKENS, MODEL_DIMENSION), 8.0, 128.0, ((0, 64),), (0, 1, 64, 4.0))
    return dict(normed_input=normed_input, stored_queries=stored_queries, stored_keys=stored_keys, stored_values=stored_values, query_weight=query_weight, key_matrix=key_matrix, value_matrix=value_matrix, output_weight=output_weight, out_cotangent=out_cotangent)


logit_scale = 1.0 / 12.0


def reference(normed_input, stored_queries, stored_keys, stored_values, query_weight, key_matrix, value_matrix, output_weight, out_cotangent):
    token_positions = normed_input.shape[0]
    blocks = token_positions // BLOCK_TOKENS
    window_extent = WINDOW_LENGTH + BLOCK_TOKENS
    output_gradient = jnp.dot(out_cotangent, output_weight.T, preferred_element_type=jnp.float32).astype(jnp.bfloat16)
    empty_rows = jnp.zeros((WINDOW_LENGTH, KEY_VALUE_HEADS * HEAD_SIZE), stored_keys.dtype)
    padded_keys = jnp.concatenate([empty_rows, stored_keys], axis=0)
    padded_values = jnp.concatenate([empty_rows, stored_values], axis=0)

    def one_block(carry_pair, block_index):
        first_row_offset = (block_index * BLOCK_TOKENS).astype(jnp.int32)
        key_running_total, value_running_total = carry_pair
        block_of_queries = lax.dynamic_slice_in_dim(stored_queries, first_row_offset, BLOCK_TOKENS, 0).reshape(BLOCK_TOKENS, KEY_VALUE_HEADS, QUERIES_PER_KEY, HEAD_SIZE).astype(jnp.float32)
        block_gradient = lax.dynamic_slice_in_dim(output_gradient, first_row_offset, BLOCK_TOKENS, 0).reshape(BLOCK_TOKENS, KEY_VALUE_HEADS, QUERIES_PER_KEY, HEAD_SIZE).astype(jnp.float32)
        block_of_keys = lax.dynamic_slice_in_dim(padded_keys, first_row_offset, window_extent, 0).reshape(window_extent, KEY_VALUE_HEADS, HEAD_SIZE).astype(jnp.float32)
        block_of_values = lax.dynamic_slice_in_dim(padded_values, first_row_offset, window_extent, 0).reshape(window_extent, KEY_VALUE_HEADS, HEAD_SIZE).astype(jnp.float32)
        query_pos = first_row_offset + jnp.arange(BLOCK_TOKENS, dtype=jnp.int32)
        key_pos = first_row_offset - WINDOW_LENGTH + jnp.arange(window_extent, dtype=jnp.int32)
        pos_gap = query_pos[:, None] - key_pos[None, :]
        allowed = (pos_gap >= 0) & (pos_gap < WINDOW_LENGTH) & (key_pos >= 0)[None, :]
        attention_logits = logit_scale * jnp.einsum("eial,cil->iaec", block_of_queries, block_of_keys)
        masked = jnp.where(allowed[None, None], attention_logits, -jnp.inf)
        row_top = jnp.max(masked, axis=-1, keepdims=True)
        exp_scores = jnp.exp(masked - row_top)
        attn_prob = exp_scores / jnp.sum(exp_scores, axis=-1, keepdims=True)
        probability_halfwidth = attn_prob.astype(jnp.bfloat16)
        attention_output = jnp.einsum("kbxh,hkj->xkbj", probability_halfwidth.astype(jnp.float32), block_of_values).astype(jnp.bfloat16)
        row_delta = jnp.sum(block_gradient * attention_output.astype(jnp.float32), axis=-1)
        row_delta = jnp.transpose(row_delta, (1, 2, 0))
        probability_gradient = jnp.einsum("eial,cil->iaec", block_gradient, block_of_values)
        score_gradient = (attn_prob * (probability_gradient - row_delta[..., None])).astype(jnp.bfloat16).astype(jnp.float32)
        query_gradient = (logit_scale * jnp.einsum("kbxh,hkj->xkbj", score_gradient, block_of_keys)).astype(jnp.bfloat16)
        key_partial = logit_scale * jnp.einsum("ozpn,pozw->now", score_gradient, block_of_queries)
        value_partial = jnp.einsum("ozpn,pozw->now", probability_halfwidth.astype(jnp.float32), block_gradient)
        previous_key = lax.dynamic_slice_in_dim(key_running_total, first_row_offset, window_extent, 0)
        previous_value = lax.dynamic_slice_in_dim(value_running_total, first_row_offset, window_extent, 0)
        key_running_total = lax.dynamic_update_slice_in_dim(key_running_total, previous_key + key_partial.reshape(window_extent, KEY_VALUE_HEADS * HEAD_SIZE), first_row_offset, 0)
        value_running_total = lax.dynamic_update_slice_in_dim(value_running_total, previous_value + value_partial.reshape(window_extent, KEY_VALUE_HEADS * HEAD_SIZE), first_row_offset, 0)
        return (key_running_total, value_running_total), (attention_output.reshape(BLOCK_TOKENS, QUERY_HEADS * HEAD_SIZE), query_gradient.reshape(BLOCK_TOKENS, QUERY_HEADS * HEAD_SIZE))

    initial_carry_pair = (jnp.zeros((WINDOW_LENGTH + token_positions, KEY_VALUE_HEADS * HEAD_SIZE), jnp.float32), jnp.zeros((WINDOW_LENGTH + token_positions, KEY_VALUE_HEADS * HEAD_SIZE), jnp.float32))
    (key_running_total, value_running_total), (attention_output, query_gradient) = lax.scan(one_block, initial_carry_pair, jnp.arange(blocks, dtype=jnp.int32))
    attention_output = attention_output.reshape(token_positions, QUERY_HEADS * HEAD_SIZE)
    query_gradient = query_gradient.reshape(token_positions, QUERY_HEADS * HEAD_SIZE)
    grad_key = key_running_total[WINDOW_LENGTH:].astype(jnp.bfloat16)
    grad_value = value_running_total[WINDOW_LENGTH:].astype(jnp.bfloat16)
    grad_input = jnp.dot(query_gradient, query_weight.T, preferred_element_type=jnp.float32)
    grad_input = grad_input + jnp.dot(grad_key, key_matrix.T, preferred_element_type=jnp.float32)
    grad_input = (grad_input + jnp.dot(grad_value, value_matrix.T, preferred_element_type=jnp.float32)).astype(jnp.bfloat16)
    grad_wvalue = jnp.dot(normed_input.T, grad_value, preferred_element_type=jnp.float32)
    grad_woutput = jnp.dot(attention_output.T, out_cotangent, preferred_element_type=jnp.float32)
    return grad_input, grad_wvalue, grad_woutput
```

```python
import functools
import math

import jax
import jax.numpy as jnp
from jax import lax
from jax.experimental import pallas as pl
from jax.experimental.pallas import tpu as pltpu
from jax.sharding import PartitionSpec as P

MESH = pl.DeviceIdType.MESH
F32 = jnp.float32
BF16 = jnp.bfloat16
LOGIT_SCALE = 1.0 / 12.0
EXP2_SCALE = LOGIT_SCALE * math.log2(math.e)
NEG = -1e30
T = 128
D = 128
SLOTS = 9
ROWS = 1024
WIN = 640
COLS = 576
SPLIT = 5
KEYS = 256
NT = (((1,), (1,)), ((), ()))


def dot(a, b):
    return jnp.dot(a, b, preferred_element_type=F32)


def place():
    i = lax.axis_index("seq")
    h = lax.axis_index("head")
    x = lax.div(i, 16)
    y = lax.rem(lax.div(i, 4), 4)
    z = lax.rem(i, 4)
    return i, h, x, y, z


def layer_kernel(
    x_hbm, q_hbm, k_hbm, v_hbm, wq_hbm, wk_hbm, wv_hbm, wo_hbm, cot_hbm,
    gi_o, gwv_o, gwo_o,
    attn_o, gq_o, gk_o, gv_o, wq, wk, wv, win, winT, ag, gvg, po, pv, yo, yv, zso, zsv, zpo, zpv, zio, ziv, tb, hin,
    kv, qg, dog, og, cot, wo, q2, do2, qT, doT, sbuf, dpbuf, pb_s, ds_s, ms, st, st_in, fin,
    oT, dqT, osend, oin, dqsend, dqin, dkv, rbuf, csend, cin, finkv, pin,
    lsem, pair_s, pair_r, q_s, q_r, do_s, do_r, kvx_s, kvy_s, kv_r, st_s, st_r, o_s, o_r, dq_s, dq_r,
    rb_s, rb_r, c_s, c_r, f_s, f_r,
    w_s, w_r, ag_s, ag_r, gg_s, gg_r, yo_s, yo_r, yv_s, yv_r, zo_s, zo_r, zv_s, zv_r, h_s, h_r,
):
    i, h, x, y, z = place()
    e, f = lax.rem(z, 2), lax.div(z, 2)
    S = x * 4 + y

    def dev(x_, y_, z_):
        return (x_ * 16 + y_ * 4 + z_, h)

    def wrap(a):
        return lax.rem(a + 4, 4)

    def remote(src, dst, s, r, to):
        return pltpu.make_async_remote_copy(
            src_ref=src, dst_ref=dst, send_sem=s, recv_sem=r, device_id=to, device_id_type=MESH
        )

    erow = pl.multiple_of(e * T, T)
    prow = pl.multiple_of((1 - e) * T, T)
    ecol2 = pl.multiple_of(e * 256, 256)
    c_wo = pltpu.make_async_copy(wo_hbm, wo, lsem.at[0])
    c_cot = pltpu.make_async_copy(cot_hbm, cot, lsem.at[1])
    c_k = pltpu.make_async_copy(k_hbm.at[:, pl.ds(erow, D)], kv.at[0, 0, pl.ds(erow, T), :], lsem.at[2])
    c_v = pltpu.make_async_copy(v_hbm.at[:, pl.ds(erow, D)], kv.at[0, 1, pl.ds(erow, T), :], lsem.at[3])
    c_q = pltpu.make_async_copy(q_hbm.at[:, pl.ds(ecol2, 256)], qg.at[z], lsem.at[4])
    for c in (c_wo, c_cot, c_k, c_v, c_q):
        c.start()

    def window(xt):
        return pl.ds(pl.multiple_of(lax.div(9 * xt, 2) * 128, 128), WIN)

    c_win = [
        pltpu.make_async_copy(src.at[:, window(x)], win.at[n, x], lsem.at[5 + n]) for n, src in ((0, x_hbm), (1, cot_hbm))
    ]
    c_w = [pltpu.make_async_copy(src, dst, lsem.at[7 + n]) for n, (src, dst) in enumerate(((wq_hbm, wq), (wk_hbm, wk), (wv_hbm, wv)))]

    bar = pltpu.get_barrier_semaphore()
    for r in (1, 2, 3):
        for to in (dev(x, y, wrap(z + r)), dev(x, wrap(y + r), z), dev(wrap(x + r), y, z)):
            pl.semaphore_signal(bar, inc=1, device_id=to, device_id_type=MESH)
    hc = h + 1 - 2 * lax.rem(h, 2)
    hz = lax.rem(h + 2, 4)
    for to in ((i, hc), (i, hz)):
        pl.semaphore_signal(bar, inc=1, device_id=to, device_id_type=MESH)
    pl.semaphore_wait(bar, 11)

    zp = z + 1 - 2 * e
    pair = [
        remote(src.at[:, pl.ds(prow, D)], kv.at[0, n, pl.ds(erow, T), :], pair_s.at[n], pair_r.at[n], dev(x, y, zp))
        for n, src in ((0, k_hbm), (1, v_hbm))
    ]
    for c in pair:
        c.start()

    def gathered(src_of, buf, s, r_):
        copies = []
        for r in (1, 2, 3):
            zt = wrap(z + r)
            copies.append(remote(src_of(zt), buf.at[z], s.at[r - 1], r_.at[r - 1], dev(x, y, zt)))
        return copies

    qcopies = gathered(
        lambda zt: q_hbm.at[:, pl.ds(pl.multiple_of(lax.rem(zt, 2) * 256, 256), 256)], qg, q_s, q_r
    )
    for c in qcopies:
        c.start()

    c_wo.wait()
    c_cot.wait()
    grad = lax.dot_general(cot[...], wo[...], NT, preferred_element_type=F32).astype(BF16)
    og[0] = grad[:, :256]
    og[1] = grad[:, 256:]
    docopies = gathered(lambda zt: og.at[lax.rem(zt, 2)], dog, do_s, do_r)
    for c in docopies:
        c.start()
    dog[z] = og[e]

    c_k.wait()
    c_v.wait()
    for c in pair:
        c.wait_recv()

    def fwd_x(src, dst):
        return remote(kv.at[src], kv.at[dst], kvx_s.at[dst // 8], kv_r.at[dst], dev(wrap(x + 1), y, z))

    def fwd_y(r, kind):
        yt = wrap(y + r)
        up = yt > y
        if kind == 0:
            src, dst = 4, 4 + yt - y
        else:
            src, dst = jnp.where(up, 0, 8), jnp.where(up, yt - y, 8 + yt - y)
        return remote(kv.at[src], kv.at[dst], kvy_s.at[kind * 3 + r - 1], kv_r.at[dst], dev(x, yt, z))

    @pl.when(x < 3)
    def _():
        fwd_x(0, 4).start()

    for r in (1, 2, 3):
        @pl.when(y + r < 4)
        def _():
            fwd_y(r, 1).start()

    def recv_slot(d):
        remote(kv.at[d], kv.at[d], kvx_s.at[0], kv_r.at[d], dev(wrap(x + 1), y, z)).wait_recv()

    @pl.when(x >= 1)
    def _():
        recv_slot(4)
        for r in (1, 2, 3):
            fwd_y(r, 0).start()

    @pl.when((x >= 1) & (x < 3))
    def _():
        fwd_x(4, 8).start()

    wcopies = []
    for r in (1, 2, 3):
        xt = wrap(x + r)
        for n, src in ((0, x_hbm), (1, cot_hbm)):
            wcopies.append(
                remote(src.at[:, window(xt)], win.at[n, x], w_s.at[n, r - 1], w_r.at[n, r - 1], dev(xt, y, z))
            )
    for c in wcopies + c_win + c_w:
        c.start()

    c_q.wait()
    for r in (1, 2, 3):
        qcopies[r - 1].wait_recv()
    for r in (1, 2, 3):
        docopies[r - 1].wait_recv()

    @pl.loop(0, 4)
    def _(zz):
        for j in range(2):
            rows = pl.ds(pl.multiple_of(j * 512 + zz * T, T), T)
            qb = qg[zz, :, j * D : (j + 1) * D]
            q2[rows, :] = qb
            qT[:, rows] = qb.T
            db = dog[zz, :, j * D : (j + 1) * D]
            do2[rows, :] = db
            doT[:, rows] = db.T

    @pl.when(x >= 2)
    def _():
        recv_slot(8)
        for r in (1, 2, 3):
            @pl.when(y + r >= 4)
            def _():
                fwd_y(r, 1).start()

    st[...] = jnp.concatenate([jnp.full((1, ROWS), NEG, F32), jnp.zeros((7, ROWS), F32)], axis=0)
    oT[...] = jnp.zeros_like(oT)
    dqT[...] = jnp.zeros_like(dqT)

    def slot_of(kind, r):
        if kind == 0:
            return 4 + jnp.where(r <= y, r, r - 4)
        return jnp.where(r <= y, r, r + 4)

    @pl.loop(0, SLOTS)
    def _(t):
        d = jnp.where(
            t < 2, t * 4, jnp.where(t == 8, 8, jnp.where(t < 5, slot_of(1, t - 1), slot_of(0, t - 4)))
        )

        @pl.when(S >= d)
        def _():
            @pl.when((t >= 2) & (t < 8))
            def _():
                recv_slot(d)

            kd = kv[d, 0]
            vd = kv[d, 1]
            vt = vd.T
            low = jnp.where(d == 0, 0, -100000)
            high = jnp.where(d == 8, 0, 100000)
            for c in range(4):
                cs = slice(c * 256, (c + 1) * 256)
                s = dot(kd, qT[:, cs])
                gap = (
                    lax.broadcasted_iota(jnp.int32, (KEYS, 256), 1)
                    - lax.broadcasted_iota(jnp.int32, (KEYS, 256), 0)
                    + ((c % 2) * 256 - f * 256)
                )
                s = jnp.where((gap >= low) & (gap < high), s, NEG)
                before = st[0:1, cs]
                top = jnp.maximum(before, jnp.max(s, axis=0, keepdims=True))
                p = jnp.exp2((s - top) * EXP2_SCALE)
                keep = jnp.exp2((before - top) * EXP2_SCALE)
                dp = dot(vd, doT[:, cs])
                st[0:1, cs] = top
                st[1:2, cs] = st[1:2, cs] * keep + jnp.sum(p, axis=0, keepdims=True)
                st[2:3, cs] = st[2:3, cs] * keep + jnp.sum(p * dp, axis=0, keepdims=True)
                ms[d, 0:1, cs] = top
                sbuf[d, :, cs] = p
                dpbuf[d, :, cs] = dp
                oT[:, cs] = oT[:, cs] * keep + dot(vt, p.astype(BF16))

    stat = remote(st, st_in, st_s, st_r, dev(x, y, wrap(z + 2)))
    stat.start()
    stat.wait()
    top = jnp.maximum(st[0:1, :], st_in[0:1, :])
    mine = jnp.exp2((st[0:1, :] - top) * EXP2_SCALE)
    other = jnp.exp2((st_in[0:1, :] - top) * EXP2_SCALE)
    inv = 1.0 / (st[1:2, :] * mine + st_in[1:2, :] * other)
    fin[0:1, :] = top
    fin[1:2, :] = inv
    fin[2:3, :] = (st[2:3, :] * mine + st_in[2:3, :] * other) * inv
    oT[...] = oT[...] * (mine * inv)

    def spread(srcT, factor, sendbuf, inbuf, s, r_):
        for j in range(2):
            for zz in range(4):
                piece = srcT[:, j * 512 + zz * T : j * 512 + (zz + 1) * T]
                sendbuf[zz, :, j * D : (j + 1) * D] = (piece * factor).T.astype(BF16)
        copies = []
        for r in (1, 2, 3):
            zt = wrap(z + r)
            copies.append(remote(sendbuf.at[zt], inbuf.at[z], s.at[r - 1], r_.at[r - 1], dev(x, y, zt)))
        for c in copies:
            c.start()
        inbuf[z] = sendbuf[z]
        return copies

    ocopies = spread(oT, 1.0, osend, oin, o_s, o_r)

    def grad_slot(d):
        w = jnp.exp2((ms[d, 0:1, :] - fin[0:1, :]) * EXP2_SCALE) * fin[1:2, :]
        kt = kv[d, 0].T
        for c in range(4):
            cs = slice(c * 256, (c + 1) * 256)
            p = sbuf[d, :, cs] * w[:, cs]
            pb_s[:, cs] = p.astype(BF16)
            ds = (p * (dpbuf[d, :, cs] - fin[2:3, cs])).astype(BF16)
            ds_s[:, cs] = ds
            dqT[:, cs] += dot(kt, ds)
        dkv[d, 0] = (LOGIT_SCALE * dot(ds_s[...], q2[...])).astype(BF16)
        dkv[d, 1] = dot(pb_s[...], do2[...]).astype(BF16)

    def back_y(kind, r):
        d = slot_of(kind, r)
        n = kind * 3 + r - 1
        return remote(dkv.at[d], rbuf.at[n], rb_s.at[n], rb_r.at[n], dev(x, wrap(y - r), z))

    def grad_step(t):
        d = jnp.where(
            t >= 6, 8 - (t - 6) * 4, jnp.where(t < 3, slot_of(0, t + 1), slot_of(1, t - 2))
        )

        @pl.when(S >= d)
        def _():
            grad_slot(d)

            @pl.when(t < 6)
            def _():
                r = lax.rem(t, 3) + 1
                remote(dkv.at[d], rbuf.at[t], rb_s.at[t], rb_r.at[t], dev(x, wrap(y - r), z)).start()

    pl.loop(0, SPLIT)(grad_step)

    def over_x(src, dst, s, r_):
        return [remote(src, dst, s.at[r - 1], r_.at[r - 1], dev(wrap(x + r), y, z)) for r in (1, 2, 3)]

    for c in ocopies:
        c.wait_recv()
    for n in range(2):
        attn_o[n] = (oin[n].astype(F32) + oin[n + 2].astype(F32)).astype(BF16)
    agcopies = over_x(attn_o, ag.at[:, x], ag_s, ag_r)
    for c in agcopies:
        c.start()
    ag[:, x] = attn_o[...]

    pl.loop(SPLIT, SLOTS)(grad_step)

    dqcopies = spread(dqT, LOGIT_SCALE, dqsend, dqin, dq_s, dq_r)

    def recv_back(n):
        remote(rbuf.at[n], rbuf.at[n], rb_s.at[n], rb_r.at[n], dev(x, wrap(y + 1), z)).wait_recv()

    chain8 = remote(csend.at[0], cin.at[0], c_s.at[0], c_r.at[0], dev(wrap(x - 1), y, z))
    chain4 = remote(csend.at[1], cin.at[1], c_s.at[1], c_r.at[1], dev(wrap(x - 1), y, z))

    for c in c_win:
        c.wait()
    for c in wcopies:
        c.wait_recv()

    @pl.loop(0, 4)
    def _(xx):
        for n in range(2):
            for b in range(WIN // 128):
                cols = slice(b * 128, (b + 1) * 128)
                winT[n, cols, pl.ds(pl.multiple_of(xx * T, T), T)] = win[n, xx, :, cols].T

    for r in (1, 2, 3):
        @pl.when((y + r < 4) | (x >= 2))
        def _():
            recv_back(3 + r - 1)

    @pl.when(x >= 2)
    def _():
        for n in range(2):
            acc = dkv[8, n].astype(F32)
            for r in (1, 2, 3):
                acc = acc + jnp.where(y + r >= 4, rbuf[3 + r - 1, n].astype(F32), 0.0)
            csend[0, n] = acc.astype(BF16)
        chain8.start()

    @pl.when(x >= 1)
    def _():
        for r in (1, 2, 3):
            recv_back(r - 1)

        @pl.when(x < 3)
        def _():
            chain8.wait_recv()

        for n in range(2):
            acc = dkv[4, n].astype(F32)
            for r in (1, 2, 3):
                acc = acc + rbuf[r - 1, n].astype(F32)
            acc = acc + jnp.where(x < 3, cin[0, n].astype(F32), 0.0)
            csend[1, n] = acc.astype(BF16)
        chain4.start()

    off = pl.multiple_of(64 * lax.rem(x, 2), 16)

    def over_y(src, buf, s, r_):
        copies = []
        for r in (1, 2, 3):
            yt = wrap(y + r)
            rows = pl.ds(pl.multiple_of(off + 144 * yt, 16), 144)
            copies.append(remote(src.at[rows, :], buf.at[r - 1], s.at[r - 1], r_.at[r - 1], dev(x, yt, z)))
        return copies

    for c in agcopies:
        c.wait_recv()
    for n in range(2):
        po[:, n * 256 : (n + 1) * 256] = dot(winT[1], ag[n].reshape(4 * T, 256)).astype(BF16)
    yocopies = over_y(po, yo, yo_s, yo_r)
    for c in yocopies:
        c.start()

    @pl.when(x < 3)
    def _():
        chain4.wait_recv()

    for n in range(2):
        acc = dkv[0, n].astype(F32)
        for r in (1, 2, 3):
            acc = acc + jnp.where(y + r < 4, rbuf[3 + r - 1, n].astype(F32), 0.0)
        acc = acc + jnp.where(x < 3, cin[1, n].astype(F32), 0.0)
        finkv[n] = acc.astype(BF16)

    swap = [
        remote(finkv.at[n, pl.ds(prow, T), :], pin.at[n], f_s.at[n], f_r.at[n], dev(x, y, zp)) for n in range(2)
    ]
    for c in swap:
        c.start()

    for c in dqcopies:
        c.wait_recv()
    for n in range(2):
        gq_o[n] = (dqin[n].astype(F32) + dqin[n + 2].astype(F32)).astype(BF16)
    for c in c_w:
        c.wait()
    for c in swap:
        c.wait_recv()
    for n, out in ((0, gk_o), (1, gv_o)):
        out[e] = finkv[n, pl.ds(erow, T), :]
        out[1 - e] = pin[n]
    ggcopies = over_x(gv_o, gvg.at[:, x], gg_s, gg_r)
    for c in ggcopies:
        c.start()
    gvg[:, x] = gv_o[...]

    def terms(hh):
        rows = pl.ds(pl.multiple_of(COLS * hh, 16), COLS)
        acc = jnp.zeros((T, COLS), F32)
        for n in range(2):
            acc = acc + lax.dot_general(gq_o[n], wq[rows, n * 256 : (n + 1) * 256], NT, preferred_element_type=F32)
            acc = acc + lax.dot_general(gk_o[n], wk[rows, n * D : (n + 1) * D], NT, preferred_element_type=F32)
            acc = acc + lax.dot_general(gv_o[n], wv[rows, n * D : (n + 1) * D], NT, preferred_element_type=F32)
        return acc

    hzc = lax.rem(hc + 2, 4)
    tb[0] = terms(hzc).astype(BF16)
    far = remote(tb.at[0], hin.at[0], h_s.at[0], h_r.at[0], (i, hc))
    far.start()
    mine_far = terms(hz)
    far.wait_recv()
    tb[1] = (mine_far + hin[0].astype(F32)).astype(BF16)
    across = remote(tb.at[1], hin.at[1], h_s.at[1], h_r.at[1], (i, hz))
    across.start()
    tb[2] = terms(hc).astype(BF16)
    near = remote(tb.at[2], hin.at[2], h_s.at[2], h_r.at[2], (i, hc))
    near.start()

    for c in ggcopies:
        c.wait_recv()
    for n in range(2):
        pv[:, n * D : (n + 1) * D] = dot(winT[0], gvg[n].reshape(4 * T, D)).astype(BF16)
    yvcopies = over_y(pv, yv, yv_s, yv_r)
    for c in yvcopies:
        c.start()

    def over_z(copies, own, buf, total_s, piece_s, in_s, s, r_):
        for c in copies:
            c.wait_recv()
        acc = own[pl.ds(pl.multiple_of(off + 144 * y, 16), 144), :].astype(F32)
        for r in range(3):
            acc = acc + buf[r].astype(F32)
        total_s[...] = acc
        for zz in range(4):
            piece_s[zz] = total_s[36 * zz : 36 * (zz + 1), :]
        out = []
        for r in (1, 2, 3):
            zt = wrap(z + r)
            out.append(remote(piece_s.at[zt], in_s.at[r - 1], s.at[r - 1], r_.at[r - 1], dev(x, y, zt)))
        for c in out:
            c.start()
        return out

    zocopies = over_z(yocopies, po, yo, zso, zpo, zio, zo_s, zo_r)
    mine_near = terms(h)
    zvcopies = over_z(yvcopies, pv, yv, zsv, zpv, ziv, zv_s, zv_r)

    for c in zocopies:
        c.wait_recv()
    acc = zpo[z]
    for r in range(3):
        acc = acc + zio[r]
    gwo_o[...] = acc
    near.wait_recv()
    across.wait_recv()
    gi_o[...] = (mine_near + hin[2].astype(F32) + hin[1].astype(F32)).astype(BF16)
    for c in zvcopies:
        c.wait_recv()
    acc = zpv[z]
    for r in range(3):
        acc = acc + ziv[r]
    gwv_o[...] = acc

    for c in (
        pair + qcopies + docopies + ocopies + dqcopies + swap + wcopies + agcopies + ggcopies
        + yocopies + yvcopies + zocopies + zvcopies + [far, across, near]
    ):
        c.wait_send()

    @pl.when(x < 3)
    def _():
        fwd_x(0, 4).wait_send()

    @pl.when((x >= 1) & (x < 3))
    def _():
        fwd_x(4, 8).wait_send()

    for r in (1, 2, 3):
        @pl.when((y + r < 4) | (x >= 2))
        def _():
            fwd_y(r, 1).wait_send()

        @pl.when(x >= 1)
        def _():
            fwd_y(r, 0).wait_send()
            back_y(0, r).wait_send()

        @pl.when((r <= y) | (x >= 2))
        def _():
            back_y(1, r).wait_send()

    @pl.when(x >= 2)
    def _():
        chain8.wait_send()

    @pl.when(x >= 1)
    def _():
        chain4.wait_send()


def layer(xn, q, k, v, wq, wk, wv, wo, cot):
    dma = pltpu.SemaphoreType.DMA
    vm = pltpu.VMEM
    return pl.pallas_call(
        layer_kernel,
        out_shape=(
            jax.ShapeDtypeStruct((T, COLS), BF16),
            jax.ShapeDtypeStruct((36, 256), F32),
            jax.ShapeDtypeStruct((36, 512), F32),
        ),
        in_specs=[pl.BlockSpec(memory_space=pl.ANY)] * 9,
        out_specs=tuple(pl.BlockSpec(memory_space=pltpu.VMEM) for _ in range(3)),
        scratch_shapes=[
            vm((2, T, 256), BF16),
            vm((2, T, 256), BF16),
            vm((2, T, D), BF16),
            vm((2, T, D), BF16),
            vm(wq.shape, BF16),
            vm(wk.shape, BF16),
            vm(wv.shape, BF16),
            vm((2, 4, T, WIN), BF16),
            vm((2, WIN, 4 * T), BF16),
            vm((2, 4, T, 256), BF16),
            vm((2, 4, T, D), BF16),
            vm((WIN, 512), BF16),
            vm((WIN, 256), BF16),
            vm((3, 144, 512), BF16),
            vm((3, 144, 256), BF16),
            vm((144, 512), F32),
            vm((144, 256), F32),
            vm((4, 36, 512), F32),
            vm((4, 36, 256), F32),
            vm((3, 36, 512), F32),
            vm((3, 36, 256), F32),
            vm((3, T, COLS), BF16),
            vm((3, T, COLS), BF16),
            vm((SLOTS, 2, KEYS, D), BF16),
            vm((4, T, 256), BF16),
            vm((4, T, 256), BF16),
            vm((2, T, 256), BF16),
            vm(cot.shape, BF16),
            vm(wo.shape, BF16),
            vm((ROWS, D), BF16),
            vm((ROWS, D), BF16),
            vm((D, ROWS), BF16),
            vm((D, ROWS), BF16),
            vm((SLOTS, KEYS, ROWS), F32),
            vm((SLOTS, KEYS, ROWS), F32),
            vm((KEYS, ROWS), BF16),
            vm((KEYS, ROWS), BF16),
            vm((SLOTS, 8, ROWS), F32),
            vm((8, ROWS), F32),
            vm((8, ROWS), F32),
            vm((8, ROWS), F32),
            vm((D, ROWS), F32),
            vm((D, ROWS), F32),
            vm((4, T, 256), BF16),
            vm((4, T, 256), BF16),
            vm((4, T, 256), BF16),
            vm((4, T, 256), BF16),
            vm((SLOTS, 2, KEYS, D), BF16),
            vm((6, 2, KEYS, D), BF16),
            vm((2, 2, KEYS, D), BF16),
            vm((2, 2, KEYS, D), BF16),
            vm((2, KEYS, D), BF16),
            vm((2, T, D), BF16),
            dma((10,)), dma((2,)), dma((2,)), dma((3,)), dma((3,)), dma((3,)), dma((3,)),
            dma((2,)), dma((6,)), dma((SLOTS,)), dma, dma, dma((3,)), dma((3,)), dma((3,)), dma((3,)),
            dma((6,)), dma((6,)), dma((2,)), dma((2,)), dma((2,)), dma((2,)),
            dma((2, 3)), dma((2, 3)), *([dma((3,))] * 14),
        ],
        compiler_params=pltpu.CompilerParams(
            collective_id=1, has_side_effects=True, vmem_limit_bytes=62 * 1024 * 1024
        ),
        name="layer",
    )(xn, q, k, v, wq, wk, wv, wo, cot)


def local(*args):
    grad_input, grad_wvalue, grad_woutput = layer(*args)
    return grad_input, grad_wvalue, grad_woutput.T


def solution(mesh):
    seq, both, cols, rows = P("seq", None), P("seq", "head"), P(None, "head"), P("head", None)
    return jax.shard_map(
        local,
        mesh=mesh,
        in_specs=(seq, both, both, both, cols, cols, cols, rows, seq),
        out_specs=(both, both, P("head", "seq")),
        check_vma=False,
    )
```

```python
import functools
import math

import jax
import jax.numpy as jnp
from jax import lax
from jax.experimental import pallas as pl
from jax.experimental.pallas import tpu as pltpu
from jax.sharding import PartitionSpec as P

MESH = pl.DeviceIdType.MESH
F32 = jnp.float32
BF16 = jnp.bfloat16
LOGIT_SCALE = 1.0 / 12.0
EXP2_SCALE = LOGIT_SCALE * math.log2(math.e)
NEG = -1e30
T = 128
D = 128
SLOTS = 9
ROWS = 1024
WIN = 640
COLS = 576
KEYS = 256
NT = (((1,), (1,)), ((), ()))


def dot(a, b):
    return jnp.dot(a, b, preferred_element_type=F32)


def place():
    i = lax.axis_index("seq")
    h = lax.axis_index("head")
    x = lax.div(i, 16)
    y = lax.rem(lax.div(i, 4), 4)
    z = lax.rem(i, 4)
    return i, h, x, y, z


def layer_kernel(
    x_hbm, q_hbm, k_hbm, v_hbm, wq_hbm, wk_hbm, wv_hbm, wo_hbm, cot_hbm,
    gi_o, gwv_o, gwo_o,
    attn_o, gq_o, gk_o, gv_o, wq, wk, wv, win, winT, ag, gvg, po, pv, yo, yv, zso, zsv, zpo, zpv, zio, ziv, tb, hin,
    facc, kv, qg, dog, og, cot, wo, q2, do2, qT, doT, sbuf, dpbuf, pb_s, ds_s, ms, st, st_in, fin,
    oT, dqT, osend, oin, dqsend, dqin, dkv, rbuf, csend, cin, finkv, pin,
    lsem, pair_s, pair_r, q_s, q_r, do_s, do_r, kvx_s, kvy_s, kv_r, st_s, st_r, o_s, o_r, dq_s, dq_r,
    rb_s, rb_r, c_s, c_r, f_s, f_r,
    fx_s, fx_r, w_s, w_r, ag_s, ag_r, gg_s, gg_r, yo_s, yo_r, yv_s, yv_r, zo_s, zo_r, zv_s, zv_r, h_s, h_r,
):
    i, h, x, y, z = place()
    e, f = lax.rem(z, 2), lax.div(z, 2)
    S = x * 4 + y

    def dev(x_, y_, z_):
        return (x_ * 16 + y_ * 4 + z_, h)

    def wrap(a):
        return lax.rem(a + 4, 4)

    def remote(src, dst, s, r, to):
        return pltpu.make_async_remote_copy(
            src_ref=src, dst_ref=dst, send_sem=s, recv_sem=r, device_id=to, device_id_type=MESH
        )

    erow = pl.multiple_of(e * T, T)
    prow = pl.multiple_of((1 - e) * T, T)
    ecol2 = pl.multiple_of(e * 256, 256)
    c_wo = pltpu.make_async_copy(wo_hbm, wo, lsem.at[0])
    c_cot = pltpu.make_async_copy(cot_hbm, cot, lsem.at[1])
    c_k = pltpu.make_async_copy(k_hbm.at[:, pl.ds(erow, D)], kv.at[0, 0, pl.ds(erow, T), :], lsem.at[2])
    c_v = pltpu.make_async_copy(v_hbm.at[:, pl.ds(erow, D)], kv.at[0, 1, pl.ds(erow, T), :], lsem.at[3])
    c_q = pltpu.make_async_copy(q_hbm.at[:, pl.ds(ecol2, 256)], qg.at[z], lsem.at[4])
    for c in (c_wo, c_cot, c_k, c_v, c_q):
        c.start()

    def window(xt):
        return pl.ds(pl.multiple_of(lax.div(9 * xt, 2) * 128, 128), WIN)

    c_win = [
        pltpu.make_async_copy(src.at[:, window(x)], win.at[n, x], lsem.at[5 + n]) for n, src in ((0, x_hbm), (1, cot_hbm))
    ]
    c_w = [pltpu.make_async_copy(src, dst, lsem.at[7 + n]) for n, (src, dst) in enumerate(((wq_hbm, wq), (wk_hbm, wk), (wv_hbm, wv)))]

    bar = pltpu.get_barrier_semaphore()
    for r in (1, 2, 3):
        for to in (dev(x, y, wrap(z + r)), dev(x, wrap(y + r), z), dev(wrap(x + r), y, z)):
            pl.semaphore_signal(bar, inc=1, device_id=to, device_id_type=MESH)
    hc = h + 1 - 2 * lax.rem(h, 2)
    hz = lax.rem(h + 2, 4)
    for to in ((i, hc), (i, hz)):
        pl.semaphore_signal(bar, inc=1, device_id=to, device_id_type=MESH)
    zp = z + 1 - 2 * e
    for r in (1, 2, 3):
        pl.semaphore_signal(bar, inc=1, device_id=dev(wrap(x + r), y, zp), device_id_type=MESH)
    pl.semaphore_wait(bar, 14)

    first = [
        remote(src.at[:, pl.ds(col, D)], kv.at[4, n, pl.ds(erow, T), :], fx_s.at[m + n], fx_r.at[m + n], dev(wrap(x + 1), y, zt))
        for m, col, zt in ((0, erow, z), (2, prow, zp))
        for n, src in ((0, k_hbm), (1, v_hbm))
    ]

    @pl.when(x < 3)
    def _():
        for c in first:
            c.start()

    pair = [
        remote(src.at[:, pl.ds(prow, D)], kv.at[0, n, pl.ds(erow, T), :], pair_s.at[n], pair_r.at[n], dev(x, y, zp))
        for n, src in ((0, k_hbm), (1, v_hbm))
    ]
    for c in pair:
        c.start()

    def gathered(src_of, buf, s, r_):
        copies = []
        for r in (1, 2, 3):
            zt = wrap(z + r)
            copies.append(remote(src_of(zt), buf.at[z], s.at[r - 1], r_.at[r - 1], dev(x, y, zt)))
        return copies

    qcopies = gathered(
        lambda zt: q_hbm.at[:, pl.ds(pl.multiple_of(lax.rem(zt, 2) * 256, 256), 256)], qg, q_s, q_r
    )
    for c in qcopies:
        c.start()

    c_wo.wait()
    c_cot.wait()
    grad = lax.dot_general(cot[...], wo[...], NT, preferred_element_type=F32).astype(BF16)
    og[0] = grad[:, :256]
    og[1] = grad[:, 256:]
    docopies = gathered(lambda zt: og.at[lax.rem(zt, 2)], dog, do_s, do_r)
    for c in docopies:
        c.start()
    dog[z] = og[e]

    c_k.wait()
    c_v.wait()
    for c in pair:
        c.wait_recv()

    def fwd_x(src, dst):
        return remote(kv.at[src], kv.at[dst], kvx_s.at[dst // 8], kv_r.at[dst], dev(wrap(x + 1), y, z))

    def fwd_y(r, kind):
        yt = wrap(y + r)
        up = yt > y
        if kind == 0:
            src, dst = 4, 4 + yt - y
        else:
            src, dst = jnp.where(up, 0, 8), jnp.where(up, yt - y, 8 + yt - y)
        return remote(kv.at[src], kv.at[dst], kvy_s.at[kind * 3 + r - 1], kv_r.at[dst], dev(x, yt, z))

    for r in (1, 2, 3):
        @pl.when(y + r < 4)
        def _():
            fwd_y(r, 1).start()

    def recv_slot(d):
        remote(kv.at[d], kv.at[d], kvx_s.at[0], kv_r.at[d], dev(wrap(x + 1), y, z)).wait_recv()

    @pl.when(x >= 1)
    def _():
        for c in first:
            c.wait_recv()
        for r in (1, 2, 3):
            fwd_y(r, 0).start()

    @pl.when((x >= 1) & (x < 3))
    def _():
        fwd_x(4, 8).start()

    wcopies = []
    for r in (1, 2, 3):
        xt = wrap(x + r)
        for n, src in ((0, x_hbm), (1, cot_hbm)):
            wcopies.append(
                remote(src.at[:, window(xt)], win.at[n, x], w_s.at[n, r - 1], w_r.at[n, r - 1], dev(xt, y, z))
            )
    for c in wcopies + c_win + c_w:
        c.start()

    c_q.wait()
    for r in (1, 2, 3):
        qcopies[r - 1].wait_recv()
    @pl.when(x >= 2)
    def _():
        recv_slot(8)
        for r in (1, 2, 3):
            @pl.when(y + r >= 4)
            def _():
                fwd_y(r, 1).start()

    for r in (1, 2, 3):
        docopies[r - 1].wait_recv()

    @pl.loop(0, 4)
    def _(zz):
        for j in range(2):
            rows = pl.ds(pl.multiple_of(j * 512 + zz * T, T), T)
            qb = qg[zz, :, j * D : (j + 1) * D]
            q2[rows, :] = qb
            qT[:, rows] = qb.T
            db = dog[zz, :, j * D : (j + 1) * D]
            do2[rows, :] = db
            doT[:, rows] = db.T

    st[...] = jnp.concatenate([jnp.full((1, ROWS), NEG, F32), jnp.zeros((7, ROWS), F32)], axis=0)
    oT[...] = jnp.zeros_like(oT)
    dqT[...] = jnp.zeros_like(dqT)

    def slot_of(kind, r):
        if kind == 0:
            return 4 + jnp.where(r <= y, r, r - 4)
        return jnp.where(r <= y, r, r + 4)

    @pl.loop(0, 12)
    def _(t):
        kind = (t >= 5) & (t < 8)
        r = jnp.where(t < 4, t, jnp.where(t < 8, t - 4, t - 8))
        d = jnp.where(r == 0, t, jnp.where(kind, slot_of(0, r), slot_of(1, r)))
        fits = (r == 0) | kind | jnp.where(t < 4, r <= y, r > y)

        @pl.when((S >= d) & fits)
        def _():
            @pl.when(r > 0)
            def _():
                recv_slot(d)

            kd = kv[d, 0]
            vd = kv[d, 1]
            vt = vd.T
            low = jnp.where(d == 0, 0, -100000)
            high = jnp.where(d == 8, 0, 100000)
            for c in range(4):
                cs = slice(c * 256, (c + 1) * 256)
                s = dot(kd, qT[:, cs])
                gap = (
                    lax.broadcasted_iota(jnp.int32, (KEYS, 256), 1)
                    - lax.broadcasted_iota(jnp.int32, (KEYS, 256), 0)
                    + ((c % 2) * 256 - f * 256)
                )
                s = jnp.where((gap >= low) & (gap < high), s, NEG)
                before = st[0:1, cs]
                top = jnp.maximum(before, jnp.max(s, axis=0, keepdims=True))
                p = jnp.exp2((s - top) * EXP2_SCALE)
                keep = jnp.exp2((before - top) * EXP2_SCALE)
                dp = dot(vd, doT[:, cs])
                st[0:1, cs] = top
                st[1:2, cs] = st[1:2, cs] * keep + jnp.sum(p, axis=0, keepdims=True)
                st[2:3, cs] = st[2:3, cs] * keep + jnp.sum(p * dp, axis=0, keepdims=True)
                ms[d, 0:1, cs] = top
                sbuf[d, :, cs] = p
                dpbuf[d, :, cs] = dp
                oT[:, cs] = oT[:, cs] * keep + dot(vt, p.astype(BF16))

    stat = remote(st, st_in, st_s, st_r, dev(x, y, wrap(z + 2)))
    stat.start()
    stat.wait()
    top = jnp.maximum(st[0:1, :], st_in[0:1, :])
    mine = jnp.exp2((st[0:1, :] - top) * EXP2_SCALE)
    other = jnp.exp2((st_in[0:1, :] - top) * EXP2_SCALE)
    inv = 1.0 / (st[1:2, :] * mine + st_in[1:2, :] * other)
    fin[0:1, :] = top
    fin[1:2, :] = inv
    fin[2:3, :] = (st[2:3, :] * mine + st_in[2:3, :] * other) * inv
    oT[...] = oT[...] * (mine * inv)

    def spread(srcT, factor, sendbuf, inbuf, s, r_):
        for j in range(2):
            for zz in range(4):
                piece = srcT[:, j * 512 + zz * T : j * 512 + (zz + 1) * T]
                sendbuf[zz, :, j * D : (j + 1) * D] = (piece * factor).T.astype(BF16)
        copies = []
        for r in (1, 2, 3):
            zt = wrap(z + r)
            copies.append(remote(sendbuf.at[zt], inbuf.at[z], s.at[r - 1], r_.at[r - 1], dev(x, y, zt)))
        for c in copies:
            c.start()
        inbuf[z] = sendbuf[z]
        return copies

    ocopies = spread(oT, 1.0, osend, oin, o_s, o_r)

    def grad_slot(d):
        w = jnp.exp2((ms[d, 0:1, :] - fin[0:1, :]) * EXP2_SCALE) * fin[1:2, :]
        kt = kv[d, 0].T
        for c in range(4):
            cs = slice(c * 256, (c + 1) * 256)
            p = sbuf[d, :, cs] * w[:, cs]
            pb_s[:, cs] = p.astype(BF16)
            ds = (p * (dpbuf[d, :, cs] - fin[2:3, cs])).astype(BF16)
            ds_s[:, cs] = ds
            dqT[:, cs] += dot(kt, ds)
        dkv[d, 0] = (LOGIT_SCALE * dot(ds_s[...], q2[...])).astype(BF16)
        dkv[d, 1] = dot(pb_s[...], do2[...]).astype(BF16)

    def back_y(kind, r):
        d = slot_of(kind, r)
        n = kind * 3 + r - 1
        return remote(dkv.at[d], rbuf.at[n], rb_s.at[n], rb_r.at[n], dev(x, wrap(y - r), z))

    @pl.loop(0, 12)
    def _(t):
        kind = (t >= 4) & (t < 7)
        r = jnp.where(t < 3, t + 1, jnp.where(kind, t - 3, jnp.where((t >= 8) & (t < 11), t - 7, 0)))
        d = jnp.where(r == 0, jnp.where(t == 3, 8, jnp.where(t == 7, 4, 0)), jnp.where(kind, slot_of(0, r), slot_of(1, r)))
        fits = (r == 0) | kind | jnp.where(t < 3, r > y, r <= y)

        @pl.when((S >= d) & fits)
        def _():
            grad_slot(d)

            @pl.when(r > 0)
            def _():
                n = jnp.where(kind, r - 1, r + 2)
                remote(dkv.at[d], rbuf.at[n], rb_s.at[n], rb_r.at[n], dev(x, wrap(y - r), z)).start()

    dqcopies = spread(dqT, LOGIT_SCALE, dqsend, dqin, dq_s, dq_r)

    def over_x(src, dst, s, r_):
        return [remote(src, dst, s.at[r - 1], r_.at[r - 1], dev(wrap(x + r), y, z)) for r in (1, 2, 3)]

    for c in ocopies:
        c.wait_recv()
    for n in range(2):
        attn_o[n] = (oin[n].astype(F32) + oin[n + 2].astype(F32)).astype(BF16)
    agcopies = over_x(attn_o, ag.at[:, x], ag_s, ag_r)
    for c in agcopies:
        c.start()
    ag[:, x] = attn_o[...]


    def recv_back(n):
        remote(rbuf.at[n], rbuf.at[n], rb_s.at[n], rb_r.at[n], dev(x, wrap(y + 1), z)).wait_recv()

    chain8, chain4 = (
        [remote(csend.at[m, n], cin.at[m, n], c_s.at[m, n], c_r.at[m, n], dev(wrap(x - 1), y, z)) for n in range(2)]
        for m in range(2)
    )

    for c in c_win:
        c.wait()
    for c in wcopies:
        c.wait_recv()

    @pl.loop(0, 4)
    def _(xx):
        for n in range(2):
            for b in range(WIN // 128):
                cols = slice(b * 128, (b + 1) * 128)
                winT[n, cols, pl.ds(pl.multiple_of(xx * T, T), T)] = win[n, xx, :, cols].T

    @pl.when(x >= 2)
    def _():
        facc[...] = dkv[8].astype(F32)
        for r in (1, 2, 3):
            @pl.when(y + r >= 4)
            def _():
                recv_back(3 + r - 1)
                facc[...] += rbuf[3 + r - 1].astype(F32)

        for n in range(2):
            csend[0, n] = facc[n].astype(BF16)
            chain8[n].start()

    @pl.when(x >= 1)
    def _():
        for r in (1, 2, 3):
            recv_back(r - 1)

        for n in range(2):
            @pl.when(x < 3)
            def _():
                chain8[n].wait_recv()

            acc = dkv[4, n].astype(F32)
            for r in (1, 2, 3):
                acc = acc + rbuf[r - 1, n].astype(F32)
            acc = acc + jnp.where(x < 3, cin[0, n].astype(F32), 0.0)
            csend[1, n] = acc.astype(BF16)
            chain4[n].start()

    off = pl.multiple_of(64 * lax.rem(x, 2), 16)

    def over_y(src, buf, s, r_):
        copies = []
        for r in (1, 2, 3):
            yt = wrap(y + r)
            rows = pl.ds(pl.multiple_of(off + 144 * yt, 16), 144)
            copies.append(remote(src.at[rows, :], buf.at[r - 1], s.at[r - 1], r_.at[r - 1], dev(x, yt, z)))
        return copies

    for c in agcopies:
        c.wait_recv()
    for n in range(2):
        po[:, n * 256 : (n + 1) * 256] = dot(winT[1], ag[n].reshape(4 * T, 256)).astype(BF16)
    yocopies = over_y(po, yo, yo_s, yo_r)
    for c in yocopies:
        c.start()

    facc[...] = dkv[0].astype(F32)
    for r in (1, 2, 3):
        @pl.when(y + r < 4)
        def _():
            recv_back(3 + r - 1)
            facc[...] += rbuf[3 + r - 1].astype(F32)

    swap = [
        remote(finkv.at[n, pl.ds(prow, T), :], pin.at[n], f_s.at[n], f_r.at[n], dev(x, y, zp)) for n in range(2)
    ]
    ggcopies = [
        remote(finkv.at[1, pl.ds(row, T), :], gvg.at[e, x], gg_s.at[m + r - 1], gg_r.at[m + r - 1], dev(wrap(x + r), y, zt))
        for r in (1, 2, 3)
        for m, row, zt in ((0, erow, z), (3, prow, zp))
    ]
    for n in range(2):
        @pl.when(x < 3)
        def _():
            chain4[n].wait_recv()

        acc = facc[n] + jnp.where(x < 3, cin[1, n].astype(F32), 0.0)
        finkv[n] = acc.astype(BF16)
        swap[n].start()
    for c in ggcopies:
        c.start()

    for c in dqcopies:
        c.wait_recv()
    for n in range(2):
        gq_o[n] = (dqin[n].astype(F32) + dqin[n + 2].astype(F32)).astype(BF16)
    for c in c_w:
        c.wait()
    for c in swap:
        c.wait_recv()
    for n, out in ((0, gk_o), (1, gv_o)):
        out[e] = finkv[n, pl.ds(erow, T), :]
        out[1 - e] = pin[n]
    gvg[:, x] = gv_o[...]

    def terms(hh):
        rows = pl.ds(pl.multiple_of(COLS * hh, 16), COLS)
        acc = jnp.zeros((COLS, T), F32)
        for n in range(2):
            acc = acc + lax.dot_general(wq[rows, n * 256 : (n + 1) * 256], gq_o[n], NT, preferred_element_type=F32)
            acc = acc + lax.dot_general(wk[rows, n * D : (n + 1) * D], gk_o[n], NT, preferred_element_type=F32)
            acc = acc + lax.dot_general(wv[rows, n * D : (n + 1) * D], gv_o[n], NT, preferred_element_type=F32)
        return acc

    hzc = lax.rem(hc + 2, 4)
    tb[0] = terms(hzc).astype(BF16)
    far = remote(tb.at[0], hin.at[0], h_s.at[0], h_r.at[0], (i, hc))
    far.start()
    mine_far = terms(hz)
    def over_z(copies, own, buf, total_s, piece_s, in_s, s, r_):
        for c in copies:
            c.wait_recv()
        acc = own[pl.ds(pl.multiple_of(off + 144 * y, 16), 144), :].astype(F32)
        for r in range(3):
            acc = acc + buf[r].astype(F32)
        total_s[...] = acc
        for zz in range(4):
            piece_s[zz] = total_s[36 * zz : 36 * (zz + 1), :].astype(piece_s.dtype)
        out = []
        for r in (1, 2, 3):
            zt = wrap(z + r)
            out.append(remote(piece_s.at[zt], in_s.at[r - 1], s.at[r - 1], r_.at[r - 1], dev(x, y, zt)))
        for c in out:
            c.start()
        return out

    zocopies = over_z(yocopies, po, yo, zso, zpo, zio, zo_s, zo_r)
    far.wait_recv()
    tb[1] = (mine_far + hin[0].astype(F32)).astype(BF16)
    across = remote(tb.at[1], hin.at[1], h_s.at[1], h_r.at[1], (i, hz))
    across.start()
    tb[2] = terms(hc).astype(BF16)
    near = remote(tb.at[2], hin.at[2], h_s.at[2], h_r.at[2], (i, hc))
    near.start()

    for c in ggcopies:
        c.wait_recv()
    for n in range(2):
        pv[:, n * D : (n + 1) * D] = dot(winT[0], gvg[n].reshape(4 * T, D)).astype(BF16)
    yvcopies = over_y(pv, yv, yv_s, yv_r)
    for c in yvcopies:
        c.start()

    mine_near = terms(h)
    zvcopies = over_z(yvcopies, pv, yv, zsv, zpv, ziv, zv_s, zv_r)

    for c in zocopies:
        c.wait_recv()
    acc = zpo[z].astype(F32)
    for r in range(3):
        acc = acc + zio[r].astype(F32)
    gwo_o[...] = acc
    near.wait_recv()
    across.wait_recv()
    gi_o[...] = (mine_near + hin[2].astype(F32) + hin[1].astype(F32)).astype(BF16)
    for c in zvcopies:
        c.wait_recv()
    acc = zpv[z]
    for r in range(3):
        acc = acc + ziv[r]
    gwv_o[...] = acc

    for c in (
        pair + qcopies + docopies + ocopies + dqcopies + swap + wcopies + agcopies + ggcopies
        + yocopies + yvcopies + zocopies + zvcopies + [far, across, near]
    ):
        c.wait_send()

    @pl.when(x < 3)
    def _():
        for c in first:
            c.wait_send()

    @pl.when((x >= 1) & (x < 3))
    def _():
        fwd_x(4, 8).wait_send()

    for r in (1, 2, 3):
        @pl.when((y + r < 4) | (x >= 2))
        def _():
            fwd_y(r, 1).wait_send()

        @pl.when(x >= 1)
        def _():
            fwd_y(r, 0).wait_send()
            back_y(0, r).wait_send()

        @pl.when((r <= y) | (x >= 2))
        def _():
            back_y(1, r).wait_send()

    @pl.when(x >= 2)
    def _():
        for c in chain8:
            c.wait_send()

    @pl.when(x >= 1)
    def _():
        for c in chain4:
            c.wait_send()


def layer(xn, q, k, v, wq, wk, wv, wo, cot):
    dma = pltpu.SemaphoreType.DMA
    vm = pltpu.VMEM
    return pl.pallas_call(
        layer_kernel,
        out_shape=(
            jax.ShapeDtypeStruct((COLS, T), BF16),
            jax.ShapeDtypeStruct((36, 256), F32),
            jax.ShapeDtypeStruct((36, 512), F32),
        ),
        in_specs=[pl.BlockSpec(memory_space=pl.ANY)] * 9,
        out_specs=tuple(pl.BlockSpec(memory_space=pltpu.VMEM) for _ in range(3)),
        scratch_shapes=[
            vm((2, T, 256), BF16),
            vm((2, T, 256), BF16),
            vm((2, T, D), BF16),
            vm((2, T, D), BF16),
            vm(wq.shape, BF16),
            vm(wk.shape, BF16),
            vm(wv.shape, BF16),
            vm((2, 4, T, WIN), BF16),
            vm((2, WIN, 4 * T), BF16),
            vm((2, 4, T, 256), BF16),
            vm((2, 4, T, D), BF16),
            vm((WIN, 512), BF16),
            vm((WIN, 256), BF16),
            vm((3, 144, 512), BF16),
            vm((3, 144, 256), BF16),
            vm((144, 512), F32),
            vm((144, 256), F32),
            vm((4, 36, 512), BF16),
            vm((4, 36, 256), F32),
            vm((3, 36, 512), BF16),
            vm((3, 36, 256), F32),
            vm((3, COLS, T), BF16),
            vm((3, COLS, T), BF16),
            vm((2, KEYS, D), F32),
            vm((SLOTS, 2, KEYS, D), BF16),
            vm((4, T, 256), BF16),
            vm((4, T, 256), BF16),
            vm((2, T, 256), BF16),
            vm(cot.shape, BF16),
            vm(wo.shape, BF16),
            vm((ROWS, D), BF16),
            vm((ROWS, D), BF16),
            vm((D, ROWS), BF16),
            vm((D, ROWS), BF16),
            vm((SLOTS, KEYS, ROWS), F32),
            vm((SLOTS, KEYS, ROWS), F32),
            vm((KEYS, ROWS), BF16),
            vm((KEYS, ROWS), BF16),
            vm((SLOTS, 8, ROWS), F32),
            vm((8, ROWS), F32),
            vm((8, ROWS), F32),
            vm((8, ROWS), F32),
            vm((D, ROWS), F32),
            vm((D, ROWS), F32),
            vm((4, T, 256), BF16),
            vm((4, T, 256), BF16),
            vm((4, T, 256), BF16),
            vm((4, T, 256), BF16),
            vm((SLOTS, 2, KEYS, D), BF16),
            vm((6, 2, KEYS, D), BF16),
            vm((2, 2, KEYS, D), BF16),
            vm((2, 2, KEYS, D), BF16),
            vm((2, KEYS, D), BF16),
            vm((2, T, D), BF16),
            dma((10,)), dma((2,)), dma((2,)), dma((3,)), dma((3,)), dma((3,)), dma((3,)),
            dma((2,)), dma((6,)), dma((SLOTS,)), dma, dma, dma((3,)), dma((3,)), dma((3,)), dma((3,)),
            dma((6,)), dma((6,)), dma((2, 2)), dma((2, 2)), dma((2,)), dma((2,)),
            dma((4,)), dma((4,)), dma((2, 3)), dma((2, 3)), *([dma((3,))] * 2), *([dma((6,))] * 2), *([dma((3,))] * 10),
        ],
        compiler_params=pltpu.CompilerParams(
            collective_id=1, has_side_effects=True, vmem_limit_bytes=62 * 1024 * 1024
        ),
        name="layer",
    )(xn, q, k, v, wq, wk, wv, wo, cot)


def hand_over(*refs):
    for n in range(3):
        refs[3 + n][...] = refs[n][...]


def local(*args):
    results = layer(*args)
    vmem = tuple(pl.BlockSpec(memory_space=pltpu.VMEM) for _ in range(3))
    grad_input, grad_wvalue, grad_woutput = pl.pallas_call(
        hand_over,
        out_shape=tuple(jax.ShapeDtypeStruct(a.shape, a.dtype) for a in results),
        in_specs=vmem,
        out_specs=vmem,
        name="hand_over",
    )(*results)
    return grad_input.T, grad_wvalue, grad_woutput.T


def solution(mesh):
    seq, both, cols, rows = P("seq", None), P("seq", "head"), P(None, "head"), P("head", None)
    return jax.shard_map(
        local,
        mesh=mesh,
        in_specs=(seq, both, both, both, cols, cols, cols, rows, seq),
        out_specs=(both, both, P("head", "seq")),
        check_vma=False,
    )
```

```python
import functools
import math

import jax
import jax.numpy as jnp
from jax import lax
from jax.experimental import pallas as pl
from jax.experimental.pallas import tpu as pltpu
from jax.sharding import PartitionSpec as P

MESH = pl.DeviceIdType.MESH
F32 = jnp.float32
BF16 = jnp.bfloat16
LOGIT_SCALE = 1.0 / 12.0
EXP2_SCALE = LOGIT_SCALE * math.log2(math.e)
NEG = -1e30
T = 128
D = 128
SLOTS = 9
ROWS = 1024
WIN = 640
COLS = 576
KEYS = 256
NT = (((1,), (1,)), ((), ()))


def dot(a, b):
    return jnp.dot(a, b, preferred_element_type=F32)


def place():
    i = lax.axis_index("seq")
    h = lax.axis_index("head")
    x = lax.div(i, 16)
    y = lax.rem(lax.div(i, 4), 4)
    z = lax.rem(i, 4)
    return i, h, x, y, z


def layer_kernel(
    x_hbm, q_hbm, k_hbm, v_hbm, wq_hbm, wk_hbm, wv_hbm, wo_hbm, cot_hbm,
    gi_o, gwv_o, gwo_o,
    attn_o, gq_o, gk_o, gv_o, wq, wk, wv, win, winT, ag, gvg, po, pv, yo, yv, zso, zsv, zpo, zpv, zio, ziv, tb, hin,
    tq, facc, kv, qg, dog, og, cot, wo, q2, do2, qT, doT, sbuf, dpbuf, pb_s, ds_s, ms, st, st_in, fin,
    oT, dqT, osend, oin, dqsend, dqin, dkv, rbuf, csend, cin, finkv, pin,
    lsem, pair_s, pair_r, q_s, q_r, do_s, do_r, kvx_s, kvy_s, kv_r, st_s, st_r, o_s, o_r, dq_s, dq_r,
    rb_s, rb_r, c_s, c_r, f_s, f_r,
    fx_s, fx_r, w_s, w_r, ag_s, ag_r, gg_s, gg_r, yo_s, yo_r, yv_s, yv_r, zo_s, zo_r, zv_s, zv_r, h_s, h_r,
):
    i, h, x, y, z = place()
    e, f = lax.rem(z, 2), lax.div(z, 2)
    S = x * 4 + y

    def dev(x_, y_, z_):
        return (x_ * 16 + y_ * 4 + z_, h)

    def wrap(a):
        return lax.rem(a + 4, 4)

    def remote(src, dst, s, r, to):
        return pltpu.make_async_remote_copy(
            src_ref=src, dst_ref=dst, send_sem=s, recv_sem=r, device_id=to, device_id_type=MESH
        )

    erow = pl.multiple_of(e * T, T)
    prow = pl.multiple_of((1 - e) * T, T)
    ecol2 = pl.multiple_of(e * 256, 256)
    c_wo = pltpu.make_async_copy(wo_hbm, wo, lsem.at[0])
    c_cot = pltpu.make_async_copy(cot_hbm, cot, lsem.at[1])
    c_k = pltpu.make_async_copy(k_hbm.at[:, pl.ds(erow, D)], kv.at[0, 0, pl.ds(erow, T), :], lsem.at[2])
    c_v = pltpu.make_async_copy(v_hbm.at[:, pl.ds(erow, D)], kv.at[0, 1, pl.ds(erow, T), :], lsem.at[3])
    c_q = pltpu.make_async_copy(q_hbm.at[:, pl.ds(ecol2, 256)], qg.at[z], lsem.at[4])
    for c in (c_wo, c_cot, c_k, c_v, c_q):
        c.start()

    def window(xt):
        return pl.ds(pl.multiple_of(lax.div(9 * xt, 2) * 128, 128), WIN)

    c_win = [
        pltpu.make_async_copy(src.at[:, window(x)], win.at[n, x], lsem.at[5 + n]) for n, src in ((0, x_hbm), (1, cot_hbm))
    ]
    c_w = [pltpu.make_async_copy(src, dst, lsem.at[7 + n]) for n, (src, dst) in enumerate(((wq_hbm, wq), (wk_hbm, wk), (wv_hbm, wv)))]

    bar = pltpu.get_barrier_semaphore()
    for r in (1, 2, 3):
        for to in (dev(x, y, wrap(z + r)), dev(x, wrap(y + r), z), dev(wrap(x + r), y, z)):
            pl.semaphore_signal(bar, inc=1, device_id=to, device_id_type=MESH)
    hc = h + 1 - 2 * lax.rem(h, 2)
    hz = lax.rem(h + 2, 4)
    for to in ((i, hc), (i, hz)):
        pl.semaphore_signal(bar, inc=1, device_id=to, device_id_type=MESH)
    zp = z + 1 - 2 * e
    for r in (1, 2, 3):
        pl.semaphore_signal(bar, inc=1, device_id=dev(wrap(x + r), y, zp), device_id_type=MESH)
    pl.semaphore_wait(bar, 14)

    pair = [
        remote(src.at[:, pl.ds(prow, D)], kv.at[0, n, pl.ds(erow, T), :], pair_s.at[n], pair_r.at[n], dev(x, y, zp))
        for n, src in ((0, k_hbm), (1, v_hbm))
    ]
    for c in pair:
        c.start()

    first = [
        remote(src.at[:, pl.ds(col, D)], kv.at[4, n, pl.ds(erow, T), :], fx_s.at[m + n], fx_r.at[m + n], dev(wrap(x + 1), y, zt))
        for m, col, zt in ((0, erow, z), (2, prow, zp))
        for n, src in ((0, k_hbm), (1, v_hbm))
    ]

    @pl.when(x < 3)
    def _():
        for c in first:
            c.start()

    def gathered(src_of, buf, s, r_):
        copies = []
        for r in (1, 2, 3):
            zt = wrap(z + r)
            copies.append(remote(src_of(zt), buf.at[z], s.at[r - 1], r_.at[r - 1], dev(x, y, zt)))
        return copies

    qcopies = gathered(
        lambda zt: q_hbm.at[:, pl.ds(pl.multiple_of(lax.rem(zt, 2) * 256, 256), 256)], qg, q_s, q_r
    )
    for c in qcopies:
        c.start()

    c_wo.wait()
    c_cot.wait()
    grad = lax.dot_general(cot[...], wo[...], NT, preferred_element_type=F32).astype(BF16)
    og[0] = grad[:, :256]
    og[1] = grad[:, 256:]
    docopies = gathered(lambda zt: og.at[lax.rem(zt, 2)], dog, do_s, do_r)
    for c in docopies:
        c.start()
    dog[z] = og[e]

    c_k.wait()
    c_v.wait()
    for c in pair:
        c.wait_recv()

    def fwd_x(src, dst):
        return remote(kv.at[src], kv.at[dst], kvx_s.at[dst // 8], kv_r.at[dst], dev(wrap(x + 1), y, z))

    def fwd_y(r, kind):
        yt = wrap(y + r)
        up = yt > y
        if kind == 0:
            src, dst = 4, 4 + yt - y
        else:
            src, dst = jnp.where(up, 0, 8), jnp.where(up, yt - y, 8 + yt - y)
        return remote(kv.at[src], kv.at[dst], kvy_s.at[kind * 3 + r - 1], kv_r.at[dst], dev(x, yt, z))

    for r in (1, 2, 3):
        @pl.when(y + r < 4)
        def _():
            fwd_y(r, 1).start()

    def recv_slot(d):
        remote(kv.at[d], kv.at[d], kvx_s.at[0], kv_r.at[d], dev(wrap(x + 1), y, z)).wait_recv()

    @pl.when(x >= 1)
    def _():
        for c in first:
            c.wait_recv()
        for r in (1, 2, 3):
            fwd_y(r, 0).start()

    @pl.when((x >= 1) & (x < 3))
    def _():
        fwd_x(4, 8).start()

    wcopies = []
    for r in (1, 2, 3):
        xt = wrap(x + r)
        for n, src in ((0, x_hbm), (1, cot_hbm)):
            wcopies.append(
                remote(src.at[:, window(xt)], win.at[n, x], w_s.at[n, r - 1], w_r.at[n, r - 1], dev(xt, y, z))
            )
    for c in wcopies + c_win + c_w:
        c.start()

    c_q.wait()
    for r in (1, 2, 3):
        qcopies[r - 1].wait_recv()
    @pl.when(x >= 2)
    def _():
        recv_slot(8)
        for r in (1, 2, 3):
            @pl.when(y + r >= 4)
            def _():
                fwd_y(r, 1).start()

    for r in (1, 2, 3):
        docopies[r - 1].wait_recv()

    @pl.loop(0, 4)
    def _(zz):
        for j in range(2):
            rows = pl.ds(pl.multiple_of(j * 512 + zz * T, T), T)
            qb = qg[zz, :, j * D : (j + 1) * D]
            q2[rows, :] = qb
            qT[:, rows] = qb.T
            db = dog[zz, :, j * D : (j + 1) * D]
            do2[rows, :] = db
            doT[:, rows] = db.T

    st[...] = jnp.concatenate([jnp.full((1, ROWS), NEG, F32), jnp.zeros((7, ROWS), F32)], axis=0)
    oT[...] = jnp.zeros_like(oT)
    dqT[...] = jnp.zeros_like(dqT)

    def slot_of(kind, r):
        if kind == 0:
            return 4 + jnp.where(r <= y, r, r - 4)
        return jnp.where(r <= y, r, r + 4)

    @pl.loop(0, 12)
    def _(t):
        kind = (t >= 5) & (t < 8)
        r = jnp.where(t < 4, t, jnp.where(t < 8, t - 4, t - 8))
        d = jnp.where(r == 0, t, jnp.where(kind, slot_of(0, r), slot_of(1, r)))
        fits = (r == 0) | kind | jnp.where(t < 4, r <= y, r > y)

        @pl.when((S >= d) & fits)
        def _():
            @pl.when(r > 0)
            def _():
                recv_slot(d)

            kd = kv[d, 0]
            vd = kv[d, 1]
            vt = vd.T
            low = jnp.where(d == 0, 0, -100000)
            high = jnp.where(d == 8, 0, 100000)
            for c in range(4):
                cs = slice(c * 256, (c + 1) * 256)
                s = dot(kd, qT[:, cs])
                gap = (
                    lax.broadcasted_iota(jnp.int32, (KEYS, 256), 1)
                    - lax.broadcasted_iota(jnp.int32, (KEYS, 256), 0)
                    + ((c % 2) * 256 - f * 256)
                )
                s = jnp.where((gap >= low) & (gap < high), s, NEG)
                before = st[0:1, cs]
                top = jnp.maximum(before, jnp.max(s, axis=0, keepdims=True))
                p = jnp.exp2((s - top) * EXP2_SCALE)
                keep = jnp.exp2((before - top) * EXP2_SCALE)
                dp = dot(vd, doT[:, cs])
                st[0:1, cs] = top
                st[1:2, cs] = st[1:2, cs] * keep + jnp.sum(p, axis=0, keepdims=True)
                st[2:3, cs] = st[2:3, cs] * keep + jnp.sum(p * dp, axis=0, keepdims=True)
                ms[d, 0:1, cs] = top
                sbuf[d, :, cs] = p
                dpbuf[d, :, cs] = dp
                oT[:, cs] = oT[:, cs] * keep + dot(vt, p.astype(BF16))

    stat = remote(st, st_in, st_s, st_r, dev(x, y, wrap(z + 2)))
    stat.start()
    stat.wait()
    top = jnp.maximum(st[0:1, :], st_in[0:1, :])
    mine = jnp.exp2((st[0:1, :] - top) * EXP2_SCALE)
    other = jnp.exp2((st_in[0:1, :] - top) * EXP2_SCALE)
    inv = 1.0 / (st[1:2, :] * mine + st_in[1:2, :] * other)
    fin[0:1, :] = top
    fin[1:2, :] = inv
    fin[2:3, :] = (st[2:3, :] * mine + st_in[2:3, :] * other) * inv
    oT[...] = oT[...] * (mine * inv)

    def spread(srcT, factor, sendbuf, inbuf, s, r_):
        for j in range(2):
            for zz in range(4):
                piece = srcT[:, j * 512 + zz * T : j * 512 + (zz + 1) * T]
                sendbuf[zz, :, j * D : (j + 1) * D] = (piece * factor).T.astype(BF16)
        copies = []
        for r in (1, 2, 3):
            zt = wrap(z + r)
            copies.append(remote(sendbuf.at[zt], inbuf.at[z], s.at[r - 1], r_.at[r - 1], dev(x, y, zt)))
        for c in copies:
            c.start()
        inbuf[z] = sendbuf[z]
        return copies

    ocopies = spread(oT, 1.0, osend, oin, o_s, o_r)

    def grad_slot(d):
        w = jnp.exp2((ms[d, 0:1, :] - fin[0:1, :]) * EXP2_SCALE) * fin[1:2, :]
        kt = kv[d, 0].T
        for c in range(4):
            cs = slice(c * 256, (c + 1) * 256)
            p = sbuf[d, :, cs] * w[:, cs]
            pb_s[:, cs] = p.astype(BF16)
            ds = (p * (dpbuf[d, :, cs] - fin[2:3, cs])).astype(BF16)
            ds_s[:, cs] = ds
            dqT[:, cs] += dot(kt, ds)
        dkv[d, 0] = (LOGIT_SCALE * dot(ds_s[...], q2[...])).astype(BF16)
        dkv[d, 1] = dot(pb_s[...], do2[...]).astype(BF16)

    def back_y(kind, r):
        d = slot_of(kind, r)
        n = kind * 3 + r - 1
        return remote(dkv.at[d], rbuf.at[n], rb_s.at[n], rb_r.at[n], dev(x, wrap(y - r), z))

    def grad_step(t):
        kind = (t >= 4) & (t < 7)
        r = jnp.where(t < 3, t + 1, jnp.where(kind, t - 3, jnp.where((t >= 8) & (t < 11), t - 7, 0)))
        d = jnp.where(r == 0, jnp.where(t == 3, 8, jnp.where(t == 7, 4, 0)), jnp.where(kind, slot_of(0, r), slot_of(1, r)))
        fits = (r == 0) | kind | jnp.where(t < 3, r > y, r <= y)

        @pl.when((S >= d) & fits)
        def _():
            grad_slot(d)

            @pl.when(r > 0)
            def _():
                n = jnp.where(kind, r - 1, r + 2)
                remote(dkv.at[d], rbuf.at[n], rb_s.at[n], rb_r.at[n], dev(x, wrap(y - r), z)).start()

    pl.loop(0, 8)(grad_step)

    def recv_back(n):
        remote(rbuf.at[n], rbuf.at[n], rb_s.at[n], rb_r.at[n], dev(x, wrap(y + 1), z)).wait_recv()

    chain8, chain4 = (
        [
            remote(
                csend.at[m, :, pl.ds(row, T), :], cin.at[m, part], c_s.at[m, part], c_r.at[m, part], dev(wrap(x - 2 + m), y, zt)
            )
            for part, row, zt in ((0, erow, z), (1, prow, zp))
        ]
        for m in range(2)
    )

    @pl.when(x >= 2)
    def _():
        facc[...] = dkv[8].astype(F32)
        for r in (1, 2, 3):
            @pl.when(y + r >= 4)
            def _():
                recv_back(3 + r - 1)
                facc[...] += rbuf[3 + r - 1].astype(F32)

        csend[0] = facc[...].astype(BF16)
        for c in chain8:
            c.start()

    pl.loop(8, 12)(grad_step)

    dqcopies = spread(dqT, LOGIT_SCALE, dqsend, dqin, dq_s, dq_r)

    def over_x(src, dst, s, r_):
        return [remote(src, dst, s.at[r - 1], r_.at[r - 1], dev(wrap(x + r), y, z)) for r in (1, 2, 3)]

    for c in ocopies:
        c.wait_recv()
    for n in range(2):
        attn_o[n] = (oin[n].astype(F32) + oin[n + 2].astype(F32)).astype(BF16)
    agcopies = over_x(attn_o, ag.at[:, x], ag_s, ag_r)
    for c in agcopies:
        c.start()
    ag[:, x] = attn_o[...]


    for c in c_win:
        c.wait()
    for c in wcopies:
        c.wait_recv()

    @pl.loop(0, 4)
    def _(xx):
        for n in range(2):
            for b in range(WIN // 128):
                cols = slice(b * 128, (b + 1) * 128)
                winT[n, cols, pl.ds(pl.multiple_of(xx * T, T), T)] = win[n, xx, :, cols].T

    @pl.when(x >= 1)
    def _():
        facc[...] = dkv[4].astype(F32)
        for r in (1, 2, 3):
            recv_back(r - 1)
            facc[...] += rbuf[r - 1].astype(F32)
        csend[1] = facc[...].astype(BF16)
        for c in chain4:
            c.start()

    off = pl.multiple_of(64 * lax.rem(x, 2), 16)

    def over_y(src, buf, s, r_):
        copies = []
        for r in (1, 2, 3):
            yt = wrap(y + r)
            rows = pl.ds(pl.multiple_of(off + 144 * yt, 16), 144)
            copies.append(remote(src.at[rows, :], buf.at[r - 1], s.at[r - 1], r_.at[r - 1], dev(x, yt, z)))
        return copies

    facc[...] = dkv[0].astype(F32)
    for r in (1, 2, 3):
        @pl.when(y + r < 4)
        def _():
            recv_back(3 + r - 1)
            facc[...] += rbuf[3 + r - 1].astype(F32)

    finkv[...] = facc[:, pl.ds(prow, T), :].astype(BF16)
    swap = [remote(finkv, pin, f_s, f_r, dev(x, y, zp))]
    swap[0].start()

    for c in dqcopies:
        c.wait_recv()
    for n in range(2):
        gq_o[n] = (dqin[n].astype(F32) + dqin[n + 2].astype(F32)).astype(BF16)
    for c in c_w:
        c.wait()

    def wrows(hh):
        return pl.ds(pl.multiple_of(COLS * hh, 16), COLS)

    @pl.loop(0, 4)
    def _(hh):
        tq[hh] = sum(
            lax.dot_general(wq[wrows(hh), n * 256 : (n + 1) * 256], gq_o[n], NT, preferred_element_type=F32)
            for n in range(2)
        )

    for c in agcopies:
        c.wait_recv()
    for n in range(2):
        po[:, n * 256 : (n + 1) * 256] = dot(winT[1], ag[n].reshape(4 * T, 256)).astype(BF16)
    yocopies = over_y(po, yo, yo_s, yo_r)
    for c in yocopies:
        c.start()

    swap[0].wait_recv()
    final = [[facc[n, pl.ds(erow, T), :], pin[n].astype(F32)] for n in range(2)]
    for m in (0, 1):
        chain = (chain8, chain4)[m]

        @pl.when(x < 2 + m)
        def _():
            for c in chain:
                c.wait_recv()

        for n in range(2):
            for part in range(2):
                final[n][part] = final[n][part] + jnp.where(x < 2 + m, cin[m, part, n].astype(F32), 0.0)
    for n, out in ((1, gv_o), (0, gk_o)):
        out[e] = final[n][0].astype(BF16)
        out[1 - e] = final[n][1].astype(BF16)
    ggcopies = over_x(gv_o, gvg.at[:, x], gg_s, gg_r)
    for c in ggcopies:
        c.start()
    gvg[:, x] = gv_o[...]

    def terms(hh):
        acc = tq[hh]
        for n in range(2):
            acc = acc + lax.dot_general(wk[wrows(hh), n * D : (n + 1) * D], gk_o[n], NT, preferred_element_type=F32)
            acc = acc + lax.dot_general(wv[wrows(hh), n * D : (n + 1) * D], gv_o[n], NT, preferred_element_type=F32)
        return acc

    hzc = lax.rem(hc + 2, 4)
    tb[0] = terms(hzc).astype(BF16)
    far = remote(tb.at[0], hin.at[0], h_s.at[0], h_r.at[0], (i, hc))
    far.start()
    for c in ggcopies:
        c.wait_recv()
    for n in range(2):
        pv[:, n * D : (n + 1) * D] = dot(winT[0], gvg[n].reshape(4 * T, D)).astype(BF16)
    yvcopies = over_y(pv, yv, yv_s, yv_r)
    for c in yvcopies:
        c.start()

    mine_far = terms(hz)
    far.wait_recv()
    tb[1] = (mine_far + hin[0].astype(F32)).astype(BF16)
    across = remote(tb.at[1], hin.at[1], h_s.at[1], h_r.at[1], (i, hz))
    across.start()
    tb[2] = terms(hc).astype(BF16)
    near = remote(tb.at[2], hin.at[2], h_s.at[2], h_r.at[2], (i, hc))
    near.start()

    def over_z(copies, own, buf, total_s, piece_s, in_s, s, r_):
        for c in copies:
            c.wait_recv()
        acc = own[pl.ds(pl.multiple_of(off + 144 * y, 16), 144), :].astype(F32)
        for r in range(3):
            acc = acc + buf[r].astype(F32)
        total_s[...] = acc
        for zz in range(4):
            piece_s[zz] = total_s[36 * zz : 36 * (zz + 1), :].astype(piece_s.dtype)
        out = []
        for r in (1, 2, 3):
            zt = wrap(z + r)
            out.append(remote(piece_s.at[zt], in_s.at[r - 1], s.at[r - 1], r_.at[r - 1], dev(x, y, zt)))
        for c in out:
            c.start()
        return out

    zocopies = over_z(yocopies, po, yo, zso, zpo, zio, zo_s, zo_r)
    mine_near = terms(h)
    zvcopies = over_z(yvcopies, pv, yv, zsv, zpv, ziv, zv_s, zv_r)

    for c in zocopies:
        c.wait_recv()
    acc = zpo[z].astype(F32)
    for r in range(3):
        acc = acc + zio[r].astype(F32)
    gwo_o[...] = acc
    near.wait_recv()
    across.wait_recv()
    gi_o[...] = (mine_near + hin[2].astype(F32) + hin[1].astype(F32)).astype(BF16)
    for c in zvcopies:
        c.wait_recv()
    acc = zpv[z].astype(F32)
    for r in range(3):
        acc = acc + ziv[r].astype(F32)
    gwv_o[...] = acc

    for c in (
        pair + qcopies + docopies + ocopies + dqcopies + swap + wcopies + agcopies + ggcopies
        + yocopies + yvcopies + zocopies + zvcopies + [far, across, near]
    ):
        c.wait_send()

    @pl.when(x < 3)
    def _():
        for c in first:
            c.wait_send()

    @pl.when((x >= 1) & (x < 3))
    def _():
        fwd_x(4, 8).wait_send()

    for r in (1, 2, 3):
        @pl.when((y + r < 4) | (x >= 2))
        def _():
            fwd_y(r, 1).wait_send()

        @pl.when(x >= 1)
        def _():
            fwd_y(r, 0).wait_send()
            back_y(0, r).wait_send()

        @pl.when((r <= y) | (x >= 2))
        def _():
            back_y(1, r).wait_send()

    @pl.when(x >= 2)
    def _():
        for c in chain8:
            c.wait_send()

    @pl.when(x >= 1)
    def _():
        for c in chain4:
            c.wait_send()


def layer(xn, q, k, v, wq, wk, wv, wo, cot):
    dma = pltpu.SemaphoreType.DMA
    vm = pltpu.VMEM
    return pl.pallas_call(
        layer_kernel,
        out_shape=(
            jax.ShapeDtypeStruct((COLS, T), BF16),
            jax.ShapeDtypeStruct((36, 256), F32),
            jax.ShapeDtypeStruct((36, 512), F32),
        ),
        in_specs=[pl.BlockSpec(memory_space=pl.ANY)] * 9,
        out_specs=tuple(pl.BlockSpec(memory_space=pltpu.VMEM) for _ in range(3)),
        scratch_shapes=[
            vm((2, T, 256), BF16),
            vm((2, T, 256), BF16),
            vm((2, T, D), BF16),
            vm((2, T, D), BF16),
            vm(wq.shape, BF16),
            vm(wk.shape, BF16),
            vm(wv.shape, BF16),
            vm((2, 4, T, WIN), BF16),
            vm((2, WIN, 4 * T), BF16),
            vm((2, 4, T, 256), BF16),
            vm((2, 4, T, D), BF16),
            vm((WIN, 512), BF16),
            vm((WIN, 256), BF16),
            vm((3, 144, 512), BF16),
            vm((3, 144, 256), BF16),
            vm((144, 512), F32),
            vm((144, 256), F32),
            vm((4, 36, 512), BF16),
            vm((4, 36, 256), BF16),
            vm((3, 36, 512), BF16),
            vm((3, 36, 256), BF16),
            vm((3, COLS, T), BF16),
            vm((3, COLS, T), BF16),
            vm((4, COLS, T), F32),
            vm((2, KEYS, D), F32),
            vm((SLOTS, 2, KEYS, D), BF16),
            vm((4, T, 256), BF16),
            vm((4, T, 256), BF16),
            vm((2, T, 256), BF16),
            vm(cot.shape, BF16),
            vm(wo.shape, BF16),
            vm((ROWS, D), BF16),
            vm((ROWS, D), BF16),
            vm((D, ROWS), BF16),
            vm((D, ROWS), BF16),
            vm((SLOTS, KEYS, ROWS), F32),
            vm((SLOTS, KEYS, ROWS), F32),
            vm((KEYS, ROWS), BF16),
            vm((KEYS, ROWS), BF16),
            vm((SLOTS, 8, ROWS), F32),
            vm((8, ROWS), F32),
            vm((8, ROWS), F32),
            vm((8, ROWS), F32),
            vm((D, ROWS), F32),
            vm((D, ROWS), F32),
            vm((4, T, 256), BF16),
            vm((4, T, 256), BF16),
            vm((4, T, 256), BF16),
            vm((4, T, 256), BF16),
            vm((SLOTS, 2, KEYS, D), BF16),
            vm((6, 2, KEYS, D), BF16),
            vm((2, 2, KEYS, D), BF16),
            vm((2, 2, 2, T, D), BF16),
            vm((2, T, D), BF16),
            vm((2, T, D), BF16),
            dma((10,)), dma((2,)), dma((2,)), dma((3,)), dma((3,)), dma((3,)), dma((3,)),
            dma((2,)), dma((6,)), dma((SLOTS,)), dma, dma, dma((3,)), dma((3,)), dma((3,)), dma((3,)),
            dma((6,)), dma((6,)), dma((2, 2)), dma((2, 2)), dma, dma,
            dma((4,)), dma((4,)), dma((2, 3)), dma((2, 3)), *([dma((3,))] * 2), *([dma((3,))] * 2), *([dma((3,))] * 10),
        ],
        compiler_params=pltpu.CompilerParams(
            collective_id=1, has_side_effects=True, vmem_limit_bytes=62 * 1024 * 1024
        ),
        name="layer",
    )(xn, q, k, v, wq, wk, wv, wo, cot)


def hand_over(*refs):
    for n in range(3):
        refs[3 + n][...] = refs[n][...]


def local(*args):
    results = layer(*args)
    vmem = tuple(pl.BlockSpec(memory_space=pltpu.VMEM) for _ in range(3))
    grad_input, grad_wvalue, grad_woutput = pl.pallas_call(
        hand_over,
        out_shape=tuple(jax.ShapeDtypeStruct(a.shape, a.dtype) for a in results),
        in_specs=vmem,
        out_specs=vmem,
        name="hand_over",
    )(*results)
    return grad_input.T, grad_wvalue, grad_woutput.T


def solution(mesh):
    seq, both, cols, rows = P("seq", None), P("seq", "head"), P(None, "head"), P("head", None)
    return jax.shard_map(
        local,
        mesh=mesh,
        in_specs=(seq, both, both, both, cols, cols, cols, rows, seq),
        out_specs=(both, both, P("head", "seq")),
        check_vma=False,
    )
```

```python
import functools
import math

import jax
import jax.numpy as jnp
from jax import lax
from jax.experimental import pallas as pl
from jax.experimental.pallas import tpu as pltpu
from jax.sharding import PartitionSpec as P

MESH = pl.DeviceIdType.MESH
F32 = jnp.float32
BF16 = jnp.bfloat16
LOGIT_SCALE = 1.0 / 12.0
EXP2_SCALE = LOGIT_SCALE * math.log2(math.e)
NEG = -1e30
T = 128
D = 128
SLOTS = 9
ROWS = 1024
WIN = 640
COLS = 576
KEYS = 256
NT = (((1,), (1,)), ((), ()))


def dot(a, b):
    return jnp.dot(a, b, preferred_element_type=F32)


def place():
    i = lax.axis_index("seq")
    h = lax.axis_index("head")
    x = lax.div(i, 16)
    y = lax.rem(lax.div(i, 4), 4)
    z = lax.rem(i, 4)
    return i, h, x, y, z


def layer_kernel(
    x_hbm, q_hbm, k_hbm, v_hbm, wq_hbm, wk_hbm, wv_hbm, wo_hbm, cot_hbm,
    gi_o, gwv_o, gwo_o,
    attn_o, gq_o, gk_o, gv_o, wq, wk, wv, win, winT, ag, gvg, po, pv, yo, yv, zso, zsv, zpo, zpv, zio, ziv, tb, hin,
    tq, facc, kv, qg, dog, og, cot, wo, q2, do2, qT, doT, sbuf, dpbuf, pb_s, ds_s, ms, st, st_in, fin,
    oT, dqT, osend, oin, dqsend, dqin, dkv, rbuf, csend, cin, finkv, pin,
    lsem, pair_s, pair_r, q_s, q_r, do_s, do_r, kvx_s, kvy_s, kv_r, st_s, st_r, o_s, o_r, dq_s, dq_r,
    rb_s, rb_r, c_s, c_r, f_s, f_r,
    fx_s, fx_r, w_s, w_r, ag_s, ag_r, gg_s, gg_r, yo_s, yo_r, yv_s, yv_r, zo_s, zo_r, zv_s, zv_r, h_s, h_r,
):
    i, h, x, y, z = place()
    e, f = lax.rem(z, 2), lax.div(z, 2)
    S = x * 4 + y

    def dev(x_, y_, z_):
        return (x_ * 16 + y_ * 4 + z_, h)

    def wrap(a):
        return lax.rem(a + 4, 4)

    def remote(src, dst, s, r, to):
        return pltpu.make_async_remote_copy(
            src_ref=src, dst_ref=dst, send_sem=s, recv_sem=r, device_id=to, device_id_type=MESH
        )

    erow = pl.multiple_of(e * T, T)
    prow = pl.multiple_of((1 - e) * T, T)
    ecol2 = pl.multiple_of(e * 256, 256)
    c_wo = pltpu.make_async_copy(wo_hbm, wo, lsem.at[0])
    c_cot = pltpu.make_async_copy(cot_hbm, cot, lsem.at[1])
    c_k = pltpu.make_async_copy(k_hbm.at[:, pl.ds(erow, D)], kv.at[0, 0, pl.ds(erow, T), :], lsem.at[2])
    c_v = pltpu.make_async_copy(v_hbm.at[:, pl.ds(erow, D)], kv.at[0, 1, pl.ds(erow, T), :], lsem.at[3])
    c_q = pltpu.make_async_copy(q_hbm.at[:, pl.ds(ecol2, 256)], qg.at[z], lsem.at[4])
    for c in (c_wo, c_cot, c_k, c_v, c_q):
        c.start()

    def window(xt):
        return pl.ds(pl.multiple_of(lax.div(9 * xt, 2) * 128, 128), WIN)

    c_win = [
        pltpu.make_async_copy(src.at[:, window(x)], win.at[n, x], lsem.at[5 + n]) for n, src in ((0, x_hbm), (1, cot_hbm))
    ]
    c_w = [pltpu.make_async_copy(src, dst, lsem.at[7 + n]) for n, (src, dst) in enumerate(((wq_hbm, wq), (wk_hbm, wk), (wv_hbm, wv)))]

    bar = pltpu.get_barrier_semaphore()
    for r in (1, 2, 3):
        for to in (dev(x, y, wrap(z + r)), dev(x, wrap(y + r), z), dev(wrap(x + r), y, z)):
            pl.semaphore_signal(bar, inc=1, device_id=to, device_id_type=MESH)
    hc = h + 1 - 2 * lax.rem(h, 2)
    hz = lax.rem(h + 2, 4)
    for to in ((i, hc), (i, hz)):
        pl.semaphore_signal(bar, inc=1, device_id=to, device_id_type=MESH)
    zp = z + 1 - 2 * e
    for r in (1, 2, 3):
        pl.semaphore_signal(bar, inc=1, device_id=dev(wrap(x + r), y, zp), device_id_type=MESH)
    pl.semaphore_wait(bar, 14)

    pair = [
        remote(src.at[:, pl.ds(prow, D)], kv.at[0, n, pl.ds(erow, T), :], pair_s.at[n], pair_r.at[n], dev(x, y, zp))
        for n, src in ((0, k_hbm), (1, v_hbm))
    ]
    for c in pair:
        c.start()

    first = [
        remote(src.at[:, pl.ds(col, D)], kv.at[4, n, pl.ds(erow, T), :], fx_s.at[m + n], fx_r.at[m + n], dev(wrap(x + 1), y, zt))
        for m, col, zt in ((0, erow, z), (2, prow, zp))
        for n, src in ((0, k_hbm), (1, v_hbm))
    ]

    @pl.when(x < 3)
    def _():
        for c in first:
            c.start()

    def gathered(src_of, buf, s, r_):
        copies = []
        for r in (1, 2, 3):
            zt = wrap(z + r)
            copies.append(remote(src_of(zt), buf.at[z], s.at[r - 1], r_.at[r - 1], dev(x, y, zt)))
        return copies

    qcopies = gathered(
        lambda zt: q_hbm.at[:, pl.ds(pl.multiple_of(lax.rem(zt, 2) * 256, 256), 256)], qg, q_s, q_r
    )
    for c in qcopies:
        c.start()

    c_wo.wait()
    c_cot.wait()
    grad = lax.dot_general(cot[...], wo[...], NT, preferred_element_type=F32).astype(BF16)
    og[0] = grad[:, :256]
    og[1] = grad[:, 256:]
    docopies = gathered(lambda zt: og.at[lax.rem(zt, 2)], dog, do_s, do_r)
    for c in docopies:
        c.start()
    dog[z] = og[e]

    c_k.wait()
    c_v.wait()
    for c in pair:
        c.wait_recv()

    def fwd_x(src, dst):
        return remote(kv.at[src], kv.at[dst], kvx_s.at[dst // 8], kv_r.at[dst], dev(wrap(x + 1), y, z))

    def fwd_y(r, kind):
        yt = wrap(y + r)
        up = yt > y
        if kind == 0:
            src, dst = 4, 4 + yt - y
        else:
            src, dst = jnp.where(up, 0, 8), jnp.where(up, yt - y, 8 + yt - y)
        return remote(kv.at[src], kv.at[dst], kvy_s.at[kind * 3 + r - 1], kv_r.at[dst], dev(x, yt, z))

    for r in (1, 2, 3):
        @pl.when(y + r < 4)
        def _():
            fwd_y(r, 1).start()

    def recv_slot(d):
        remote(kv.at[d], kv.at[d], kvx_s.at[0], kv_r.at[d], dev(wrap(x + 1), y, z)).wait_recv()

    @pl.when(x >= 1)
    def _():
        for c in first:
            c.wait_recv()
        for r in (1, 2, 3):
            fwd_y(r, 0).start()

    @pl.when((x >= 1) & (x < 3))
    def _():
        fwd_x(4, 8).start()

    wcopies = []
    for r in (1, 2, 3):
        xt = wrap(x + r)
        for n, src in ((0, x_hbm), (1, cot_hbm)):
            wcopies.append(
                remote(src.at[:, window(xt)], win.at[n, x], w_s.at[n, r - 1], w_r.at[n, r - 1], dev(xt, y, z))
            )

    c_q.wait()
    for c in qcopies:
        c.wait_recv()

    @pl.loop(0, 4)
    def _(zz):
        for j in range(2):
            rows = pl.ds(pl.multiple_of(j * 512 + zz * T, T), T)
            qb = qg[zz, :, j * D : (j + 1) * D]
            q2[rows, :] = qb
            qT[:, rows] = qb.T

    st[...] = jnp.concatenate([jnp.full((1, ROWS), NEG, F32), jnp.zeros((7, ROWS), F32)], axis=0)
    oT[...] = jnp.zeros_like(oT)
    dqT[...] = jnp.zeros_like(dqT)

    def slot_of(kind, r):
        if kind == 0:
            return 4 + jnp.where(r <= y, r, r - 4)
        return jnp.where(r <= y, r, r + 4)

    def probabilities(d, edge):
        kd = kv[d, 0]
        vt = kv[d, 1].T
        low = jnp.where(d == 0, 0, -100000)
        high = jnp.where(d == 8, 0, 100000)
        for c in range(4):
            cs = slice(c * 256, (c + 1) * 256)
            s = dot(kd, qT[:, cs])
            if edge:
                gap = (
                    lax.broadcasted_iota(jnp.int32, (KEYS, 256), 1)
                    - lax.broadcasted_iota(jnp.int32, (KEYS, 256), 0)
                    + ((c % 2) * 256 - f * 256)
                )
                s = jnp.where((gap >= low) & (gap < high), s, NEG)
            before = st[0:1, cs]
            top = jnp.maximum(before, jnp.max(s, axis=0, keepdims=True))
            p = jnp.exp2((s - top) * EXP2_SCALE)
            keep = jnp.exp2((before - top) * EXP2_SCALE)
            st[0:1, cs] = top
            st[1:2, cs] = st[1:2, cs] * keep + jnp.sum(p, axis=0, keepdims=True)
            ms[d, 0:1, cs] = top
            sbuf[d, :, cs] = p
            oT[:, cs] = oT[:, cs] * keep + dot(vt, p.astype(BF16))

    def prob_step(t):
        kind = (t >= 5) & (t < 8)
        r = jnp.where(t < 4, t, jnp.where(t < 8, t - 4, t - 8))
        d = jnp.where(r == 0, t, jnp.where(kind, slot_of(0, r), slot_of(1, r)))
        fits = (r == 0) | kind | jnp.where(t < 4, r <= y, r > y)

        @pl.when((S >= d) & fits & (r == 0) & (t != 4))
        def _():
            probabilities(d, True)

        @pl.when((S >= d) & fits & ((r > 0) | (t == 4)))
        def _():
            @pl.when(r > 0)
            def _():
                recv_slot(d)

            probabilities(d, False)

    pl.loop(0, 5)(prob_step)

    @pl.when(x >= 2)
    def _():
        recv_slot(8)
        for r in (1, 2, 3):
            @pl.when(y + r >= 4)
            def _():
                fwd_y(r, 1).start()

    pl.loop(5, 12)(prob_step)

    for c in docopies:
        c.wait_recv()
    for c in wcopies + c_win + c_w:
        c.start()

    @pl.loop(0, 4)
    def _(zz):
        for j in range(2):
            rows = pl.ds(pl.multiple_of(j * 512 + zz * T, T), T)
            db = dog[zz, :, j * D : (j + 1) * D]
            do2[rows, :] = db
            doT[:, rows] = db.T

    @pl.loop(0, SLOTS)
    def _(d):
        @pl.when(S >= d)
        def _():
            vd = kv[d, 1]
            scale = jnp.exp2((ms[d, 0:1, :] - st[0:1, :]) * EXP2_SCALE)
            for c in range(4):
                cs = slice(c * 256, (c + 1) * 256)
                dp = dot(vd, doT[:, cs])
                dpbuf[d, :, cs] = dp
                st[2:3, cs] += scale[:, cs] * jnp.sum(sbuf[d, :, cs] * dp, axis=0, keepdims=True)

    stat = remote(st, st_in, st_s, st_r, dev(x, y, wrap(z + 2)))
    stat.start()
    stat.wait()
    top = jnp.maximum(st[0:1, :], st_in[0:1, :])
    mine = jnp.exp2((st[0:1, :] - top) * EXP2_SCALE)
    other = jnp.exp2((st_in[0:1, :] - top) * EXP2_SCALE)
    inv = 1.0 / (st[1:2, :] * mine + st_in[1:2, :] * other)
    fin[0:1, :] = top
    fin[1:2, :] = inv
    fin[2:3, :] = (st[2:3, :] * mine + st_in[2:3, :] * other) * inv
    oT[...] = oT[...] * (mine * inv)

    def spread(srcT, factor, sendbuf, inbuf, s, r_):
        for j in range(2):
            for zz in range(4):
                piece = srcT[:, j * 512 + zz * T : j * 512 + (zz + 1) * T]
                sendbuf[zz, :, j * D : (j + 1) * D] = (piece * factor).T.astype(BF16)
        copies = []
        for r in (1, 2, 3):
            zt = wrap(z + r)
            copies.append(remote(sendbuf.at[zt], inbuf.at[z], s.at[r - 1], r_.at[r - 1], dev(x, y, zt)))
        for c in copies:
            c.start()
        inbuf[z] = sendbuf[z]
        return copies

    ocopies = spread(oT, 1.0, osend, oin, o_s, o_r)

    def grad_slot(d):
        w = jnp.exp2((ms[d, 0:1, :] - fin[0:1, :]) * EXP2_SCALE) * fin[1:2, :]
        kt = kv[d, 0].T
        for c in range(4):
            cs = slice(c * 256, (c + 1) * 256)
            p = sbuf[d, :, cs] * w[:, cs]
            pb_s[:, cs] = p.astype(BF16)
            ds = (p * (dpbuf[d, :, cs] - fin[2:3, cs])).astype(BF16)
            ds_s[:, cs] = ds
            dqT[:, cs] += dot(kt, ds)
        dkv[d, 0] = (LOGIT_SCALE * dot(ds_s[...], q2[...])).astype(BF16)
        dkv[d, 1] = dot(pb_s[...], do2[...]).astype(BF16)

    def back_y(kind, r):
        d = slot_of(kind, r)
        n = kind * 3 + r - 1
        return remote(dkv.at[d], rbuf.at[n], rb_s.at[n], rb_r.at[n], dev(x, wrap(y - r), z))

    def grad_step(t):
        kind = (t >= 4) & (t < 7)
        r = jnp.where(t < 3, t + 1, jnp.where(kind, t - 3, jnp.where((t >= 8) & (t < 11), t - 7, 0)))
        d = jnp.where(r == 0, jnp.where(t == 3, 8, jnp.where(t == 7, 4, 0)), jnp.where(kind, slot_of(0, r), slot_of(1, r)))
        fits = (r == 0) | kind | jnp.where(t < 3, r > y, r <= y)

        @pl.when((S >= d) & fits)
        def _():
            grad_slot(d)

            @pl.when(r > 0)
            def _():
                n = jnp.where(kind, r - 1, r + 2)
                remote(dkv.at[d], rbuf.at[n], rb_s.at[n], rb_r.at[n], dev(x, wrap(y - r), z)).start()

    pl.loop(0, 8)(grad_step)

    def recv_back(n):
        remote(rbuf.at[n], rbuf.at[n], rb_s.at[n], rb_r.at[n], dev(x, wrap(y + 1), z)).wait_recv()

    chain8, chain4 = (
        [
            remote(
                csend.at[m, :, pl.ds(row, T), :], cin.at[m, part], c_s.at[m, part], c_r.at[m, part], dev(wrap(x - 2 + m), y, zt)
            )
            for part, row, zt in ((0, erow, z), (1, prow, zp))
        ]
        for m in range(2)
    )

    @pl.when(x >= 2)
    def _():
        facc[...] = dkv[8].astype(F32)
        for r in (1, 2, 3):
            @pl.when(y + r >= 4)
            def _():
                recv_back(3 + r - 1)
                facc[...] += rbuf[3 + r - 1].astype(F32)

        csend[0] = facc[...].astype(BF16)
        for c in chain8:
            c.start()

    pl.loop(8, 12)(grad_step)

    dqcopies = spread(dqT, LOGIT_SCALE, dqsend, dqin, dq_s, dq_r)

    def over_x(src, dst, s, r_):
        return [remote(src, dst, s.at[r - 1], r_.at[r - 1], dev(wrap(x + r), y, z)) for r in (1, 2, 3)]

    for c in ocopies:
        c.wait_recv()
    for n in range(2):
        attn_o[n] = (oin[n].astype(F32) + oin[n + 2].astype(F32)).astype(BF16)
    agcopies = over_x(attn_o, ag.at[:, x], ag_s, ag_r)
    for c in agcopies:
        c.start()
    ag[:, x] = attn_o[...]


    for c in c_win:
        c.wait()
    for c in wcopies:
        c.wait_recv()

    @pl.loop(0, 4)
    def _(xx):
        for n in range(2):
            for b in range(WIN // 128):
                cols = slice(b * 128, (b + 1) * 128)
                winT[n, cols, pl.ds(pl.multiple_of(xx * T, T), T)] = win[n, xx, :, cols].T

    @pl.when(x >= 1)
    def _():
        facc[...] = dkv[4].astype(F32)
        for r in (1, 2, 3):
            recv_back(r - 1)
            facc[...] += rbuf[r - 1].astype(F32)
        csend[1] = facc[...].astype(BF16)
        for c in chain4:
            c.start()

    off = pl.multiple_of(64 * lax.rem(x, 2), 16)

    def over_y(src, buf, s, r_):
        copies = []
        for r in (1, 2, 3):
            yt = wrap(y + r)
            rows = pl.ds(pl.multiple_of(off + 144 * yt, 16), 144)
            copies.append(remote(src.at[rows, :], buf.at[r - 1], s.at[r - 1], r_.at[r - 1], dev(x, yt, z)))
        return copies

    facc[...] = dkv[0].astype(F32)
    for r in (1, 2, 3):
        @pl.when(y + r < 4)
        def _():
            recv_back(3 + r - 1)
            facc[...] += rbuf[3 + r - 1].astype(F32)

    finkv[...] = facc[:, pl.ds(prow, T), :].astype(BF16)
    swap = [remote(finkv, pin, f_s, f_r, dev(x, y, zp))]
    swap[0].start()

    for c in dqcopies:
        c.wait_recv()
    for n in range(2):
        gq_o[n] = (dqin[n].astype(F32) + dqin[n + 2].astype(F32)).astype(BF16)
    for c in c_w:
        c.wait()

    def wrows(hh):
        return pl.ds(pl.multiple_of(COLS * hh, 16), COLS)

    @pl.loop(0, 4)
    def _(hh):
        tq[hh] = sum(
            lax.dot_general(wq[wrows(hh), n * 256 : (n + 1) * 256], gq_o[n], NT, preferred_element_type=F32)
            for n in range(2)
        )

    for c in agcopies:
        c.wait_recv()
    for n in range(2):
        po[:, n * 256 : (n + 1) * 256] = dot(winT[1], ag[n].reshape(4 * T, 256)).astype(BF16)
    yocopies = over_y(po, yo, yo_s, yo_r)
    for c in yocopies:
        c.start()

    swap[0].wait_recv()
    ggcopies = over_x(gv_o, gvg.at[:, x], gg_s, gg_r)
    for m, chain in enumerate((chain8, chain4)):
        @pl.when(x < 2 + m)
        def _():
            for c in chain:
                c.wait_recv()

    for n, out in ((1, gv_o), (0, gk_o)):
        parts = [facc[n, pl.ds(erow, T), :], pin[n].astype(F32)]
        for m in (0, 1):
            parts = [a + jnp.where(x < 2 + m, cin[m, part, n].astype(F32), 0.0) for part, a in enumerate(parts)]
        out[e] = parts[0].astype(BF16)
        out[1 - e] = parts[1].astype(BF16)
        if n == 1:
            for c in ggcopies:
                c.start()
    gvg[:, x] = gv_o[...]

    def terms(hh):
        acc = tq[hh]
        for n in range(2):
            acc = acc + lax.dot_general(wk[wrows(hh), n * D : (n + 1) * D], gk_o[n], NT, preferred_element_type=F32)
            acc = acc + lax.dot_general(wv[wrows(hh), n * D : (n + 1) * D], gv_o[n], NT, preferred_element_type=F32)
        return acc

    hzc = lax.rem(hc + 2, 4)
    tb[0] = terms(hzc).astype(BF16)
    far = remote(tb.at[0], hin.at[0], h_s.at[0], h_r.at[0], (i, hc))
    far.start()
    mine_far = terms(hz)
    far.wait_recv()
    tb[1] = (mine_far + hin[0].astype(F32)).astype(BF16)
    across = remote(tb.at[1], hin.at[1], h_s.at[1], h_r.at[1], (i, hz))
    across.start()
    for c in ggcopies:
        c.wait_recv()
    for n in range(2):
        pv[:, n * D : (n + 1) * D] = dot(winT[0], gvg[n].reshape(4 * T, D)).astype(BF16)
    yvcopies = over_y(pv, yv, yv_s, yv_r)
    for c in yvcopies:
        c.start()

    tb[2] = terms(hc).astype(BF16)
    near = remote(tb.at[2], hin.at[2], h_s.at[2], h_r.at[2], (i, hc))
    near.start()

    def over_z(copies, own, buf, total_s, piece_s, in_s, s, r_):
        for c in copies:
            c.wait_recv()
        acc = own[pl.ds(pl.multiple_of(off + 144 * y, 16), 144), :].astype(F32)
        for r in range(3):
            acc = acc + buf[r].astype(F32)
        total_s[...] = acc
        for zz in range(4):
            piece_s[zz] = total_s[36 * zz : 36 * (zz + 1), :].astype(piece_s.dtype)
        out = []
        for r in (1, 2, 3):
            zt = wrap(z + r)
            out.append(remote(piece_s.at[zt], in_s.at[r - 1], s.at[r - 1], r_.at[r - 1], dev(x, y, zt)))
        for c in out:
            c.start()
        return out

    zocopies = over_z(yocopies, po, yo, zso, zpo, zio, zo_s, zo_r)
    mine_near = terms(h)
    zvcopies = over_z(yvcopies, pv, yv, zsv, zpv, ziv, zv_s, zv_r)

    for c in zocopies:
        c.wait_recv()
    acc = zpo[z].astype(F32)
    for r in range(3):
        acc = acc + zio[r].astype(F32)
    gwo_o[...] = acc
    near.wait_recv()
    across.wait_recv()
    gi_o[...] = (mine_near + hin[2].astype(F32) + hin[1].astype(F32)).astype(BF16)
    for c in zvcopies:
        c.wait_recv()
    acc = zpv[z].astype(F32)
    for r in range(3):
        acc = acc + ziv[r].astype(F32)
    gwv_o[...] = acc

    for c in (
        pair + qcopies + docopies + ocopies + dqcopies + swap + wcopies + agcopies + ggcopies
        + yocopies + yvcopies + zocopies + zvcopies + [far, across, near]
    ):
        c.wait_send()

    @pl.when(x < 3)
    def _():
        for c in first:
            c.wait_send()

    @pl.when((x >= 1) & (x < 3))
    def _():
        fwd_x(4, 8).wait_send()

    for r in (1, 2, 3):
        @pl.when((y + r < 4) | (x >= 2))
        def _():
            fwd_y(r, 1).wait_send()

        @pl.when(x >= 1)
        def _():
            fwd_y(r, 0).wait_send()
            back_y(0, r).wait_send()

        @pl.when((r <= y) | (x >= 2))
        def _():
            back_y(1, r).wait_send()

    @pl.when(x >= 2)
    def _():
        for c in chain8:
            c.wait_send()

    @pl.when(x >= 1)
    def _():
        for c in chain4:
            c.wait_send()


def layer(xn, q, k, v, wq, wk, wv, wo, cot):
    dma = pltpu.SemaphoreType.DMA
    vm = pltpu.VMEM
    return pl.pallas_call(
        layer_kernel,
        out_shape=(
            jax.ShapeDtypeStruct((COLS, T), BF16),
            jax.ShapeDtypeStruct((36, 256), F32),
            jax.ShapeDtypeStruct((36, 512), F32),
        ),
        in_specs=[pl.BlockSpec(memory_space=pl.ANY)] * 9,
        out_specs=tuple(pl.BlockSpec(memory_space=pltpu.VMEM) for _ in range(3)),
        scratch_shapes=[
            vm((2, T, 256), BF16),
            vm((2, T, 256), BF16),
            vm((2, T, D), BF16),
            vm((2, T, D), BF16),
            vm(wq.shape, BF16),
            vm(wk.shape, BF16),
            vm(wv.shape, BF16),
            vm((2, 4, T, WIN), BF16),
            vm((2, WIN, 4 * T), BF16),
            vm((2, 4, T, 256), BF16),
            vm((2, 4, T, D), BF16),
            vm((WIN, 512), BF16),
            vm((WIN, 256), BF16),
            vm((3, 144, 512), BF16),
            vm((3, 144, 256), BF16),
            vm((144, 512), F32),
            vm((144, 256), F32),
            vm((4, 36, 512), BF16),
            vm((4, 36, 256), BF16),
            vm((3, 36, 512), BF16),
            vm((3, 36, 256), BF16),
            vm((3, COLS, T), BF16),
            vm((3, COLS, T), BF16),
            vm((4, COLS, T), F32),
            vm((2, KEYS, D), F32),
            vm((SLOTS, 2, KEYS, D), BF16),
            vm((4, T, 256), BF16),
            vm((4, T, 256), BF16),
            vm((2, T, 256), BF16),
            vm(cot.shape, BF16),
            vm(wo.shape, BF16),
            vm((ROWS, D), BF16),
            vm((ROWS, D), BF16),
            vm((D, ROWS), BF16),
            vm((D, ROWS), BF16),
            vm((SLOTS, KEYS, ROWS), F32),
            vm((SLOTS, KEYS, ROWS), F32),
            vm((KEYS, ROWS), BF16),
            vm((KEYS, ROWS), BF16),
            vm((SLOTS, 8, ROWS), F32),
            vm((8, ROWS), F32),
            vm((8, ROWS), F32),
            vm((8, ROWS), F32),
            vm((D, ROWS), F32),
            vm((D, ROWS), F32),
            vm((4, T, 256), BF16),
            vm((4, T, 256), BF16),
            vm((4, T, 256), BF16),
            vm((4, T, 256), BF16),
            vm((SLOTS, 2, KEYS, D), BF16),
            vm((6, 2, KEYS, D), BF16),
            vm((2, 2, KEYS, D), BF16),
            vm((2, 2, 2, T, D), BF16),
            vm((2, T, D), BF16),
            vm((2, T, D), BF16),
            dma((10,)), dma((2,)), dma((2,)), dma((3,)), dma((3,)), dma((3,)), dma((3,)),
            dma((2,)), dma((6,)), dma((SLOTS,)), dma, dma, dma((3,)), dma((3,)), dma((3,)), dma((3,)),
            dma((6,)), dma((6,)), dma((2, 2)), dma((2, 2)), dma, dma,
            dma((4,)), dma((4,)), dma((2, 3)), dma((2, 3)), *([dma((3,))] * 2), *([dma((3,))] * 2), *([dma((3,))] * 10),
        ],
        compiler_params=pltpu.CompilerParams(
            collective_id=1, has_side_effects=True, vmem_limit_bytes=62 * 1024 * 1024
        ),
        name="layer",
    )(xn, q, k, v, wq, wk, wv, wo, cot)


def hand_over(*refs):
    for n in range(3):
        refs[3 + n][...] = refs[n][...]


def local(*args):
    results = layer(*args)
    vmem = tuple(pl.BlockSpec(memory_space=pltpu.VMEM) for _ in range(3))
    grad_input, grad_wvalue, grad_woutput = pl.pallas_call(
        hand_over,
        out_shape=tuple(jax.ShapeDtypeStruct(a.shape, a.dtype) for a in results),
        in_specs=vmem,
        out_specs=vmem,
        name="hand_over",
    )(*results)
    return grad_input.T, grad_wvalue, grad_woutput.T


def solution(mesh):
    seq, both, cols, rows = P("seq", None), P("seq", "head"), P(None, "head"), P("head", None)
    return jax.shard_map(
        local,
        mesh=mesh,
        in_specs=(seq, both, both, both, cols, cols, cols, rows, seq),
        out_specs=(both, both, P("head", "seq")),
        check_vma=False,
    )
```

```python
import functools
import math

import jax
import jax.numpy as jnp
from jax import lax
from jax.experimental import pallas as pl
from jax.experimental.pallas import tpu as pltpu
from jax.sharding import PartitionSpec as P

MESH = pl.DeviceIdType.MESH
F32 = jnp.float32
BF16 = jnp.bfloat16
LOGIT_SCALE = 1.0 / 12.0
EXP2_SCALE = LOGIT_SCALE * math.log2(math.e)
NEG = -1e30
T = 128
D = 128
SLOTS = 9
ROWS = 1024
WIN = 640
COLS = 576
KEYS = 256
NT = (((1,), (1,)), ((), ()))


def dot(a, b):
    return jnp.dot(a, b, preferred_element_type=F32)


def place():
    i = lax.axis_index("seq")
    h = lax.axis_index("head")
    x = lax.div(i, 16)
    y = lax.rem(lax.div(i, 4), 4)
    z = lax.rem(i, 4)
    return i, h, x, y, z


def layer_kernel(
    x_hbm, q_hbm, k_hbm, v_hbm, wq_hbm, wk_hbm, wv_hbm, wo_hbm, cot_hbm,
    gi_o, gwv_o, gwo_o,
    attn_o, gq_o, gk_o, gv_o, wq, wk, wv, win, winT, ag, gvg, po, pv, yo, yv, zso, zsv, zpo, zpv, zio, ziv, tb, hin,
    tq, facc, kv, qg, dog, og, cot, wo, q2, do2, qT, doT, sbuf, dpbuf, pb_s, ds_s, ms, st, st_in, fin,
    oT, dqT, osend, oin, dqsend, dqin, dkv, rbuf, csend, cin, finkv, pin,
    lsem, pair_s, pair_r, q_s, q_r, do_s, do_r, kvx_s, kvy_s, kv_r, st_s, st_r, o_s, o_r, dq_s, dq_r,
    rb_s, rb_r, c_s, c_r, f_s, f_r,
    fx_s, fx_r, w_s, w_r, ag_s, ag_r, gg_s, gg_r, yo_s, yo_r, yv_s, yv_r, zo_s, zo_r, zv_s, zv_r, h_s, h_r,
):
    i, h, x, y, z = place()
    e, f = lax.rem(z, 2), lax.div(z, 2)
    S = x * 4 + y

    def dev(x_, y_, z_):
        return (x_ * 16 + y_ * 4 + z_, h)

    def wrap(a):
        return lax.rem(a + 4, 4)

    def remote(src, dst, s, r, to):
        return pltpu.make_async_remote_copy(
            src_ref=src, dst_ref=dst, send_sem=s, recv_sem=r, device_id=to, device_id_type=MESH
        )

    erow = pl.multiple_of(e * T, T)
    prow = pl.multiple_of((1 - e) * T, T)
    ecol2 = pl.multiple_of(e * 256, 256)
    c_wo = pltpu.make_async_copy(wo_hbm, wo, lsem.at[0])
    c_cot = pltpu.make_async_copy(cot_hbm, cot, lsem.at[1])
    c_k = pltpu.make_async_copy(k_hbm.at[:, pl.ds(erow, D)], kv.at[0, 0, pl.ds(erow, T), :], lsem.at[2])
    c_v = pltpu.make_async_copy(v_hbm.at[:, pl.ds(erow, D)], kv.at[0, 1, pl.ds(erow, T), :], lsem.at[3])
    c_q = pltpu.make_async_copy(q_hbm.at[:, pl.ds(ecol2, 256)], qg.at[z], lsem.at[4])
    for c in (c_wo, c_cot, c_k, c_v, c_q):
        c.start()

    def window(xt):
        return pl.ds(pl.multiple_of(lax.div(9 * xt, 2) * 128, 128), WIN)

    c_win = [
        pltpu.make_async_copy(src.at[:, window(x)], win.at[n, x], lsem.at[5 + n]) for n, src in ((0, x_hbm), (1, cot_hbm))
    ]
    c_w = [pltpu.make_async_copy(src, dst, lsem.at[7 + n]) for n, (src, dst) in enumerate(((wq_hbm, wq), (wk_hbm, wk), (wv_hbm, wv)))]

    bar = pltpu.get_barrier_semaphore()
    for r in (1, 2, 3):
        for to in (dev(x, y, wrap(z + r)), dev(x, wrap(y + r), z), dev(wrap(x + r), y, z)):
            pl.semaphore_signal(bar, inc=1, device_id=to, device_id_type=MESH)
    hc = h + 1 - 2 * lax.rem(h, 2)
    hz = lax.rem(h + 2, 4)
    for to in ((i, hc), (i, hz)):
        pl.semaphore_signal(bar, inc=1, device_id=to, device_id_type=MESH)
    zp = z + 1 - 2 * e
    for r in (1, 2, 3):
        pl.semaphore_signal(bar, inc=1, device_id=dev(wrap(x + r), y, zp), device_id_type=MESH)
    pl.semaphore_wait(bar, 14)

    pair = [
        remote(src.at[:, pl.ds(prow, D)], kv.at[0, n, pl.ds(erow, T), :], pair_s.at[n], pair_r.at[n], dev(x, y, zp))
        for n, src in ((0, k_hbm), (1, v_hbm))
    ]
    for c in pair:
        c.start()

    first = [
        remote(src.at[:, pl.ds(col, D)], kv.at[4, n, pl.ds(erow, T), :], fx_s.at[m + n], fx_r.at[m + n], dev(wrap(x + 1), y, zt))
        for m, col, zt in ((0, erow, z), (2, prow, zp))
        for n, src in ((0, k_hbm), (1, v_hbm))
    ]

    @pl.when(x < 3)
    def _():
        for c in first:
            c.start()

    def gathered(src_of, buf, s, r_):
        copies = []
        for r in (1, 2, 3):
            zt = wrap(z + r)
            copies.append(remote(src_of(zt), buf.at[z], s.at[r - 1], r_.at[r - 1], dev(x, y, zt)))
        return copies

    qcopies = gathered(
        lambda zt: q_hbm.at[:, pl.ds(pl.multiple_of(lax.rem(zt, 2) * 256, 256), 256)], qg, q_s, q_r
    )
    for c in qcopies:
        c.start()

    c_wo.wait()
    c_cot.wait()
    grad = lax.dot_general(cot[...], wo[...], NT, preferred_element_type=F32).astype(BF16)
    og[0] = grad[:, :256]
    og[1] = grad[:, 256:]
    docopies = gathered(lambda zt: og.at[lax.rem(zt, 2)], dog, do_s, do_r)
    for c in docopies:
        c.start()
    dog[z] = og[e]

    c_k.wait()
    c_v.wait()
    for c in pair:
        c.wait_recv()

    def fwd_x(src, dst):
        return remote(kv.at[src], kv.at[dst], kvx_s.at[dst // 8], kv_r.at[dst], dev(wrap(x + 1), y, z))

    def fwd_y(r, kind):
        yt = wrap(y + r)
        up = yt > y
        if kind == 0:
            src, dst = 4, 4 + yt - y
        else:
            src, dst = jnp.where(up, 0, 8), jnp.where(up, yt - y, 8 + yt - y)
        return remote(kv.at[src], kv.at[dst], kvy_s.at[kind * 3 + r - 1], kv_r.at[dst], dev(x, yt, z))

    for r in (1, 2, 3):
        @pl.when(y + r < 4)
        def _():
            fwd_y(r, 1).start()

    def recv_slot(d):
        remote(kv.at[d], kv.at[d], kvx_s.at[0], kv_r.at[d], dev(wrap(x + 1), y, z)).wait_recv()

    @pl.when(x >= 1)
    def _():
        for c in first:
            c.wait_recv()
        for r in (1, 2, 3):
            fwd_y(r, 0).start()

    @pl.when((x >= 1) & (x < 3))
    def _():
        fwd_x(4, 8).start()

    wcopies = []
    for r in (1, 2, 3):
        xt = wrap(x + r)
        for n, src in ((0, x_hbm), (1, cot_hbm)):
            wcopies.append(
                remote(src.at[:, window(xt)], win.at[n, x], w_s.at[n, r - 1], w_r.at[n, r - 1], dev(xt, y, z))
            )

    c_q.wait()
    @pl.when(x >= 2)
    def _():
        recv_slot(8)
        for r in (1, 2, 3):
            @pl.when(y + r >= 4)
            def _():
                fwd_y(r, 1).start()

    for c in qcopies:
        c.wait_recv()

    @pl.loop(0, 4)
    def _(zz):
        for j in range(2):
            rows = pl.ds(pl.multiple_of(j * 512 + zz * T, T), T)
            qb = qg[zz, :, j * D : (j + 1) * D]
            q2[rows, :] = qb
            qT[:, rows] = qb.T

    for c in docopies:
        c.wait_recv()
    for c in wcopies + c_win + c_w:
        c.start()

    @pl.loop(0, 4)
    def _(zz):
        for j in range(2):
            rows = pl.ds(pl.multiple_of(j * 512 + zz * T, T), T)
            db = dog[zz, :, j * D : (j + 1) * D]
            do2[rows, :] = db
            doT[:, rows] = db.T

    st[...] = jnp.concatenate([jnp.full((1, ROWS), NEG, F32), jnp.zeros((7, ROWS), F32)], axis=0)
    oT[...] = jnp.zeros_like(oT)
    dqT[...] = jnp.zeros_like(dqT)

    def slot_of(kind, r):
        if kind == 0:
            return 4 + jnp.where(r <= y, r, r - 4)
        return jnp.where(r <= y, r, r + 4)

    def probabilities(d, edge):
        kd = kv[d, 0]
        vd = kv[d, 1]
        vt = vd.T
        low = jnp.where(d == 0, 0, -100000)
        high = jnp.where(d == 8, 0, 100000)
        for c in range(4):
            cs = slice(c * 256, (c + 1) * 256)
            s = dot(kd, qT[:, cs])
            if edge:
                gap = (
                    lax.broadcasted_iota(jnp.int32, (KEYS, 256), 1)
                    - lax.broadcasted_iota(jnp.int32, (KEYS, 256), 0)
                    + ((c % 2) * 256 - f * 256)
                )
                s = jnp.where((gap >= low) & (gap < high), s, NEG)
            before = st[0:1, cs]
            top = jnp.maximum(before, jnp.max(s, axis=0, keepdims=True))
            p = jnp.exp2((s - top) * EXP2_SCALE)
            keep = jnp.exp2((before - top) * EXP2_SCALE)
            dp = dot(vd, doT[:, cs])
            st[0:1, cs] = top
            st[1:2, cs] = st[1:2, cs] * keep + jnp.sum(p, axis=0, keepdims=True)
            st[2:3, cs] = st[2:3, cs] * keep + jnp.sum(p * dp, axis=0, keepdims=True)
            ms[d, 0:1, cs] = top
            sbuf[d, :, cs] = p
            dpbuf[d, :, cs] = dp
            oT[:, cs] = oT[:, cs] * keep + dot(vt, p.astype(BF16))

    def prob_step(t):
        kind = (t >= 5) & (t < 8)
        r = jnp.where(t < 4, t, jnp.where(t < 8, t - 4, t - 8))
        d = jnp.where(r == 0, t, jnp.where(kind, slot_of(0, r), slot_of(1, r)))
        fits = (r == 0) | kind | jnp.where(t < 4, r <= y, r > y)

        @pl.when((S >= d) & fits & (r == 0) & (t != 4))
        def _():
            probabilities(d, True)

        @pl.when((S >= d) & fits & ((r > 0) | (t == 4)))
        def _():
            @pl.when(r > 0)
            def _():
                recv_slot(d)

            probabilities(d, False)

    pl.loop(0, 12)(prob_step)

    stat = remote(st, st_in, st_s, st_r, dev(x, y, wrap(z + 2)))
    stat.start()
    stat.wait()
    top = jnp.maximum(st[0:1, :], st_in[0:1, :])
    mine = jnp.exp2((st[0:1, :] - top) * EXP2_SCALE)
    other = jnp.exp2((st_in[0:1, :] - top) * EXP2_SCALE)
    inv = 1.0 / (st[1:2, :] * mine + st_in[1:2, :] * other)
    fin[0:1, :] = top
    fin[1:2, :] = inv
    fin[2:3, :] = (st[2:3, :] * mine + st_in[2:3, :] * other) * inv
    oT[...] = oT[...] * (mine * inv)

    def spread(srcT, factor, sendbuf, inbuf, s, r_):
        for j in range(2):
            for zz in range(4):
                piece = srcT[:, j * 512 + zz * T : j * 512 + (zz + 1) * T]
                sendbuf[zz, :, j * D : (j + 1) * D] = (piece * factor).T.astype(BF16)
        copies = []
        for r in (1, 2, 3):
            zt = wrap(z + r)
            copies.append(remote(sendbuf.at[zt], inbuf.at[z], s.at[r - 1], r_.at[r - 1], dev(x, y, zt)))
        for c in copies:
            c.start()
        inbuf[z] = sendbuf[z]
        return copies

    ocopies = spread(oT, 1.0, osend, oin, o_s, o_r)

    def grad_slot(d):
        w = jnp.exp2((ms[d, 0:1, :] - fin[0:1, :]) * EXP2_SCALE) * fin[1:2, :]
        kt = kv[d, 0].T
        for c in range(4):
            cs = slice(c * 256, (c + 1) * 256)
            p = sbuf[d, :, cs] * w[:, cs]
            pb_s[:, cs] = p.astype(BF16)
            ds = (p * (dpbuf[d, :, cs] - fin[2:3, cs])).astype(BF16)
            ds_s[:, cs] = ds
            dqT[:, cs] += dot(kt, ds)
        dkv[d, 0] = (LOGIT_SCALE * dot(ds_s[...], q2[...])).astype(BF16)
        dkv[d, 1] = dot(pb_s[...], do2[...]).astype(BF16)

    def back_y(kind, r):
        d = slot_of(kind, r)
        n = kind * 3 + r - 1
        return remote(dkv.at[d], rbuf.at[n], rb_s.at[n], rb_r.at[n], dev(x, wrap(y - r), z))

    def grad_step(t):
        kind = (t >= 4) & (t < 7)
        r = jnp.where(t < 3, t + 1, jnp.where(kind, t - 3, jnp.where((t >= 8) & (t < 11), t - 7, 0)))
        d = jnp.where(r == 0, jnp.where(t == 3, 8, jnp.where(t == 7, 4, 0)), jnp.where(kind, slot_of(0, r), slot_of(1, r)))
        fits = (r == 0) | kind | jnp.where(t < 3, r > y, r <= y)

        @pl.when((S >= d) & fits)
        def _():
            grad_slot(d)

            @pl.when(r > 0)
            def _():
                n = jnp.where(kind, r - 1, r + 2)
                remote(dkv.at[d], rbuf.at[n], rb_s.at[n], rb_r.at[n], dev(x, wrap(y - r), z)).start()

    pl.loop(0, 12)(grad_step)

    def recv_back(n):
        remote(rbuf.at[n], rbuf.at[n], rb_s.at[n], rb_r.at[n], dev(x, wrap(y + 1), z)).wait_recv()

    chain8, chain4 = (
        [
            remote(
                csend.at[m, :, pl.ds(row, T), :], cin.at[m, part], c_s.at[m, part], c_r.at[m, part], dev(wrap(x - 2 + m), y, zt)
            )
            for part, row, zt in ((0, erow, z), (1, prow, zp))
        ]
        for m in range(2)
    )

    @pl.when(x >= 2)
    def _():
        facc[...] = dkv[8].astype(F32)
        for r in (1, 2, 3):
            @pl.when(y + r >= 4)
            def _():
                recv_back(3 + r - 1)
                facc[...] += rbuf[3 + r - 1].astype(F32)

        csend[0] = facc[...].astype(BF16)
        for c in chain8:
            c.start()

    dqcopies = spread(dqT, LOGIT_SCALE, dqsend, dqin, dq_s, dq_r)

    def over_x(src, dst, s, r_):
        return [remote(src, dst, s.at[r - 1], r_.at[r - 1], dev(wrap(x + r), y, z)) for r in (1, 2, 3)]

    for c in ocopies:
        c.wait_recv()
    for n in range(2):
        attn_o[n] = (oin[n].astype(F32) + oin[n + 2].astype(F32)).astype(BF16)
    agcopies = over_x(attn_o, ag.at[:, x], ag_s, ag_r)
    for c in agcopies:
        c.start()
    ag[:, x] = attn_o[...]


    for c in c_win:
        c.wait()
    for c in wcopies:
        c.wait_recv()

    @pl.loop(0, 4)
    def _(xx):
        for n in range(2):
            for b in range(WIN // 128):
                cols = slice(b * 128, (b + 1) * 128)
                winT[n, cols, pl.ds(pl.multiple_of(xx * T, T), T)] = win[n, xx, :, cols].T

    @pl.when(x >= 1)
    def _():
        facc[...] = dkv[4].astype(F32)
        for r in (1, 2, 3):
            recv_back(r - 1)
            facc[...] += rbuf[r - 1].astype(F32)
        csend[1] = facc[...].astype(BF16)
        for c in chain4:
            c.start()

    off = pl.multiple_of(64 * lax.rem(x, 2), 16)

    def over_y(src, buf, s, r_):
        copies = []
        for r in (1, 2, 3):
            yt = wrap(y + r)
            rows = pl.ds(pl.multiple_of(off + 144 * yt, 16), 144)
            copies.append(remote(src.at[rows, :], buf.at[r - 1], s.at[r - 1], r_.at[r - 1], dev(x, yt, z)))
        return copies

    facc[...] = dkv[0].astype(F32)
    for r in (1, 2, 3):
        @pl.when(y + r < 4)
        def _():
            recv_back(3 + r - 1)
            facc[...] += rbuf[3 + r - 1].astype(F32)

    finkv[...] = facc[:, pl.ds(prow, T), :].astype(BF16)
    swap = [remote(finkv, pin, f_s, f_r, dev(x, y, zp))]
    swap[0].start()

    for c in dqcopies:
        c.wait_recv()
    for n in range(2):
        gq_o[n] = (dqin[n].astype(F32) + dqin[n + 2].astype(F32)).astype(BF16)
    for c in c_w:
        c.wait()

    def wrows(hh):
        return pl.ds(pl.multiple_of(COLS * hh, 16), COLS)

    @pl.loop(0, 4)
    def _(hh):
        tq[hh] = sum(
            lax.dot_general(wq[wrows(hh), n * 256 : (n + 1) * 256], gq_o[n], NT, preferred_element_type=F32)
            for n in range(2)
        )

    for c in agcopies:
        c.wait_recv()
    for n in range(2):
        po[:, n * 256 : (n + 1) * 256] = dot(winT[1], ag[n].reshape(4 * T, 256)).astype(BF16)
    yocopies = over_y(po, yo, yo_s, yo_r)
    for c in yocopies:
        c.start()

    swap[0].wait_recv()
    ggcopies = over_x(gv_o, gvg.at[:, x], gg_s, gg_r)
    for m, chain in enumerate((chain8, chain4)):
        @pl.when(x < 2 + m)
        def _():
            for c in chain:
                c.wait_recv()

    for n, out in ((1, gv_o), (0, gk_o)):
        parts = [facc[n, pl.ds(erow, T), :], pin[n].astype(F32)]
        for m in (0, 1):
            parts = [a + jnp.where(x < 2 + m, cin[m, part, n].astype(F32), 0.0) for part, a in enumerate(parts)]
        out[e] = parts[0].astype(BF16)
        out[1 - e] = parts[1].astype(BF16)
        if n == 1:
            for c in ggcopies:
                c.start()
    gvg[:, x] = gv_o[...]

    def terms(hh):
        acc = tq[hh]
        for n in range(2):
            acc = acc + lax.dot_general(wk[wrows(hh), n * D : (n + 1) * D], gk_o[n], NT, preferred_element_type=F32)
            acc = acc + lax.dot_general(wv[wrows(hh), n * D : (n + 1) * D], gv_o[n], NT, preferred_element_type=F32)
        return acc

    hzc = lax.rem(hc + 2, 4)
    tb[0] = terms(hzc).astype(BF16)
    far = remote(tb.at[0], hin.at[0], h_s.at[0], h_r.at[0], (i, hc))
    far.start()
    mine_far = terms(hz)
    far.wait_recv()
    tb[1] = (mine_far + hin[0].astype(F32)).astype(BF16)
    across = remote(tb.at[1], hin.at[1], h_s.at[1], h_r.at[1], (i, hz))
    across.start()
    for c in ggcopies:
        c.wait_recv()
    for n in range(2):
        pv[:, n * D : (n + 1) * D] = dot(winT[0], gvg[n].reshape(4 * T, D)).astype(BF16)
    yvcopies = over_y(pv, yv, yv_s, yv_r)
    for c in yvcopies:
        c.start()

    tb[2] = terms(hc).astype(BF16)
    near = remote(tb.at[2], hin.at[2], h_s.at[2], h_r.at[2], (i, hc))
    near.start()

    def over_z(copies, own, buf, total_s, piece_s, in_s, s, r_):
        for c in copies:
            c.wait_recv()
        acc = own[pl.ds(pl.multiple_of(off + 144 * y, 16), 144), :].astype(F32)
        for r in range(3):
            acc = acc + buf[r].astype(F32)
        total_s[...] = acc
        for zz in range(4):
            piece_s[zz] = total_s[36 * zz : 36 * (zz + 1), :].astype(piece_s.dtype)
        out = []
        for r in (1, 2, 3):
            zt = wrap(z + r)
            out.append(remote(piece_s.at[zt], in_s.at[r - 1], s.at[r - 1], r_.at[r - 1], dev(x, y, zt)))
        for c in out:
            c.start()
        return out

    zocopies = over_z(yocopies, po, yo, zso, zpo, zio, zo_s, zo_r)
    mine_near = terms(h)
    zvcopies = over_z(yvcopies, pv, yv, zsv, zpv, ziv, zv_s, zv_r)

    for c in zocopies:
        c.wait_recv()
    acc = zpo[z].astype(F32)
    for r in range(3):
        acc = acc + zio[r].astype(F32)
    gwo_o[...] = acc
    near.wait_recv()
    across.wait_recv()
    gi_o[...] = (mine_near + hin[2].astype(F32) + hin[1].astype(F32)).astype(BF16)
    for c in zvcopies:
        c.wait_recv()
    acc = zpv[z].astype(F32)
    for r in range(3):
        acc = acc + ziv[r].astype(F32)
    gwv_o[...] = acc

    for c in (
        pair + qcopies + docopies + ocopies + dqcopies + swap + wcopies + agcopies + ggcopies
        + yocopies + yvcopies + zocopies + zvcopies + [far, across, near]
    ):
        c.wait_send()

    @pl.when(x < 3)
    def _():
        for c in first:
            c.wait_send()

    @pl.when((x >= 1) & (x < 3))
    def _():
        fwd_x(4, 8).wait_send()

    for r in (1, 2, 3):
        @pl.when((y + r < 4) | (x >= 2))
        def _():
            fwd_y(r, 1).wait_send()

        @pl.when(x >= 1)
        def _():
            fwd_y(r, 0).wait_send()
            back_y(0, r).wait_send()

        @pl.when((r <= y) | (x >= 2))
        def _():
            back_y(1, r).wait_send()

    @pl.when(x >= 2)
    def _():
        for c in chain8:
            c.wait_send()

    @pl.when(x >= 1)
    def _():
        for c in chain4:
            c.wait_send()


def layer(xn, q, k, v, wq, wk, wv, wo, cot):
    dma = pltpu.SemaphoreType.DMA
    vm = pltpu.VMEM
    return pl.pallas_call(
        layer_kernel,
        out_shape=(
            jax.ShapeDtypeStruct((COLS, T), BF16),
            jax.ShapeDtypeStruct((36, 256), F32),
            jax.ShapeDtypeStruct((36, 512), F32),
        ),
        in_specs=[pl.BlockSpec(memory_space=pl.ANY)] * 9,
        out_specs=tuple(pl.BlockSpec(memory_space=pltpu.VMEM) for _ in range(3)),
        scratch_shapes=[
            vm((2, T, 256), BF16),
            vm((2, T, 256), BF16),
            vm((2, T, D), BF16),
            vm((2, T, D), BF16),
            vm(wq.shape, BF16),
            vm(wk.shape, BF16),
            vm(wv.shape, BF16),
            vm((2, 4, T, WIN), BF16),
            vm((2, WIN, 4 * T), BF16),
            vm((2, 4, T, 256), BF16),
            vm((2, 4, T, D), BF16),
            vm((WIN, 512), BF16),
            vm((WIN, 256), BF16),
            vm((3, 144, 512), BF16),
            vm((3, 144, 256), BF16),
            vm((144, 512), F32),
            vm((144, 256), F32),
            vm((4, 36, 512), BF16),
            vm((4, 36, 256), BF16),
            vm((3, 36, 512), BF16),
            vm((3, 36, 256), BF16),
            vm((3, COLS, T), BF16),
            vm((3, COLS, T), BF16),
            vm((4, COLS, T), F32),
            vm((2, KEYS, D), F32),
            vm((SLOTS, 2, KEYS, D), BF16),
            vm((4, T, 256), BF16),
            vm((4, T, 256), BF16),
            vm((2, T, 256), BF16),
            vm(cot.shape, BF16),
            vm(wo.shape, BF16),
            vm((ROWS, D), BF16),
            vm((ROWS, D), BF16),
            vm((D, ROWS), BF16),
            vm((D, ROWS), BF16),
            vm((SLOTS, KEYS, ROWS), F32),
            vm((SLOTS, KEYS, ROWS), F32),
            vm((KEYS, ROWS), BF16),
            vm((KEYS, ROWS), BF16),
            vm((SLOTS, 8, ROWS), F32),
            vm((8, ROWS), F32),
            vm((8, ROWS), F32),
            vm((8, ROWS), F32),
            vm((D, ROWS), F32),
            vm((D, ROWS), F32),
            vm((4, T, 256), BF16),
            vm((4, T, 256), BF16),
            vm((4, T, 256), BF16),
            vm((4, T, 256), BF16),
            vm((SLOTS, 2, KEYS, D), BF16),
            vm((6, 2, KEYS, D), BF16),
            vm((2, 2, KEYS, D), BF16),
            vm((2, 2, 2, T, D), BF16),
            vm((2, T, D), BF16),
            vm((2, T, D), BF16),
            dma((10,)), dma((2,)), dma((2,)), dma((3,)), dma((3,)), dma((3,)), dma((3,)),
            dma((2,)), dma((6,)), dma((SLOTS,)), dma, dma, dma((3,)), dma((3,)), dma((3,)), dma((3,)),
            dma((6,)), dma((6,)), dma((2, 2)), dma((2, 2)), dma, dma,
            dma((4,)), dma((4,)), dma((2, 3)), dma((2, 3)), *([dma((3,))] * 2), *([dma((3,))] * 2), *([dma((3,))] * 10),
        ],
        compiler_params=pltpu.CompilerParams(
            collective_id=1, has_side_effects=True, vmem_limit_bytes=62 * 1024 * 1024
        ),
        name="layer",
    )(xn, q, k, v, wq, wk, wv, wo, cot)


def hand_over(*refs):
    for n in range(3):
        refs[3 + n][...] = refs[n][...]


def local(*args):
    results = layer(*args)
    vmem = tuple(pl.BlockSpec(memory_space=pltpu.VMEM) for _ in range(3))
    grad_input, grad_wvalue, grad_woutput = pl.pallas_call(
        hand_over,
        out_shape=tuple(jax.ShapeDtypeStruct(a.shape, a.dtype) for a in results),
        in_specs=vmem,
        out_specs=vmem,
        name="hand_over",
    )(*results)
    return grad_input.T, grad_wvalue, grad_woutput.T


def solution(mesh):
    seq, both, cols, rows = P("seq", None), P("seq", "head"), P(None, "head"), P("head", None)
    return jax.shard_map(
        local,
        mesh=mesh,
        in_specs=(seq, both, both, both, cols, cols, cols, rows, seq),
        out_specs=(both, both, P("head", "seq")),
        check_vma=False,
    )
```

```python
import functools
import math

import jax
import jax.numpy as jnp
from jax import lax
from jax.experimental import pallas as pl
from jax.experimental.pallas import tpu as pltpu
from jax.sharding import PartitionSpec as P

MESH = pl.DeviceIdType.MESH
F32 = jnp.float32
BF16 = jnp.bfloat16
LOGIT_SCALE = 1.0 / 12.0
EXP2_SCALE = LOGIT_SCALE * math.log2(math.e)
NEG = -1e30
T = 128
D = 128
SLOTS = 9
ROWS = 1024
WIN = 640
COLS = 576
KEYS = 256
NT = (((1,), (1,)), ((), ()))


def dot(a, b):
    return jnp.dot(a, b, preferred_element_type=F32)


def place():
    i = lax.axis_index("seq")
    h = lax.axis_index("head")
    x = lax.div(i, 16)
    y = lax.rem(lax.div(i, 4), 4)
    z = lax.rem(i, 4)
    return i, h, x, y, z


def layer_kernel(
    x_hbm, q_hbm, k_hbm, v_hbm, wq_hbm, wk_hbm, wv_hbm, wo_hbm, cot_hbm,
    gi_o, gwv_o, gwo_o,
    attn_o, gq_o, gk_o, gv_o, wq, wk, wv, win, winT, ag, gvg, po, pv, yo, yv, zso, zsv, zpo, zpv, zio, ziv, tb, hin,
    tq, facc, kv, qg, dog, og, cot, wo, q2, do2, qT, doT, sbuf, dpbuf, pb_s, ds_s, ms, st, st_in, fin,
    oT, dqT, osend, oin, dqsend, dqin, dkv, rbuf, csend, cin, finkv, pin,
    lsem, pair_s, pair_r, q_s, q_r, do_s, do_r, kvx_s, kvy_s, kv_r, st_s, st_r, o_s, o_r, dq_s, dq_r,
    rb_s, rb_r, c_s, c_r, f_s, f_r,
    fx_s, fx_r, w_s, w_r, ag_s, ag_r, gg_s, gg_r, yo_s, yo_r, yv_s, yv_r, zo_s, zo_r, zv_s, zv_r, h_s, h_r,
):
    i, h, x, y, z = place()
    e, f = lax.rem(z, 2), lax.div(z, 2)
    S = x * 4 + y

    def dev(x_, y_, z_):
        return (x_ * 16 + y_ * 4 + z_, h)

    def wrap(a):
        return lax.rem(a + 4, 4)

    def remote(src, dst, s, r, to):
        return pltpu.make_async_remote_copy(
            src_ref=src, dst_ref=dst, send_sem=s, recv_sem=r, device_id=to, device_id_type=MESH
        )

    erow = pl.multiple_of(e * T, T)
    prow = pl.multiple_of((1 - e) * T, T)
    ecol2 = pl.multiple_of(e * 256, 256)
    c_wo = pltpu.make_async_copy(wo_hbm, wo, lsem.at[0])
    c_cot = pltpu.make_async_copy(cot_hbm, cot, lsem.at[1])
    c_k = pltpu.make_async_copy(k_hbm.at[:, pl.ds(erow, D)], kv.at[0, 0, pl.ds(erow, T), :], lsem.at[2])
    c_v = pltpu.make_async_copy(v_hbm.at[:, pl.ds(erow, D)], kv.at[0, 1, pl.ds(erow, T), :], lsem.at[3])
    c_q = pltpu.make_async_copy(q_hbm.at[:, pl.ds(ecol2, 256)], qg.at[z], lsem.at[4])
    for c in (c_wo, c_cot, c_k, c_v, c_q):
        c.start()

    def window(xt):
        return pl.ds(pl.multiple_of(lax.div(9 * xt, 2) * 128, 128), WIN)

    c_win = [
        pltpu.make_async_copy(src.at[:, window(x)], win.at[n, x], lsem.at[5 + n]) for n, src in ((0, x_hbm), (1, cot_hbm))
    ]
    c_w = [pltpu.make_async_copy(src, dst, lsem.at[7 + n]) for n, (src, dst) in enumerate(((wq_hbm, wq), (wk_hbm, wk), (wv_hbm, wv)))]

    bar = pltpu.get_barrier_semaphore()
    for r in (1, 2, 3):
        for to in (dev(x, y, wrap(z + r)), dev(x, wrap(y + r), z), dev(wrap(x + r), y, z)):
            pl.semaphore_signal(bar, inc=1, device_id=to, device_id_type=MESH)
    hc = h + 1 - 2 * lax.rem(h, 2)
    hz = lax.rem(h + 2, 4)
    for to in ((i, hc), (i, hz)):
        pl.semaphore_signal(bar, inc=1, device_id=to, device_id_type=MESH)
    zp = z + 1 - 2 * e
    for r in (1, 2, 3):
        pl.semaphore_signal(bar, inc=1, device_id=dev(wrap(x + r), y, zp), device_id_type=MESH)
    pl.semaphore_wait(bar, 14)

    pair = [
        remote(src.at[:, pl.ds(prow, D)], kv.at[0, n, pl.ds(erow, T), :], pair_s.at[n], pair_r.at[n], dev(x, y, zp))
        for n, src in ((0, k_hbm), (1, v_hbm))
    ]
    for c in pair:
        c.start()

    first = [
        remote(src.at[:, pl.ds(col, D)], kv.at[4, n, pl.ds(erow, T), :], fx_s.at[m + n], fx_r.at[m + n], dev(wrap(x + 1), y, zt))
        for m, col, zt in ((0, erow, z), (2, prow, zp))
        for n, src in ((0, k_hbm), (1, v_hbm))
    ]

    @pl.when(x < 3)
    def _():
        for c in first:
            c.start()

    def gathered(src_of, buf, s, r_):
        copies = []
        for r in (1, 2, 3):
            zt = wrap(z + r)
            copies.append(remote(src_of(zt), buf.at[z], s.at[r - 1], r_.at[r - 1], dev(x, y, zt)))
        return copies

    qcopies = gathered(
        lambda zt: q_hbm.at[:, pl.ds(pl.multiple_of(lax.rem(zt, 2) * 256, 256), 256)], qg, q_s, q_r
    )
    for c in qcopies:
        c.start()

    c_wo.wait()
    c_cot.wait()
    grad = lax.dot_general(cot[...], wo[...], NT, preferred_element_type=F32).astype(BF16)
    og[0] = grad[:, :256]
    og[1] = grad[:, 256:]
    docopies = gathered(lambda zt: og.at[lax.rem(zt, 2)], dog, do_s, do_r)
    for c in docopies:
        c.start()
    dog[z] = og[e]

    c_k.wait()
    c_v.wait()
    for c in pair:
        c.wait_recv()

    def fwd_x(src, dst):
        return remote(kv.at[src], kv.at[dst], kvx_s.at[dst // 8], kv_r.at[dst], dev(wrap(x + 1), y, z))

    def fwd_y(r, kind):
        yt = wrap(y + r)
        up = yt > y
        if kind == 0:
            src, dst = 4, 4 + yt - y
        else:
            src, dst = jnp.where(up, 0, 8), jnp.where(up, yt - y, 8 + yt - y)
        return remote(kv.at[src], kv.at[dst], kvy_s.at[kind * 3 + r - 1], kv_r.at[dst], dev(x, yt, z))

    for r in (1, 2, 3):
        @pl.when(y + r < 4)
        def _():
            fwd_y(r, 1).start()

    def recv_slot(d):
        remote(kv.at[d], kv.at[d], kvx_s.at[0], kv_r.at[d], dev(wrap(x + 1), y, z)).wait_recv()

    @pl.when(x >= 1)
    def _():
        for c in first:
            c.wait_recv()
        for r in (1, 2, 3):
            fwd_y(r, 0).start()

    @pl.when((x >= 1) & (x < 3))
    def _():
        fwd_x(4, 8).start()

    wcopies = []
    for r in (1, 2, 3):
        xt = wrap(x + r)
        for n, src in ((0, x_hbm), (1, cot_hbm)):
            wcopies.append(
                remote(src.at[:, window(xt)], win.at[n, x], w_s.at[n, r - 1], w_r.at[n, r - 1], dev(xt, y, z))
            )

    c_q.wait()
    @pl.when(x >= 2)
    def _():
        recv_slot(8)
        for r in (1, 2, 3):
            @pl.when(y + r >= 4)
            def _():
                fwd_y(r, 1).start()

    for c in qcopies:
        c.wait_recv()

    @pl.loop(0, 4)
    def _(zz):
        for j in range(2):
            rows = pl.ds(pl.multiple_of(j * 512 + zz * T, T), T)
            qb = qg[zz, :, j * D : (j + 1) * D]
            q2[rows, :] = qb
            qT[:, rows] = qb.T

    st[...] = jnp.concatenate([jnp.full((1, ROWS), NEG, F32), jnp.zeros((7, ROWS), F32)], axis=0)
    oT[...] = jnp.zeros_like(oT)
    dqT[...] = jnp.zeros_like(dqT)

    def slot_of(kind, r):
        if kind == 0:
            return 4 + jnp.where(r <= y, r, r - 4)
        return jnp.where(r <= y, r, r + 4)

    quarters = [slice(c * 256, (c + 1) * 256) for c in range(4)]

    def scores(d, edge):
        kd = kv[d, 0]
        low = jnp.where(d == 0, 0, -100000)
        high = jnp.where(d == 8, 0, 100000)
        for c, cs in enumerate(quarters):
            s = dot(kd, qT[:, cs])
            if edge:
                gap = (
                    lax.broadcasted_iota(jnp.int32, (KEYS, 256), 1)
                    - lax.broadcasted_iota(jnp.int32, (KEYS, 256), 0)
                    + ((c % 2) * 256 - f * 256)
                )
                s = jnp.where((gap >= low) & (gap < high), s, NEG)
            sbuf[d, :, cs] = s
            ms[d, 0:1, cs] = jnp.max(s, axis=0, keepdims=True)

    def probabilities(d):
        vd = kv[d, 1]
        vt = vd.T
        for cs in quarters:
            dpbuf[d, :, cs] = dot(vd, doT[:, cs])
        for cs in quarters:
            before = st[0:1, cs]
            top = jnp.maximum(before, ms[d, 0:1, cs])
            p = jnp.exp2((sbuf[d, :, cs] - top) * EXP2_SCALE)
            keep = jnp.exp2((before - top) * EXP2_SCALE)
            st[0:1, cs] = top
            st[1:2, cs] = st[1:2, cs] * keep + jnp.sum(p, axis=0, keepdims=True)
            st[2:3, cs] = st[2:3, cs] * keep + jnp.sum(p * dpbuf[d, :, cs], axis=0, keepdims=True)
            ms[d, 0:1, cs] = top
            sbuf[d, :, cs] = p
            pb_s[:, cs] = p.astype(BF16)
            oT[:, cs] = oT[:, cs] * keep + dot(vt, pb_s[:, cs])

    def order(t):
        kind = (t >= 5) & (t < 8)
        r = jnp.where(t < 4, t, jnp.where(t < 8, t - 4, t - 8))
        d = jnp.where(r == 0, t, jnp.where(kind, slot_of(0, r), slot_of(1, r)))
        fits = (S >= d) & ((r == 0) | kind | jnp.where(t < 4, r <= y, r > y))
        return d, r, fits

    def score_step(t):
        d, r, fits = order(t)

        @pl.when(fits & ((t == 0) | (t == 8)))
        def _():
            scores(d, True)

        @pl.when(fits & (t != 0) & (t != 8))
        def _():
            @pl.when(r > 0)
            def _():
                recv_slot(d)

            scores(d, False)

    def prob_step(t):
        d, r, fits = order(t)

        @pl.when(fits)
        def _():
            probabilities(d)

    pl.loop(0, 5)(score_step)

    for c in docopies:
        c.wait_recv()
    for c in wcopies + c_win + c_w:
        c.start()

    @pl.loop(0, 4)
    def _(zz):
        for j in range(2):
            rows = pl.ds(pl.multiple_of(j * 512 + zz * T, T), T)
            db = dog[zz, :, j * D : (j + 1) * D]
            do2[rows, :] = db
            doT[:, rows] = db.T

    pl.loop(0, 5)(prob_step)

    @pl.loop(5, 12)
    def _(t):
        score_step(t)
        prob_step(t)

    stat = remote(st, st_in, st_s, st_r, dev(x, y, wrap(z + 2)))
    stat.start()
    stat.wait()
    top = jnp.maximum(st[0:1, :], st_in[0:1, :])
    mine = jnp.exp2((st[0:1, :] - top) * EXP2_SCALE)
    other = jnp.exp2((st_in[0:1, :] - top) * EXP2_SCALE)
    inv = 1.0 / (st[1:2, :] * mine + st_in[1:2, :] * other)
    fin[0:1, :] = top
    fin[1:2, :] = inv
    fin[2:3, :] = (st[2:3, :] * mine + st_in[2:3, :] * other) * inv
    oT[...] = oT[...] * (mine * inv)

    def spread(srcT, factor, sendbuf, inbuf, s, r_):
        for j in range(2):
            for zz in range(4):
                piece = srcT[:, j * 512 + zz * T : j * 512 + (zz + 1) * T]
                sendbuf[zz, :, j * D : (j + 1) * D] = (piece * factor).T.astype(BF16)
        copies = []
        for r in (1, 2, 3):
            zt = wrap(z + r)
            copies.append(remote(sendbuf.at[zt], inbuf.at[z], s.at[r - 1], r_.at[r - 1], dev(x, y, zt)))
        for c in copies:
            c.start()
        inbuf[z] = sendbuf[z]
        return copies

    ocopies = spread(oT, 1.0, osend, oin, o_s, o_r)

    def grad_slot(d):
        w = jnp.exp2((ms[d, 0:1, :] - fin[0:1, :]) * EXP2_SCALE) * fin[1:2, :]
        kt = kv[d, 0].T
        for c in range(4):
            cs = slice(c * 256, (c + 1) * 256)
            p = sbuf[d, :, cs] * w[:, cs]
            pb_s[:, cs] = p.astype(BF16)
            ds = (p * (dpbuf[d, :, cs] - fin[2:3, cs])).astype(BF16)
            ds_s[:, cs] = ds
            dqT[:, cs] += dot(kt, ds)
        dkv[d, 0] = (LOGIT_SCALE * dot(ds_s[...], q2[...])).astype(BF16)
        dkv[d, 1] = dot(pb_s[...], do2[...]).astype(BF16)

    def back_y(kind, r):
        d = slot_of(kind, r)
        n = kind * 3 + r - 1
        return remote(dkv.at[d], rbuf.at[n], rb_s.at[n], rb_r.at[n], dev(x, wrap(y - r), z))

    def grad_step(t):
        kind = (t >= 4) & (t < 7)
        r = jnp.where(t < 3, t + 1, jnp.where(kind, t - 3, jnp.where((t >= 8) & (t < 11), t - 7, 0)))
        d = jnp.where(r == 0, jnp.where(t == 3, 8, jnp.where(t == 7, 4, 0)), jnp.where(kind, slot_of(0, r), slot_of(1, r)))
        fits = (r == 0) | kind | jnp.where(t < 3, r > y, r <= y)

        @pl.when((S >= d) & fits)
        def _():
            grad_slot(d)

            @pl.when(r > 0)
            def _():
                n = jnp.where(kind, r - 1, r + 2)
                remote(dkv.at[d], rbuf.at[n], rb_s.at[n], rb_r.at[n], dev(x, wrap(y - r), z)).start()

    pl.loop(0, 12)(grad_step)

    dqcopies = spread(dqT, LOGIT_SCALE, dqsend, dqin, dq_s, dq_r)

    def over_x(src, dst, s, r_):
        return [remote(src, dst, s.at[r - 1], r_.at[r - 1], dev(wrap(x + r), y, z)) for r in (1, 2, 3)]

    for c in ocopies:
        c.wait_recv()
    for n in range(2):
        attn_o[n] = (oin[n].astype(F32) + oin[n + 2].astype(F32)).astype(BF16)
    agcopies = over_x(attn_o, ag.at[:, x], ag_s, ag_r)
    for c in agcopies:
        c.start()
    ag[:, x] = attn_o[...]


    def recv_back(n):
        remote(rbuf.at[n], rbuf.at[n], rb_s.at[n], rb_r.at[n], dev(x, wrap(y + 1), z)).wait_recv()

    chain8, chain4 = (
        [
            remote(
                csend.at[m, :, pl.ds(row, T), :], cin.at[m, part], c_s.at[m, part], c_r.at[m, part], dev(wrap(x - 2 + m), y, zt)
            )
            for part, row, zt in ((0, erow, z), (1, prow, zp))
        ]
        for m in range(2)
    )

    @pl.when(x >= 2)
    def _():
        facc[...] = dkv[8].astype(F32)
        for r in (1, 2, 3):
            @pl.when(y + r >= 4)
            def _():
                recv_back(3 + r - 1)
                facc[...] += rbuf[3 + r - 1].astype(F32)

        csend[0] = facc[...].astype(BF16)
        for c in chain8:
            c.start()

    for c in c_win:
        c.wait()
    for c in wcopies:
        c.wait_recv()

    @pl.loop(0, 4)
    def _(xx):
        for n in range(2):
            for b in range(WIN // 128):
                cols = slice(b * 128, (b + 1) * 128)
                winT[n, cols, pl.ds(pl.multiple_of(xx * T, T), T)] = win[n, xx, :, cols].T

    @pl.when(x >= 1)
    def _():
        facc[...] = dkv[4].astype(F32)
        for r in (1, 2, 3):
            recv_back(r - 1)
            facc[...] += rbuf[r - 1].astype(F32)
        csend[1] = facc[...].astype(BF16)
        for c in chain4:
            c.start()

    off = pl.multiple_of(64 * lax.rem(x, 2), 16)

    def over_y(src, buf, s, r_):
        copies = []
        for r in (1, 2, 3):
            yt = wrap(y + r)
            rows = pl.ds(pl.multiple_of(off + 144 * yt, 16), 144)
            copies.append(remote(src.at[rows, :], buf.at[r - 1], s.at[r - 1], r_.at[r - 1], dev(x, yt, z)))
        return copies

    facc[...] = dkv[0].astype(F32)
    for r in (1, 2, 3):
        @pl.when(y + r < 4)
        def _():
            recv_back(3 + r - 1)
            facc[...] += rbuf[3 + r - 1].astype(F32)

    finkv[...] = facc[:, pl.ds(prow, T), :].astype(BF16)
    swap = [remote(finkv, pin, f_s, f_r, dev(x, y, zp))]
    swap[0].start()

    for c in dqcopies:
        c.wait_recv()
    for n in range(2):
        gq_o[n] = (dqin[n].astype(F32) + dqin[n + 2].astype(F32)).astype(BF16)
    for c in c_w:
        c.wait()

    def wrows(hh):
        return pl.ds(pl.multiple_of(COLS * hh, 16), COLS)

    @pl.loop(0, 4)
    def _(hh):
        tq[hh] = sum(
            lax.dot_general(wq[wrows(hh), n * 256 : (n + 1) * 256], gq_o[n], NT, preferred_element_type=F32)
            for n in range(2)
        )

    for c in agcopies:
        c.wait_recv()
    for n in range(2):
        po[:, n * 256 : (n + 1) * 256] = dot(winT[1], ag[n].reshape(4 * T, 256)).astype(BF16)
    yocopies = over_y(po, yo, yo_s, yo_r)
    for c in yocopies:
        c.start()

    swap[0].wait_recv()
    ggcopies = over_x(gv_o, gvg.at[:, x], gg_s, gg_r)
    for m, chain in enumerate((chain8, chain4)):
        @pl.when(x < 2 + m)
        def _():
            for c in chain:
                c.wait_recv()

    for n, out in ((1, gv_o), (0, gk_o)):
        parts = [facc[n, pl.ds(erow, T), :], pin[n].astype(F32)]
        for m in (0, 1):
            parts = [a + jnp.where(x < 2 + m, cin[m, part, n].astype(F32), 0.0) for part, a in enumerate(parts)]
        out[e] = parts[0].astype(BF16)
        out[1 - e] = parts[1].astype(BF16)
        if n == 1:
            for c in ggcopies:
                c.start()
    gvg[:, x] = gv_o[...]

    def terms(hh):
        acc = tq[hh]
        for n in range(2):
            acc = acc + lax.dot_general(wk[wrows(hh), n * D : (n + 1) * D], gk_o[n], NT, preferred_element_type=F32)
            acc = acc + lax.dot_general(wv[wrows(hh), n * D : (n + 1) * D], gv_o[n], NT, preferred_element_type=F32)
        return acc

    hzc = lax.rem(hc + 2, 4)
    tb[0] = terms(hzc).astype(BF16)
    far = remote(tb.at[0], hin.at[0], h_s.at[0], h_r.at[0], (i, hc))
    far.start()
    mine_far = terms(hz)
    far.wait_recv()
    tb[1] = (mine_far + hin[0].astype(F32)).astype(BF16)
    across = remote(tb.at[1], hin.at[1], h_s.at[1], h_r.at[1], (i, hz))
    across.start()
    for c in ggcopies:
        c.wait_recv()
    for n in range(2):
        pv[:, n * D : (n + 1) * D] = dot(winT[0], gvg[n].reshape(4 * T, D)).astype(BF16)
    yvcopies = over_y(pv, yv, yv_s, yv_r)
    for c in yvcopies:
        c.start()

    tb[2] = terms(hc).astype(BF16)
    near = remote(tb.at[2], hin.at[2], h_s.at[2], h_r.at[2], (i, hc))
    near.start()

    def over_z(copies, own, buf, total_s, piece_s, in_s, s, r_):
        for c in copies:
            c.wait_recv()
        acc = own[pl.ds(pl.multiple_of(off + 144 * y, 16), 144), :].astype(F32)
        for r in range(3):
            acc = acc + buf[r].astype(F32)
        total_s[...] = acc
        for zz in range(4):
            piece_s[zz] = total_s[36 * zz : 36 * (zz + 1), :].astype(piece_s.dtype)
        out = []
        for r in (1, 2, 3):
            zt = wrap(z + r)
            out.append(remote(piece_s.at[zt], in_s.at[r - 1], s.at[r - 1], r_.at[r - 1], dev(x, y, zt)))
        for c in out:
            c.start()
        return out

    zocopies = over_z(yocopies, po, yo, zso, zpo, zio, zo_s, zo_r)
    mine_near = terms(h)
    zvcopies = over_z(yvcopies, pv, yv, zsv, zpv, ziv, zv_s, zv_r)

    for c in zocopies:
        c.wait_recv()
    acc = zpo[z].astype(F32)
    for r in range(3):
        acc = acc + zio[r].astype(F32)
    gwo_o[...] = acc
    near.wait_recv()
    across.wait_recv()
    gi_o[...] = (mine_near + hin[2].astype(F32) + hin[1].astype(F32)).astype(BF16)
    for c in zvcopies:
        c.wait_recv()
    acc = zpv[z].astype(F32)
    for r in range(3):
        acc = acc + ziv[r].astype(F32)
    gwv_o[...] = acc

    for c in (
        pair + qcopies + docopies + ocopies + dqcopies + swap + wcopies + agcopies + ggcopies
        + yocopies + yvcopies + zocopies + zvcopies + [far, across, near]
    ):
        c.wait_send()

    @pl.when(x < 3)
    def _():
        for c in first:
            c.wait_send()

    @pl.when((x >= 1) & (x < 3))
    def _():
        fwd_x(4, 8).wait_send()

    for r in (1, 2, 3):
        @pl.when((y + r < 4) | (x >= 2))
        def _():
            fwd_y(r, 1).wait_send()

        @pl.when(x >= 1)
        def _():
            fwd_y(r, 0).wait_send()
            back_y(0, r).wait_send()

        @pl.when((r <= y) | (x >= 2))
        def _():
            back_y(1, r).wait_send()

    @pl.when(x >= 2)
    def _():
        for c in chain8:
            c.wait_send()

    @pl.when(x >= 1)
    def _():
        for c in chain4:
            c.wait_send()


def layer(xn, q, k, v, wq, wk, wv, wo, cot):
    dma = pltpu.SemaphoreType.DMA
    vm = pltpu.VMEM
    return pl.pallas_call(
        layer_kernel,
        out_shape=(
            jax.ShapeDtypeStruct((COLS, T), BF16),
            jax.ShapeDtypeStruct((36, 256), F32),
            jax.ShapeDtypeStruct((36, 512), F32),
        ),
        in_specs=[pl.BlockSpec(memory_space=pl.ANY)] * 9,
        out_specs=tuple(pl.BlockSpec(memory_space=pltpu.VMEM) for _ in range(3)),
        scratch_shapes=[
            vm((2, T, 256), BF16),
            vm((2, T, 256), BF16),
            vm((2, T, D), BF16),
            vm((2, T, D), BF16),
            vm(wq.shape, BF16),
            vm(wk.shape, BF16),
            vm(wv.shape, BF16),
            vm((2, 4, T, WIN), BF16),
            vm((2, WIN, 4 * T), BF16),
            vm((2, 4, T, 256), BF16),
            vm((2, 4, T, D), BF16),
            vm((WIN, 512), BF16),
            vm((WIN, 256), BF16),
            vm((3, 144, 512), BF16),
            vm((3, 144, 256), BF16),
            vm((144, 512), F32),
            vm((144, 256), F32),
            vm((4, 36, 512), BF16),
            vm((4, 36, 256), BF16),
            vm((3, 36, 512), BF16),
            vm((3, 36, 256), BF16),
            vm((3, COLS, T), BF16),
            vm((3, COLS, T), BF16),
            vm((4, COLS, T), F32),
            vm((2, KEYS, D), F32),
            vm((SLOTS, 2, KEYS, D), BF16),
            vm((4, T, 256), BF16),
            vm((4, T, 256), BF16),
            vm((2, T, 256), BF16),
            vm(cot.shape, BF16),
            vm(wo.shape, BF16),
            vm((ROWS, D), BF16),
            vm((ROWS, D), BF16),
            vm((D, ROWS), BF16),
            vm((D, ROWS), BF16),
            vm((SLOTS, KEYS, ROWS), F32),
            vm((SLOTS, KEYS, ROWS), F32),
            vm((KEYS, ROWS), BF16),
            vm((KEYS, ROWS), BF16),
            vm((SLOTS, 8, ROWS), F32),
            vm((8, ROWS), F32),
            vm((8, ROWS), F32),
            vm((8, ROWS), F32),
            vm((D, ROWS), F32),
            vm((D, ROWS), F32),
            vm((4, T, 256), BF16),
            vm((4, T, 256), BF16),
            vm((4, T, 256), BF16),
            vm((4, T, 256), BF16),
            vm((SLOTS, 2, KEYS, D), BF16),
            vm((6, 2, KEYS, D), BF16),
            vm((2, 2, KEYS, D), BF16),
            vm((2, 2, 2, T, D), BF16),
            vm((2, T, D), BF16),
            vm((2, T, D), BF16),
            dma((10,)), dma((2,)), dma((2,)), dma((3,)), dma((3,)), dma((3,)), dma((3,)),
            dma((2,)), dma((6,)), dma((SLOTS,)), dma, dma, dma((3,)), dma((3,)), dma((3,)), dma((3,)),
            dma((6,)), dma((6,)), dma((2, 2)), dma((2, 2)), dma, dma,
            dma((4,)), dma((4,)), dma((2, 3)), dma((2, 3)), *([dma((3,))] * 2), *([dma((3,))] * 2), *([dma((3,))] * 10),
        ],
        compiler_params=pltpu.CompilerParams(
            collective_id=1, has_side_effects=True, vmem_limit_bytes=62 * 1024 * 1024,
        ),
        name="layer",
    )(xn, q, k, v, wq, wk, wv, wo, cot)


def hand_over(*refs):
    for n in range(3):
        refs[3 + n][...] = refs[n][...]


def local(*args):
    results = layer(*args)
    vmem = tuple(pl.BlockSpec(memory_space=pltpu.VMEM) for _ in range(3))
    grad_input, grad_wvalue, grad_woutput = pl.pallas_call(
        hand_over,
        out_shape=tuple(jax.ShapeDtypeStruct(a.shape, a.dtype) for a in results),
        in_specs=vmem,
        out_specs=vmem,
        name="hand_over",
    )(*results)
    return grad_input.T, grad_wvalue, grad_woutput.T


def solution(mesh):
    seq, both, cols, rows = P("seq", None), P("seq", "head"), P(None, "head"), P("head", None)
    return jax.shard_map(
        local,
        mesh=mesh,
        in_specs=(seq, both, both, both, cols, cols, cols, rows, seq),
        out_specs=(both, both, P("head", "seq")),
        check_vma=False,
    )
```

```python
import functools
import math

import jax
import jax.numpy as jnp
from jax import lax
from jax.experimental import pallas as pl
from jax.experimental.pallas import tpu as pltpu
from jax.sharding import PartitionSpec as P

MESH = pl.DeviceIdType.MESH
F32 = jnp.float32
BF16 = jnp.bfloat16
LOGIT_SCALE = 1.0 / 12.0
EXP2_SCALE = LOGIT_SCALE * math.log2(math.e)
NEG = -1e30
T = 128
D = 128
SLOTS = 9
ROWS = 1024
WIN = 640
COLS = 576
KEYS = 256
NT = (((1,), (1,)), ((), ()))


def dot(a, b):
    return jnp.dot(a, b, preferred_element_type=F32)


def place():
    i = lax.axis_index("seq")
    h = lax.axis_index("head")
    x = lax.div(i, 16)
    y = lax.rem(lax.div(i, 4), 4)
    z = lax.rem(i, 4)
    return i, h, x, y, z


def layer_kernel(
    x_hbm, q_hbm, k_hbm, v_hbm, wq_hbm, wk_hbm, wv_hbm, wo_hbm, cot_hbm,
    gi_o, gwv_o, gwo_o,
    attn_o, gq_o, gk_o, gv_o, wq, wk, wv, win, winT, ag, gvg, po, pv, yo, yv, zso, zsv, zpo, zpv, zio, ziv, tb, hin,
    tq, facc, kv, qg, dog, og, cot, wo, q2, do2, qT, doT, sbuf, dpbuf, pb_s, ds_s, ms, st, st_in, fin,
    oT, dqT, osend, oin, dqsend, dqin, dkv, rbuf, csend, cin, finkv, pin,
    lsem, pair_s, pair_r, q_s, q_r, do_s, do_r, kvx_s, kvy_s, kv_r, st_s, st_r, o_s, o_r, dq_s, dq_r,
    rb_s, rb_r, c_s, c_r, f_s, f_r,
    xw_s, fx_s, fx_r, w_s, w_r, ag_s, ag_r, gg_s, gg_r, yo_s, yo_r, yv_s, yv_r, zo_s, zo_r, zv_s, zv_r, h_s, h_r,
):
    i, h, x, y, z = place()
    e, f = lax.rem(z, 2), lax.div(z, 2)
    S = x * 4 + y

    def dev(x_, y_, z_):
        return (x_ * 16 + y_ * 4 + z_, h)

    def wrap(a):
        return lax.rem(a + 4, 4)

    def remote(src, dst, s, r, to):
        return pltpu.make_async_remote_copy(
            src_ref=src, dst_ref=dst, send_sem=s, recv_sem=r, device_id=to, device_id_type=MESH
        )

    erow = pl.multiple_of(e * T, T)
    prow = pl.multiple_of((1 - e) * T, T)
    ecol2 = pl.multiple_of(e * 256, 256)
    c_wo = pltpu.make_async_copy(wo_hbm, wo, lsem.at[0])
    c_cot = pltpu.make_async_copy(cot_hbm, cot, lsem.at[1])
    c_k = pltpu.make_async_copy(k_hbm.at[:, pl.ds(erow, D)], kv.at[0, 0, pl.ds(erow, T), :], lsem.at[2])
    c_v = pltpu.make_async_copy(v_hbm.at[:, pl.ds(erow, D)], kv.at[0, 1, pl.ds(erow, T), :], lsem.at[3])
    c_q = pltpu.make_async_copy(q_hbm.at[:, pl.ds(ecol2, 256)], qg.at[z], lsem.at[4])
    for c in (c_wo, c_cot, c_k, c_v, c_q):
        c.start()

    def window(xt):
        return pl.ds(pl.multiple_of(lax.div(9 * xt, 2) * 128, 128), WIN)

    c_win = [
        pltpu.make_async_copy(src.at[:, window(x)], win.at[n, x], lsem.at[5 + n]) for n, src in ((0, x_hbm), (1, cot_hbm))
    ]
    c_w = [pltpu.make_async_copy(src, dst, lsem.at[7 + n]) for n, (src, dst) in enumerate(((wq_hbm, wq), (wk_hbm, wk), (wv_hbm, wv)))]

    bar = pltpu.get_barrier_semaphore()
    for r in (1, 2, 3):
        for to in (dev(x, y, wrap(z + r)), dev(x, wrap(y + r), z), dev(wrap(x + r), y, z)):
            pl.semaphore_signal(bar, inc=1, device_id=to, device_id_type=MESH)
    hc = h + 1 - 2 * lax.rem(h, 2)
    hz = lax.rem(h + 2, 4)
    for to in ((i, hc), (i, hz)):
        pl.semaphore_signal(bar, inc=1, device_id=to, device_id_type=MESH)
    zp = z + 1 - 2 * e
    for r in (1, 2, 3):
        pl.semaphore_signal(bar, inc=1, device_id=dev(wrap(x + r), y, zp), device_id_type=MESH)
    pl.semaphore_wait(bar, 14)

    pair = [
        remote(src.at[:, pl.ds(prow, D)], kv.at[0, n, pl.ds(erow, T), :], pair_s.at[n], pair_r.at[n], dev(x, y, zp))
        for n, src in ((0, k_hbm), (1, v_hbm))
    ]
    for c in pair:
        c.start()

    first = [
        remote(src.at[:, pl.ds(col, D)], kv.at[4, n, pl.ds(erow, T), :], fx_s.at[m + n], fx_r.at[m + n], dev(wrap(x + 1), y, zt))
        for m, col, zt in ((0, erow, z), (2, prow, zp))
        for n, src in ((0, k_hbm), (1, v_hbm))
    ]

    @pl.when(x < 3)
    def _():
        for c in first:
            c.start()

    def gathered(src_of, buf, s, r_):
        copies = []
        for r in (1, 2, 3):
            zt = wrap(z + r)
            copies.append(remote(src_of(zt), buf.at[z], s.at[r - 1], r_.at[r - 1], dev(x, y, zt)))
        return copies

    qcopies = gathered(
        lambda zt: q_hbm.at[:, pl.ds(pl.multiple_of(lax.rem(zt, 2) * 256, 256), 256)], qg, q_s, q_r
    )
    for c in qcopies:
        c.start()

    c_wo.wait()
    c_cot.wait()
    grad = lax.dot_general(cot[...], wo[...], NT, preferred_element_type=F32).astype(BF16)
    og[0] = grad[:, :256]
    og[1] = grad[:, 256:]
    docopies = gathered(lambda zt: og.at[lax.rem(zt, 2)], dog, do_s, do_r)
    for c in docopies:
        c.start()
    dog[z] = og[e]

    c_k.wait()
    c_v.wait()
    for c in pair:
        c.wait_recv()

    def fwd_x(src, dst):
        return remote(kv.at[src], kv.at[dst], kvx_s.at[dst // 8], kv_r.at[dst], dev(wrap(x + 1), y, z))

    def fwd_y(r, kind):
        yt = wrap(y + r)
        up = yt > y
        if kind == 0:
            src, dst = 4, 4 + yt - y
        else:
            src, dst = jnp.where(up, 0, 8), jnp.where(up, yt - y, 8 + yt - y)
        return remote(kv.at[src], kv.at[dst], kvy_s.at[kind * 3 + r - 1], kv_r.at[dst], dev(x, yt, z))

    for r in (1, 2, 3):
        @pl.when(y + r < 4)
        def _():
            fwd_y(r, 1).start()

    def recv_slot(d):
        remote(kv.at[d], kv.at[d], kvx_s.at[0], kv_r.at[d], dev(wrap(x + 1), y, z)).wait_recv()

    @pl.when(x >= 1)
    def _():
        for c in first:
            c.wait_recv()
        for r in (1, 2, 3):
            fwd_y(r, 0).start()

    @pl.when((x >= 1) & (x < 3))
    def _():
        fwd_x(4, 8).start()

    wcopies = []
    for r in (1, 2, 3):
        xt = wrap(x + r)
        for n, src in ((0, x_hbm), (1, cot_hbm)):
            wcopies.append(
                remote(src.at[:, window(xt)], win.at[n, x], w_s.at[n, r - 1], w_r.at[n, r - 1], dev(xt, y, z))
            )

    c_q.wait()
    @pl.when(x >= 2)
    def _():
        recv_slot(8)

        @pl.when(y >= 1)
        def _():
            fwd_y(3, 1).start()

    for c in qcopies:
        c.wait_recv()

    @pl.loop(0, 4)
    def _(zz):
        for j in range(2):
            rows = pl.ds(pl.multiple_of(j * 512 + zz * T, T), T)
            qb = qg[zz, :, j * D : (j + 1) * D]
            q2[rows, :] = qb
            qT[:, rows] = qb.T

    st[...] = jnp.concatenate([jnp.full((1, ROWS), NEG, F32), jnp.zeros((7, ROWS), F32)], axis=0)
    oT[...] = jnp.zeros_like(oT)
    dqT[...] = jnp.zeros_like(dqT)

    def slot_of(kind, r):
        if kind == 0:
            return 4 + jnp.where(r <= y, r, r - 4)
        return jnp.where(r <= y, r, r + 4)

    quarters = [slice(c * 256, (c + 1) * 256) for c in range(4)]

    def scores(d, edge):
        kd = kv[d, 0]
        low = jnp.where(d == 0, 0, -100000)
        high = jnp.where(d == 8, 0, 100000)
        for c, cs in enumerate(quarters):
            s = dot(kd, qT[:, cs])
            if edge:
                gap = (
                    lax.broadcasted_iota(jnp.int32, (KEYS, 256), 1)
                    - lax.broadcasted_iota(jnp.int32, (KEYS, 256), 0)
                    + ((c % 2) * 256 - f * 256)
                )
                s = jnp.where((gap >= low) & (gap < high), s, NEG)
            sbuf[d, :, cs] = s
            ms[d, 0:1, cs] = jnp.max(s, axis=0, keepdims=True)

    def probabilities(d):
        vd = kv[d, 1]
        vt = vd.T
        for cs in quarters:
            dpbuf[d, :, cs] = dot(vd, doT[:, cs])
        for cs in quarters:
            before = st[0:1, cs]
            top = jnp.maximum(before, ms[d, 0:1, cs])
            p = jnp.exp2((sbuf[d, :, cs] - top) * EXP2_SCALE)
            keep = jnp.exp2((before - top) * EXP2_SCALE)
            st[0:1, cs] = top
            st[1:2, cs] = st[1:2, cs] * keep + jnp.sum(p, axis=0, keepdims=True)
            st[2:3, cs] = st[2:3, cs] * keep + jnp.sum(p * dpbuf[d, :, cs], axis=0, keepdims=True)
            ms[d, 0:1, cs] = top
            sbuf[d, :, cs] = p
            pb_s[:, cs] = p.astype(BF16)
            oT[:, cs] = oT[:, cs] * keep + dot(vt, pb_s[:, cs])

    def order(t):
        kind = (t >= 5) & (t < 8)
        r = jnp.where(t < 4, t, jnp.where(t < 8, t - 4, t - 8))
        d = jnp.where(r == 0, t, jnp.where(kind, slot_of(0, r), slot_of(1, r)))
        fits = (S >= d) & ((r == 0) | kind | jnp.where(t < 4, r <= y, r > y))
        return d, r, fits

    def pass_on(r, d):
        return remote(kv.at[d], kv.at[r + 4], xw_s.at[r - 1], kv_r.at[r + 4], dev(wrap(x + 1), y, z))

    def score_step(t):
        d, r, fits = order(t)

        @pl.when(fits & ((t == 0) | (t == 8)))
        def _():
            scores(d, True)

        @pl.when(fits & (t != 0) & (t != 8))
        def _():
            @pl.when(r > 0)
            def _():
                recv_slot(d)

            @pl.when((t >= 5) & (t < 7) & (r > y) & (x < 3))
            def _():
                pass_on(r, d).start()

            scores(d, False)

    def prob_step(t):
        d, r, fits = order(t)

        @pl.when(fits)
        def _():
            probabilities(d)

    pl.loop(0, 8)(score_step)

    for c in docopies:
        c.wait_recv()
    for c in c_win + c_w:
        c.start()

    @pl.when(x >= 2)
    def _():
        for c in wcopies:
            c.start()


    @pl.loop(0, 4)
    def _(zz):
        for j in range(2):
            rows = pl.ds(pl.multiple_of(j * 512 + zz * T, T), T)
            db = dog[zz, :, j * D : (j + 1) * D]
            do2[rows, :] = db
            doT[:, rows] = db.T

    pl.loop(0, 8)(prob_step)

    @pl.loop(8, 12)
    def _(t):
        score_step(t)
        prob_step(t)

    stat = remote(st, st_in, st_s, st_r, dev(x, y, wrap(z + 2)))
    stat.start()
    stat.wait()

    @pl.when(x < 2)
    def _():
        for c in wcopies:
            c.start()

    top = jnp.maximum(st[0:1, :], st_in[0:1, :])
    mine = jnp.exp2((st[0:1, :] - top) * EXP2_SCALE)
    other = jnp.exp2((st_in[0:1, :] - top) * EXP2_SCALE)
    inv = 1.0 / (st[1:2, :] * mine + st_in[1:2, :] * other)
    fin[0:1, :] = top
    fin[1:2, :] = inv
    fin[2:3, :] = (st[2:3, :] * mine + st_in[2:3, :] * other) * inv
    oT[...] = oT[...] * (mine * inv)

    def spread(srcT, factor, sendbuf, inbuf, s, r_):
        for j in range(2):
            for zz in range(4):
                piece = srcT[:, j * 512 + zz * T : j * 512 + (zz + 1) * T]
                sendbuf[zz, :, j * D : (j + 1) * D] = (piece * factor).T.astype(BF16)
        copies = []
        for r in (1, 2, 3):
            zt = wrap(z + r)
            copies.append(remote(sendbuf.at[zt], inbuf.at[z], s.at[r - 1], r_.at[r - 1], dev(x, y, zt)))
        for c in copies:
            c.start()
        inbuf[z] = sendbuf[z]
        return copies

    ocopies = spread(oT, 1.0, osend, oin, o_s, o_r)

    def grad_slot(d):
        w = jnp.exp2((ms[d, 0:1, :] - fin[0:1, :]) * EXP2_SCALE) * fin[1:2, :]
        kt = kv[d, 0].T
        for c in range(4):
            cs = slice(c * 256, (c + 1) * 256)
            p = sbuf[d, :, cs] * w[:, cs]
            pb_s[:, cs] = p.astype(BF16)
            ds = (p * (dpbuf[d, :, cs] - fin[2:3, cs])).astype(BF16)
            ds_s[:, cs] = ds
            dqT[:, cs] += dot(kt, ds)
        dkv[d, 0] = (LOGIT_SCALE * dot(ds_s[...], q2[...])).astype(BF16)
        dkv[d, 1] = dot(pb_s[...], do2[...]).astype(BF16)

    def back_y(kind, r):
        d = slot_of(kind, r)
        n = kind * 3 + r - 1
        return remote(dkv.at[d], rbuf.at[n], rb_s.at[n], rb_r.at[n], dev(x, wrap(y - r), z))

    def grad_step(t):
        kind = (t >= 4) & (t < 7)
        r = jnp.where(t < 3, t + 1, jnp.where(kind, t - 3, jnp.where((t >= 8) & (t < 11), t - 7, 0)))
        d = jnp.where(r == 0, jnp.where(t == 3, 8, jnp.where(t == 7, 4, 0)), jnp.where(kind, slot_of(0, r), slot_of(1, r)))
        fits = (r == 0) | kind | jnp.where(t < 3, r > y, r <= y)

        @pl.when((S >= d) & fits)
        def _():
            grad_slot(d)

            @pl.when(r > 0)
            def _():
                n = jnp.where(kind, r - 1, r + 2)
                remote(dkv.at[d], rbuf.at[n], rb_s.at[n], rb_r.at[n], dev(x, wrap(y - r), z)).start()

    pl.loop(0, 12)(grad_step)

    dqcopies = spread(dqT, LOGIT_SCALE, dqsend, dqin, dq_s, dq_r)

    def over_x(src, dst, s, r_):
        return [remote(src, dst, s.at[r - 1], r_.at[r - 1], dev(wrap(x + r), y, z)) for r in (1, 2, 3)]

    for c in ocopies:
        c.wait_recv()
    for n in range(2):
        attn_o[n] = (oin[n].astype(F32) + oin[n + 2].astype(F32)).astype(BF16)
    agcopies = over_x(attn_o, ag.at[:, x], ag_s, ag_r)
    for c in agcopies:
        c.start()
    ag[:, x] = attn_o[...]


    def recv_back(n):
        remote(rbuf.at[n], rbuf.at[n], rb_s.at[n], rb_r.at[n], dev(x, wrap(y + 1), z)).wait_recv()

    chain8, chain4 = (
        [
            remote(
                csend.at[m, :, pl.ds(row, T), :], cin.at[m, part], c_s.at[m, part], c_r.at[m, part], dev(wrap(x - 2 + m), y, zt)
            )
            for part, row, zt in ((0, erow, z), (1, prow, zp))
        ]
        for m in range(2)
    )

    @pl.when(x >= 2)
    def _():
        facc[...] = dkv[8].astype(F32)
        for r in (1, 2, 3):
            @pl.when(y + r >= 4)
            def _():
                recv_back(3 + r - 1)
                facc[...] += rbuf[3 + r - 1].astype(F32)

        csend[0] = facc[...].astype(BF16)
        for c in chain8:
            c.start()

    for c in c_win:
        c.wait()
    for c in wcopies:
        c.wait_recv()

    @pl.loop(0, 4)
    def _(xx):
        for n in range(2):
            for b in range(WIN // 128):
                cols = slice(b * 128, (b + 1) * 128)
                winT[n, cols, pl.ds(pl.multiple_of(xx * T, T), T)] = win[n, xx, :, cols].T

    @pl.when(x >= 1)
    def _():
        facc[...] = dkv[4].astype(F32)
        for r in (1, 2, 3):
            recv_back(r - 1)
            facc[...] += rbuf[r - 1].astype(F32)
        csend[1] = facc[...].astype(BF16)
        for c in chain4:
            c.start()

    off = pl.multiple_of(64 * lax.rem(x, 2), 16)

    def over_y(src, buf, s, r_):
        copies = []
        for r in (1, 2, 3):
            yt = wrap(y + r)
            rows = pl.ds(pl.multiple_of(off + 144 * yt, 16), 144)
            copies.append(remote(src.at[rows, :], buf.at[r - 1], s.at[r - 1], r_.at[r - 1], dev(x, yt, z)))
        return copies

    facc[...] = dkv[0].astype(F32)
    for r in (1, 2, 3):
        @pl.when(y + r < 4)
        def _():
            recv_back(3 + r - 1)
            facc[...] += rbuf[3 + r - 1].astype(F32)

    finkv[...] = facc[:, pl.ds(prow, T), :].astype(BF16)
    swap = [remote(finkv, pin, f_s, f_r, dev(x, y, zp))]
    swap[0].start()

    for c in dqcopies:
        c.wait_recv()
    for n in range(2):
        gq_o[n] = (dqin[n].astype(F32) + dqin[n + 2].astype(F32)).astype(BF16)
    for c in c_w:
        c.wait()

    def wrows(hh):
        return pl.ds(pl.multiple_of(COLS * hh, 16), COLS)

    @pl.loop(0, 4)
    def _(hh):
        tq[hh] = sum(
            lax.dot_general(wq[wrows(hh), n * 256 : (n + 1) * 256], gq_o[n], NT, preferred_element_type=F32)
            for n in range(2)
        )

    for c in agcopies:
        c.wait_recv()
    for n in range(2):
        po[:, n * 256 : (n + 1) * 256] = dot(winT[1], ag[n].reshape(4 * T, 256)).astype(BF16)
    yocopies = over_y(po, yo, yo_s, yo_r)
    for c in yocopies:
        c.start()

    swap[0].wait_recv()
    ggcopies = over_x(gv_o, gvg.at[:, x], gg_s, gg_r)
    for m, chain in enumerate((chain8, chain4)):
        @pl.when(x < 2 + m)
        def _():
            for c in chain:
                c.wait_recv()

    for n, out in ((1, gv_o), (0, gk_o)):
        parts = [facc[n, pl.ds(erow, T), :], pin[n].astype(F32)]
        for m in (0, 1):
            parts = [a + jnp.where(x < 2 + m, cin[m, part, n].astype(F32), 0.0) for part, a in enumerate(parts)]
        out[e] = parts[0].astype(BF16)
        out[1 - e] = parts[1].astype(BF16)
        if n == 1:
            for c in ggcopies:
                c.start()
    gvg[:, x] = gv_o[...]

    def terms(hh):
        acc = tq[hh]
        for n in range(2):
            acc = acc + lax.dot_general(wk[wrows(hh), n * D : (n + 1) * D], gk_o[n], NT, preferred_element_type=F32)
            acc = acc + lax.dot_general(wv[wrows(hh), n * D : (n + 1) * D], gv_o[n], NT, preferred_element_type=F32)
        return acc

    hzc = lax.rem(hc + 2, 4)
    tb[0] = terms(hzc).astype(BF16)
    far = remote(tb.at[0], hin.at[0], h_s.at[0], h_r.at[0], (i, hc))
    far.start()
    mine_far = terms(hz)
    far.wait_recv()
    tb[1] = (mine_far + hin[0].astype(F32)).astype(BF16)
    across = remote(tb.at[1], hin.at[1], h_s.at[1], h_r.at[1], (i, hz))
    across.start()
    for c in ggcopies:
        c.wait_recv()
    for n in range(2):
        pv[:, n * D : (n + 1) * D] = dot(winT[0], gvg[n].reshape(4 * T, D)).astype(BF16)
    yvcopies = over_y(pv, yv, yv_s, yv_r)
    for c in yvcopies:
        c.start()

    tb[2] = terms(hc).astype(BF16)
    near = remote(tb.at[2], hin.at[2], h_s.at[2], h_r.at[2], (i, hc))
    near.start()

    def over_z(copies, own, buf, total_s, piece_s, in_s, s, r_):
        for c in copies:
            c.wait_recv()
        acc = own[pl.ds(pl.multiple_of(off + 144 * y, 16), 144), :].astype(F32)
        for r in range(3):
            acc = acc + buf[r].astype(F32)
        total_s[...] = acc
        for zz in range(4):
            piece_s[zz] = total_s[36 * zz : 36 * (zz + 1), :].astype(piece_s.dtype)
        out = []
        for r in (1, 2, 3):
            zt = wrap(z + r)
            out.append(remote(piece_s.at[zt], in_s.at[r - 1], s.at[r - 1], r_.at[r - 1], dev(x, y, zt)))
        for c in out:
            c.start()
        return out

    zocopies = over_z(yocopies, po, yo, zso, zpo, zio, zo_s, zo_r)
    mine_near = terms(h)
    zvcopies = over_z(yvcopies, pv, yv, zsv, zpv, ziv, zv_s, zv_r)

    for c in zocopies:
        c.wait_recv()
    acc = zpo[z].astype(F32)
    for r in range(3):
        acc = acc + zio[r].astype(F32)
    gwo_o[...] = acc
    near.wait_recv()
    across.wait_recv()
    gi_o[...] = (mine_near + hin[2].astype(F32) + hin[1].astype(F32)).astype(BF16)
    for c in zvcopies:
        c.wait_recv()
    acc = zpv[z].astype(F32)
    for r in range(3):
        acc = acc + ziv[r].astype(F32)
    gwv_o[...] = acc

    for c in (
        pair + qcopies + docopies + ocopies + dqcopies + swap + wcopies + agcopies + ggcopies
        + yocopies + yvcopies + zocopies + zvcopies + [far, across, near]
    ):
        c.wait_send()

    @pl.when(x < 3)
    def _():
        for c in first:
            c.wait_send()

    @pl.when((x >= 1) & (x < 3))
    def _():
        fwd_x(4, 8).wait_send()

    for r in (1, 2, 3):
        @pl.when((y + r < 4) | ((x >= 2) & (r == 3)))
        def _():
            fwd_y(r, 1).wait_send()

        if r < 3:
            @pl.when((r > y) & (x >= 1) & (x < 3))
            def _():
                pass_on(r, slot_of(0, r)).wait_send()

        @pl.when(x >= 1)
        def _():
            fwd_y(r, 0).wait_send()
            back_y(0, r).wait_send()

        @pl.when((r <= y) | (x >= 2))
        def _():
            back_y(1, r).wait_send()

    @pl.when(x >= 2)
    def _():
        for c in chain8:
            c.wait_send()

    @pl.when(x >= 1)
    def _():
        for c in chain4:
            c.wait_send()


def layer(xn, q, k, v, wq, wk, wv, wo, cot):
    dma = pltpu.SemaphoreType.DMA
    vm = pltpu.VMEM
    return pl.pallas_call(
        layer_kernel,
        out_shape=(
            jax.ShapeDtypeStruct((COLS, T), BF16),
            jax.ShapeDtypeStruct((36, 256), F32),
            jax.ShapeDtypeStruct((36, 512), F32),
        ),
        in_specs=[pl.BlockSpec(memory_space=pl.ANY)] * 9,
        out_specs=tuple(pl.BlockSpec(memory_space=pltpu.VMEM) for _ in range(3)),
        scratch_shapes=[
            vm((2, T, 256), BF16),
            vm((2, T, 256), BF16),
            vm((2, T, D), BF16),
            vm((2, T, D), BF16),
            vm(wq.shape, BF16),
            vm(wk.shape, BF16),
            vm(wv.shape, BF16),
            vm((2, 4, T, WIN), BF16),
            vm((2, WIN, 4 * T), BF16),
            vm((2, 4, T, 256), BF16),
            vm((2, 4, T, D), BF16),
            vm((WIN, 512), BF16),
            vm((WIN, 256), BF16),
            vm((3, 144, 512), BF16),
            vm((3, 144, 256), BF16),
            vm((144, 512), F32),
            vm((144, 256), F32),
            vm((4, 36, 512), BF16),
            vm((4, 36, 256), BF16),
            vm((3, 36, 512), BF16),
            vm((3, 36, 256), BF16),
            vm((3, COLS, T), BF16),
            vm((3, COLS, T), BF16),
            vm((4, COLS, T), F32),
            vm((2, KEYS, D), F32),
            vm((SLOTS, 2, KEYS, D), BF16),
            vm((4, T, 256), BF16),
            vm((4, T, 256), BF16),
            vm((2, T, 256), BF16),
            vm(cot.shape, BF16),
            vm(wo.shape, BF16),
            vm((ROWS, D), BF16),
            vm((ROWS, D), BF16),
            vm((D, ROWS), BF16),
            vm((D, ROWS), BF16),
            vm((SLOTS, KEYS, ROWS), F32),
            vm((SLOTS, KEYS, ROWS), F32),
            vm((KEYS, ROWS), BF16),
            vm((KEYS, ROWS), BF16),
            vm((SLOTS, 8, ROWS), F32),
            vm((8, ROWS), F32),
            vm((8, ROWS), F32),
            vm((8, ROWS), F32),
            vm((D, ROWS), F32),
            vm((D, ROWS), F32),
            vm((4, T, 256), BF16),
            vm((4, T, 256), BF16),
            vm((4, T, 256), BF16),
            vm((4, T, 256), BF16),
            vm((SLOTS, 2, KEYS, D), BF16),
            vm((6, 2, KEYS, D), BF16),
            vm((2, 2, KEYS, D), BF16),
            vm((2, 2, 2, T, D), BF16),
            vm((2, T, D), BF16),
            vm((2, T, D), BF16),
            dma((10,)), dma((2,)), dma((2,)), dma((3,)), dma((3,)), dma((3,)), dma((3,)),
            dma((2,)), dma((6,)), dma((SLOTS,)), dma, dma, dma((3,)), dma((3,)), dma((3,)), dma((3,)),
            dma((6,)), dma((6,)), dma((2, 2)), dma((2, 2)), dma, dma,
            dma((2,)), dma((4,)), dma((4,)), dma((2, 3)), dma((2, 3)), *([dma((3,))] * 2), *([dma((3,))] * 2), *([dma((3,))] * 10),
        ],
        compiler_params=pltpu.CompilerParams(
            collective_id=1, has_side_effects=True, vmem_limit_bytes=62 * 1024 * 1024,
        ),
        name="layer",
    )(xn, q, k, v, wq, wk, wv, wo, cot)


def hand_over(*refs):
    for n in range(3):
        refs[3 + n][...] = refs[n][...]


def local(*args):
    results = layer(*args)
    vmem = tuple(pl.BlockSpec(memory_space=pltpu.VMEM) for _ in range(3))
    grad_input, grad_wvalue, grad_woutput = pl.pallas_call(
        hand_over,
        out_shape=tuple(jax.ShapeDtypeStruct(a.shape, a.dtype) for a in results),
        in_specs=vmem,
        out_specs=vmem,
        name="hand_over",
    )(*results)
    return grad_input.T, grad_wvalue, grad_woutput.T


def solution(mesh):
    seq, both, cols, rows = P("seq", None), P("seq", "head"), P(None, "head"), P("head", None)
    return jax.shard_map(
        local,
        mesh=mesh,
        in_specs=(seq, both, both, both, cols, cols, cols, rows, seq),
        out_specs=(both, both, P("head", "seq")),
        check_vma=False,
    )
```

```python
import functools
import math

import jax
import jax.numpy as jnp
from jax import lax
from jax.experimental import pallas as pl
from jax.experimental.pallas import tpu as pltpu
from jax.sharding import PartitionSpec as P

MESH = pl.DeviceIdType.MESH
F32 = jnp.float32
BF16 = jnp.bfloat16
LOGIT_SCALE = 1.0 / 12.0
EXP2_SCALE = LOGIT_SCALE * math.log2(math.e)
NEG = -1e30
T = 128
D = 128
SLOTS = 9
ROWS = 1024
WIN = 640
COLS = 576
KEYS = 256
NT = (((1,), (1,)), ((), ()))


def dot(a, b):
    return jnp.dot(a, b, preferred_element_type=F32)


def place():
    i = lax.axis_index("seq")
    h = lax.axis_index("head")
    x = lax.div(i, 16)
    y = lax.rem(lax.div(i, 4), 4)
    z = lax.rem(i, 4)
    return i, h, x, y, z


def layer_kernel(
    x_hbm, q_hbm, k_hbm, v_hbm, wq_hbm, wk_hbm, wv_hbm, wo_hbm, cot_hbm,
    gi_h, gwv_h, gwo_h, gi_o, gwv_o, gwo_o, res_s,
    attn_o, gq_o, gk_o, gv_o, wq, wk, wv, win, winT, ag, gvg, po, pv, yo, yv, zso, zsv, zpo, zpv, zio, ziv, tb, hin,
    tq, facc, kv, qg, dog, og, cot, wo, q2, do2, qT, doT, sbuf, dpbuf, pb_s, ds_s, ms, st, st_in, fin,
    oT, dqT, osend, oin, dqsend, dqin, dkv, rbuf, csend, cin, finkv, pin,
    lsem, pair_s, pair_r, q_s, q_r, do_s, do_r, kvx_s, kvy_s, kv_r, st_s, st_r, o_s, o_r, dq_s, dq_r,
    rb_s, rb_r, c_s, c_r, f_s, f_r,
    xw_s, fx_s, fx_r, w_s, w_r, ag_s, ag_r, gg_s, gg_r, yo_s, yo_r, yv_s, yv_r, zo_s, zo_r, zv_s, zv_r, h_s, h_r,
):
    i, h, x, y, z = place()
    e, f = lax.rem(z, 2), lax.div(z, 2)
    S = x * 4 + y

    def dev(x_, y_, z_):
        return (x_ * 16 + y_ * 4 + z_, h)

    def wrap(a):
        return lax.rem(a + 4, 4)

    def remote(src, dst, s, r, to):
        return pltpu.make_async_remote_copy(
            src_ref=src, dst_ref=dst, send_sem=s, recv_sem=r, device_id=to, device_id_type=MESH
        )

    erow = pl.multiple_of(e * T, T)
    prow = pl.multiple_of((1 - e) * T, T)
    ecol2 = pl.multiple_of(e * 256, 256)
    c_wo = pltpu.make_async_copy(wo_hbm, wo, lsem.at[0])
    c_cot = pltpu.make_async_copy(cot_hbm, cot, lsem.at[1])
    c_k = pltpu.make_async_copy(k_hbm.at[:, pl.ds(erow, D)], kv.at[0, 0, pl.ds(erow, T), :], lsem.at[2])
    c_v = pltpu.make_async_copy(v_hbm.at[:, pl.ds(erow, D)], kv.at[0, 1, pl.ds(erow, T), :], lsem.at[3])
    c_q = pltpu.make_async_copy(q_hbm.at[:, pl.ds(ecol2, 256)], qg.at[z], lsem.at[4])
    for c in (c_wo, c_cot, c_k, c_v, c_q):
        c.start()

    def window(xt):
        return pl.ds(pl.multiple_of(lax.div(9 * xt, 2) * 128, 128), WIN)

    c_win = [
        pltpu.make_async_copy(src.at[:, window(x)], win.at[n, x], lsem.at[5 + n]) for n, src in ((0, x_hbm), (1, cot_hbm))
    ]
    c_w = [pltpu.make_async_copy(src, dst, lsem.at[7 + n]) for n, (src, dst) in enumerate(((wq_hbm, wq), (wk_hbm, wk), (wv_hbm, wv)))]

    bar = pltpu.get_barrier_semaphore()
    for r in (1, 2, 3):
        for to in (dev(x, y, wrap(z + r)), dev(x, wrap(y + r), z), dev(wrap(x + r), y, z)):
            pl.semaphore_signal(bar, inc=1, device_id=to, device_id_type=MESH)
    hc = h + 1 - 2 * lax.rem(h, 2)
    hz = lax.rem(h + 2, 4)
    for to in ((i, hc), (i, hz)):
        pl.semaphore_signal(bar, inc=1, device_id=to, device_id_type=MESH)
    zp = z + 1 - 2 * e
    for r in (1, 2, 3):
        pl.semaphore_signal(bar, inc=1, device_id=dev(wrap(x + r), y, zp), device_id_type=MESH)
    pl.semaphore_wait(bar, 14)

    pair = [
        remote(src.at[:, pl.ds(prow, D)], kv.at[0, n, pl.ds(erow, T), :], pair_s.at[n], pair_r.at[n], dev(x, y, zp))
        for n, src in ((0, k_hbm), (1, v_hbm))
    ]
    for c in pair:
        c.start()

    first = [
        remote(src.at[:, pl.ds(col, D)], kv.at[4, n, pl.ds(erow, T), :], fx_s.at[m + n], fx_r.at[m + n], dev(wrap(x + 1), y, zt))
        for m, col, zt in ((0, erow, z), (2, prow, zp))
        for n, src in ((0, k_hbm), (1, v_hbm))
    ]

    @pl.when(x < 3)
    def _():
        for c in first:
            c.start()

    def gathered(src_of, buf, s, r_):
        copies = []
        for r in (1, 2, 3):
            zt = wrap(z + r)
            copies.append(remote(src_of(zt), buf.at[z], s.at[r - 1], r_.at[r - 1], dev(x, y, zt)))
        return copies

    qcopies = gathered(
        lambda zt: q_hbm.at[:, pl.ds(pl.multiple_of(lax.rem(zt, 2) * 256, 256), 256)], qg, q_s, q_r
    )
    for c in qcopies:
        c.start()

    c_wo.wait()
    c_cot.wait()
    grad = lax.dot_general(cot[...], wo[...], NT, preferred_element_type=F32).astype(BF16)
    og[0] = grad[:, :256]
    og[1] = grad[:, 256:]
    docopies = gathered(lambda zt: og.at[lax.rem(zt, 2)], dog, do_s, do_r)
    for c in docopies:
        c.start()
    dog[z] = og[e]

    c_k.wait()
    c_v.wait()
    for c in pair:
        c.wait_recv()

    def fwd_x(src, dst):
        return remote(kv.at[src], kv.at[dst], kvx_s.at[dst // 8], kv_r.at[dst], dev(wrap(x + 1), y, z))

    def fwd_y(r, kind):
        yt = wrap(y + r)
        up = yt > y
        if kind == 0:
            src, dst = 4, 4 + yt - y
        else:
            src, dst = jnp.where(up, 0, 8), jnp.where(up, yt - y, 8 + yt - y)
        return remote(kv.at[src], kv.at[dst], kvy_s.at[kind * 3 + r - 1], kv_r.at[dst], dev(x, yt, z))

    for r in (1, 2, 3):
        @pl.when(y + r < 4)
        def _():
            fwd_y(r, 1).start()

    def recv_slot(d):
        remote(kv.at[d], kv.at[d], kvx_s.at[0], kv_r.at[d], dev(wrap(x + 1), y, z)).wait_recv()

    @pl.when(x >= 1)
    def _():
        for c in first:
            c.wait_recv()
        for r in (1, 2, 3):
            fwd_y(r, 0).start()

    @pl.when((x >= 1) & (x < 3))
    def _():
        fwd_x(4, 8).start()

    wcopies = []
    for r in (1, 2, 3):
        xt = wrap(x + r)
        for n, src in ((0, x_hbm), (1, cot_hbm)):
            wcopies.append(
                remote(src.at[:, window(xt)], win.at[n, x], w_s.at[n, r - 1], w_r.at[n, r - 1], dev(xt, y, z))
            )

    c_q.wait()
    @pl.when(x >= 2)
    def _():
        recv_slot(8)

        @pl.when(y >= 1)
        def _():
            fwd_y(3, 1).start()

    for c in qcopies:
        c.wait_recv()

    @pl.loop(0, 4)
    def _(zz):
        for j in range(2):
            rows = pl.ds(pl.multiple_of(j * 512 + zz * T, T), T)
            qb = qg[zz, :, j * D : (j + 1) * D]
            q2[rows, :] = qb
            qT[:, rows] = qb.T

    st[...] = jnp.concatenate([jnp.full((1, ROWS), NEG, F32), jnp.zeros((7, ROWS), F32)], axis=0)
    oT[...] = jnp.zeros_like(oT)
    dqT[...] = jnp.zeros_like(dqT)

    def slot_of(kind, r):
        if kind == 0:
            return 4 + jnp.where(r <= y, r, r - 4)
        return jnp.where(r <= y, r, r + 4)

    quarters = [slice(c * 256, (c + 1) * 256) for c in range(4)]

    def scores(d, edge):
        kd = kv[d, 0]
        low = jnp.where(d == 0, 0, -100000)
        high = jnp.where(d == 8, 0, 100000)
        for c, cs in enumerate(quarters):
            s = dot(kd, qT[:, cs])
            if edge:
                gap = (
                    lax.broadcasted_iota(jnp.int32, (KEYS, 256), 1)
                    - lax.broadcasted_iota(jnp.int32, (KEYS, 256), 0)
                    + ((c % 2) * 256 - f * 256)
                )
                s = jnp.where((gap >= low) & (gap < high), s, NEG)
            sbuf[d, :, cs] = s
            ms[d, 0:1, cs] = jnp.max(s, axis=0, keepdims=True)

    def probabilities(d):
        vd = kv[d, 1]
        vt = vd.T
        for cs in quarters:
            dpbuf[d, :, cs] = dot(vd, doT[:, cs])
        for cs in quarters:
            before = st[0:1, cs]
            top = jnp.maximum(before, ms[d, 0:1, cs])
            p = jnp.exp2((sbuf[d, :, cs] - top) * EXP2_SCALE)
            keep = jnp.exp2((before - top) * EXP2_SCALE)
            st[0:1, cs] = top
            st[1:2, cs] = st[1:2, cs] * keep + jnp.sum(p, axis=0, keepdims=True)
            st[2:3, cs] = st[2:3, cs] * keep + jnp.sum(p * dpbuf[d, :, cs], axis=0, keepdims=True)
            ms[d, 0:1, cs] = top
            sbuf[d, :, cs] = p
            pb_s[:, cs] = p.astype(BF16)
            oT[:, cs] = oT[:, cs] * keep + dot(vt, pb_s[:, cs])

    def order(t):
        kind = (t >= 5) & (t < 8)
        r = jnp.where(t < 4, t, jnp.where(t < 8, t - 4, t - 8))
        d = jnp.where(r == 0, t, jnp.where(kind, slot_of(0, r), slot_of(1, r)))
        fits = (S >= d) & ((r == 0) | kind | jnp.where(t < 4, r <= y, r > y))
        return d, r, fits

    def pass_on(r, d):
        return remote(kv.at[d], kv.at[r + 4], xw_s.at[r - 1], kv_r.at[r + 4], dev(wrap(x + 1), y, z))

    def score_step(t):
        d, r, fits = order(t)

        @pl.when(fits & ((t == 0) | (t == 8)))
        def _():
            scores(d, True)

        @pl.when(fits & (t != 0) & (t != 8))
        def _():
            @pl.when(r > 0)
            def _():
                recv_slot(d)

            @pl.when((t >= 5) & (t < 7) & (r > y) & (x < 3))
            def _():
                pass_on(r, d).start()

            scores(d, False)

    def prob_step(t):
        d, r, fits = order(t)

        @pl.when(fits)
        def _():
            probabilities(d)

    pl.loop(0, 8)(score_step)

    for c in docopies:
        c.wait_recv()
    for c in wcopies + c_win + c_w:
        c.start()


    @pl.loop(0, 4)
    def _(zz):
        for j in range(2):
            rows = pl.ds(pl.multiple_of(j * 512 + zz * T, T), T)
            db = dog[zz, :, j * D : (j + 1) * D]
            do2[rows, :] = db
            doT[:, rows] = db.T

    pl.loop(0, 8)(prob_step)

    @pl.loop(8, 12)
    def _(t):
        score_step(t)
        prob_step(t)

    stat = remote(st, st_in, st_s, st_r, dev(x, y, wrap(z + 2)))
    stat.start()
    stat.wait()
    top = jnp.maximum(st[0:1, :], st_in[0:1, :])
    mine = jnp.exp2((st[0:1, :] - top) * EXP2_SCALE)
    other = jnp.exp2((st_in[0:1, :] - top) * EXP2_SCALE)
    inv = 1.0 / (st[1:2, :] * mine + st_in[1:2, :] * other)
    fin[0:1, :] = top
    fin[1:2, :] = inv
    fin[2:3, :] = (st[2:3, :] * mine + st_in[2:3, :] * other) * inv
    oT[...] = oT[...] * (mine * inv)

    def spread(srcT, factor, sendbuf, inbuf, s, r_):
        for j in range(2):
            for zz in range(4):
                piece = srcT[:, j * 512 + zz * T : j * 512 + (zz + 1) * T]
                sendbuf[zz, :, j * D : (j + 1) * D] = (piece * factor).T.astype(BF16)
        copies = []
        for r in (1, 2, 3):
            zt = wrap(z + r)
            copies.append(remote(sendbuf.at[zt], inbuf.at[z], s.at[r - 1], r_.at[r - 1], dev(x, y, zt)))
        for c in copies:
            c.start()
        inbuf[z] = sendbuf[z]
        return copies

    ocopies = spread(oT, 1.0, osend, oin, o_s, o_r)

    def grad_slot(d):
        w = jnp.exp2((ms[d, 0:1, :] - fin[0:1, :]) * EXP2_SCALE) * fin[1:2, :]
        kt = kv[d, 0].T
        for c in range(4):
            cs = slice(c * 256, (c + 1) * 256)
            p = sbuf[d, :, cs] * w[:, cs]
            pb_s[:, cs] = p.astype(BF16)
            ds = (p * (dpbuf[d, :, cs] - fin[2:3, cs])).astype(BF16)
            ds_s[:, cs] = ds
            dqT[:, cs] += dot(kt, ds)
        dkv[d, 0] = (LOGIT_SCALE * dot(ds_s[...], q2[...])).astype(BF16)
        dkv[d, 1] = dot(pb_s[...], do2[...]).astype(BF16)

    def back_y(kind, r):
        d = slot_of(kind, r)
        n = kind * 3 + r - 1
        return remote(dkv.at[d], rbuf.at[n], rb_s.at[n], rb_r.at[n], dev(x, wrap(y - r), z))

    def grad_step(t):
        kind = (t >= 4) & (t < 7)
        r = jnp.where(t < 3, t + 1, jnp.where(kind, t - 3, jnp.where((t >= 8) & (t < 11), t - 7, 0)))
        d = jnp.where(r == 0, jnp.where(t == 3, 8, jnp.where(t == 7, 4, 0)), jnp.where(kind, slot_of(0, r), slot_of(1, r)))
        fits = (r == 0) | kind | jnp.where(t < 3, r > y, r <= y)

        @pl.when((S >= d) & fits)
        def _():
            grad_slot(d)

            @pl.when(r > 0)
            def _():
                n = jnp.where(kind, r - 1, r + 2)
                remote(dkv.at[d], rbuf.at[n], rb_s.at[n], rb_r.at[n], dev(x, wrap(y - r), z)).start()

    pl.loop(0, 12)(grad_step)

    dqcopies = spread(dqT, LOGIT_SCALE, dqsend, dqin, dq_s, dq_r)

    def over_x(src, dst, s, r_):
        return [remote(src, dst, s.at[r - 1], r_.at[r - 1], dev(wrap(x + r), y, z)) for r in (1, 2, 3)]

    for c in ocopies:
        c.wait_recv()
    for n in range(2):
        attn_o[n] = (oin[n].astype(F32) + oin[n + 2].astype(F32)).astype(BF16)
    agcopies = over_x(attn_o, ag.at[:, x], ag_s, ag_r)
    for c in agcopies:
        c.start()
    ag[:, x] = attn_o[...]


    def recv_back(n):
        remote(rbuf.at[n], rbuf.at[n], rb_s.at[n], rb_r.at[n], dev(x, wrap(y + 1), z)).wait_recv()

    chain8, chain4 = (
        [
            remote(
                csend.at[m, :, pl.ds(row, T), :], cin.at[m, part], c_s.at[m, part], c_r.at[m, part], dev(wrap(x - 2 + m), y, zt)
            )
            for part, row, zt in ((0, erow, z), (1, prow, zp))
        ]
        for m in range(2)
    )

    @pl.when(x >= 2)
    def _():
        facc[...] = dkv[8].astype(F32)
        for r in (1, 2, 3):
            @pl.when(y + r >= 4)
            def _():
                recv_back(3 + r - 1)
                facc[...] += rbuf[3 + r - 1].astype(F32)

        csend[0] = facc[...].astype(BF16)
        for c in chain8:
            c.start()

    @pl.when(x >= 1)
    def _():
        facc[...] = dkv[4].astype(F32)
        for r in (1, 2, 3):
            recv_back(r - 1)
            facc[...] += rbuf[r - 1].astype(F32)
        csend[1] = facc[...].astype(BF16)
        for c in chain4:
            c.start()

    off = pl.multiple_of(64 * lax.rem(x, 2), 16)

    def over_y(src, buf, s, r_):
        copies = []
        for r in (1, 2, 3):
            yt = wrap(y + r)
            rows = pl.ds(pl.multiple_of(off + 144 * yt, 16), 144)
            copies.append(remote(src.at[rows, :], buf.at[r - 1], s.at[r - 1], r_.at[r - 1], dev(x, yt, z)))
        return copies

    facc[...] = dkv[0].astype(F32)
    for r in (1, 2, 3):
        @pl.when(y + r < 4)
        def _():
            recv_back(3 + r - 1)
            facc[...] += rbuf[3 + r - 1].astype(F32)

    finkv[...] = facc[:, pl.ds(prow, T), :].astype(BF16)
    swap = [remote(finkv, pin, f_s, f_r, dev(x, y, zp))]
    swap[0].start()

    for c in dqcopies:
        c.wait_recv()
    for n in range(2):
        gq_o[n] = (dqin[n].astype(F32) + dqin[n + 2].astype(F32)).astype(BF16)
    for c in c_w:
        c.wait()

    def wrows(hh):
        return pl.ds(pl.multiple_of(COLS * hh, 16), COLS)

    @pl.loop(0, 4)
    def _(hh):
        tq[hh] = sum(
            lax.dot_general(wq[wrows(hh), n * 256 : (n + 1) * 256], gq_o[n], NT, preferred_element_type=F32)
            for n in range(2)
        )

    for c in c_win:
        c.wait()
    for c in wcopies:
        c.wait_recv()

    @pl.loop(0, 4)
    def _(xx):
        for n in range(2):
            for b in range(WIN // 128):
                cols = slice(b * 128, (b + 1) * 128)
                winT[n, cols, pl.ds(pl.multiple_of(xx * T, T), T)] = win[n, xx, :, cols].T

    for c in agcopies:
        c.wait_recv()
    for n in range(2):
        po[:, n * 256 : (n + 1) * 256] = dot(winT[1], ag[n].reshape(4 * T, 256)).astype(BF16)
    yocopies = over_y(po, yo, yo_s, yo_r)
    for c in yocopies:
        c.start()

    swap[0].wait_recv()
    ggcopies = over_x(gv_o, gvg.at[:, x], gg_s, gg_r)
    for m, chain in enumerate((chain8, chain4)):
        @pl.when(x < 2 + m)
        def _():
            for c in chain:
                c.wait_recv()

    for n, out in ((1, gv_o), (0, gk_o)):
        parts = [facc[n, pl.ds(erow, T), :], pin[n].astype(F32)]
        for m in (0, 1):
            parts = [a + jnp.where(x < 2 + m, cin[m, part, n].astype(F32), 0.0) for part, a in enumerate(parts)]
        out[e] = parts[0].astype(BF16)
        out[1 - e] = parts[1].astype(BF16)
        if n == 1:
            for c in ggcopies:
                c.start()
    gvg[:, x] = gv_o[...]

    def terms(hh):
        acc = tq[hh]
        for n in range(2):
            acc = acc + lax.dot_general(wk[wrows(hh), n * D : (n + 1) * D], gk_o[n], NT, preferred_element_type=F32)
            acc = acc + lax.dot_general(wv[wrows(hh), n * D : (n + 1) * D], gv_o[n], NT, preferred_element_type=F32)
        return acc

    hzc = lax.rem(hc + 2, 4)
    tb[0] = terms(hzc).astype(BF16)
    far = remote(tb.at[0], hin.at[0], h_s.at[0], h_r.at[0], (i, hc))
    far.start()
    mine_far = terms(hz)
    far.wait_recv()
    tb[1] = (mine_far + hin[0].astype(F32)).astype(BF16)
    across = remote(tb.at[1], hin.at[1], h_s.at[1], h_r.at[1], (i, hz))
    across.start()
    for c in ggcopies:
        c.wait_recv()
    for n in range(2):
        pv[:, n * D : (n + 1) * D] = dot(winT[0], gvg[n].reshape(4 * T, D)).astype(BF16)
    yvcopies = over_y(pv, yv, yv_s, yv_r)
    for c in yvcopies:
        c.start()

    tb[2] = terms(hc).astype(BF16)
    near = remote(tb.at[2], hin.at[2], h_s.at[2], h_r.at[2], (i, hc))
    near.start()

    def over_z(copies, own, buf, total_s, piece_s, in_s, s, r_):
        for c in copies:
            c.wait_recv()
        acc = own[pl.ds(pl.multiple_of(off + 144 * y, 16), 144), :].astype(F32)
        for r in range(3):
            acc = acc + buf[r].astype(F32)
        total_s[...] = acc
        for zz in range(4):
            piece_s[zz] = total_s[36 * zz : 36 * (zz + 1), :].astype(piece_s.dtype)
        out = []
        for r in (1, 2, 3):
            zt = wrap(z + r)
            out.append(remote(piece_s.at[zt], in_s.at[r - 1], s.at[r - 1], r_.at[r - 1], dev(x, y, zt)))
        for c in out:
            c.start()
        return out

    zocopies = over_z(yocopies, po, yo, zso, zpo, zio, zo_s, zo_r)
    mine_near = terms(h)
    zvcopies = over_z(yvcopies, pv, yv, zsv, zpv, ziv, zv_s, zv_r)

    for c in zocopies:
        c.wait_recv()
    acc = zpo[z].astype(F32)
    for r in range(3):
        acc = acc + zio[r].astype(F32)
    gwo_o[...] = acc
    results = [
        pltpu.make_async_copy(src, dst, res_s.at[n])
        for n, (src, dst) in enumerate(((gi_o, gi_h), (gwv_o, gwv_h), (gwo_o, gwo_h)))
    ]
    results[2].start()
    near.wait_recv()
    across.wait_recv()
    gi_o[...] = (mine_near + hin[2].astype(F32) + hin[1].astype(F32)).astype(BF16)
    results[0].start()
    for c in zvcopies:
        c.wait_recv()
    acc = zpv[z].astype(F32)
    for r in range(3):
        acc = acc + ziv[r].astype(F32)
    gwv_o[...] = acc

    results[1].start()
    for c in results:
        c.wait()

    for c in (
        pair + qcopies + docopies + ocopies + dqcopies + swap + wcopies + agcopies + ggcopies
        + yocopies + yvcopies + zocopies + zvcopies + [far, across, near]
    ):
        c.wait_send()

    @pl.when(x < 3)
    def _():
        for c in first:
            c.wait_send()

    @pl.when((x >= 1) & (x < 3))
    def _():
        fwd_x(4, 8).wait_send()

    for r in (1, 2, 3):
        @pl.when((y + r < 4) | ((x >= 2) & (r == 3)))
        def _():
            fwd_y(r, 1).wait_send()

        if r < 3:
            @pl.when((r > y) & (x >= 1) & (x < 3))
            def _():
                pass_on(r, slot_of(0, r)).wait_send()

        @pl.when(x >= 1)
        def _():
            fwd_y(r, 0).wait_send()
            back_y(0, r).wait_send()

        @pl.when((r <= y) | (x >= 2))
        def _():
            back_y(1, r).wait_send()

    @pl.when(x >= 2)
    def _():
        for c in chain8:
            c.wait_send()

    @pl.when(x >= 1)
    def _():
        for c in chain4:
            c.wait_send()


def layer(xn, q, k, v, wq, wk, wv, wo, cot):
    dma = pltpu.SemaphoreType.DMA
    vm = pltpu.VMEM
    return pl.pallas_call(
        layer_kernel,
        out_shape=(
            jax.ShapeDtypeStruct((COLS, T), BF16),
            jax.ShapeDtypeStruct((36, 256), F32),
            jax.ShapeDtypeStruct((36, 512), F32),
        ),
        in_specs=[pl.BlockSpec(memory_space=pl.ANY)] * 9,
        out_specs=tuple(pl.BlockSpec(memory_space=pl.ANY) for _ in range(3)),
        scratch_shapes=[
            vm((COLS, T), BF16),
            vm((36, 256), F32),
            vm((36, 512), F32),
            dma((3,)),
            vm((2, T, 256), BF16),
            vm((2, T, 256), BF16),
            vm((2, T, D), BF16),
            vm((2, T, D), BF16),
            vm(wq.shape, BF16),
            vm(wk.shape, BF16),
            vm(wv.shape, BF16),
            vm((2, 4, T, WIN), BF16),
            vm((2, WIN, 4 * T), BF16),
            vm((2, 4, T, 256), BF16),
            vm((2, 4, T, D), BF16),
            vm((WIN, 512), BF16),
            vm((WIN, 256), BF16),
            vm((3, 144, 512), BF16),
            vm((3, 144, 256), BF16),
            vm((144, 512), F32),
            vm((144, 256), F32),
            vm((4, 36, 512), BF16),
            vm((4, 36, 256), BF16),
            vm((3, 36, 512), BF16),
            vm((3, 36, 256), BF16),
            vm((3, COLS, T), BF16),
            vm((3, COLS, T), BF16),
            vm((4, COLS, T), F32),
            vm((2, KEYS, D), F32),
            vm((SLOTS, 2, KEYS, D), BF16),
            vm((4, T, 256), BF16),
            vm((4, T, 256), BF16),
            vm((2, T, 256), BF16),
            vm(cot.shape, BF16),
            vm(wo.shape, BF16),
            vm((ROWS, D), BF16),
            vm((ROWS, D), BF16),
            vm((D, ROWS), BF16),
            vm((D, ROWS), BF16),
            vm((SLOTS, KEYS, ROWS), F32),
            vm((SLOTS, KEYS, ROWS), F32),
            vm((KEYS, ROWS), BF16),
            vm((KEYS, ROWS), BF16),
            vm((SLOTS, 8, ROWS), F32),
            vm((8, ROWS), F32),
            vm((8, ROWS), F32),
            vm((8, ROWS), F32),
            vm((D, ROWS), F32),
            vm((D, ROWS), F32),
            vm((4, T, 256), BF16),
            vm((4, T, 256), BF16),
            vm((4, T, 256), BF16),
            vm((4, T, 256), BF16),
            vm((SLOTS, 2, KEYS, D), BF16),
            vm((6, 2, KEYS, D), BF16),
            vm((2, 2, KEYS, D), BF16),
            vm((2, 2, 2, T, D), BF16),
            vm((2, T, D), BF16),
            vm((2, T, D), BF16),
            dma((10,)), dma((2,)), dma((2,)), dma((3,)), dma((3,)), dma((3,)), dma((3,)),
            dma((2,)), dma((6,)), dma((SLOTS,)), dma, dma, dma((3,)), dma((3,)), dma((3,)), dma((3,)),
            dma((6,)), dma((6,)), dma((2, 2)), dma((2, 2)), dma, dma,
            dma((2,)), dma((4,)), dma((4,)), dma((2, 3)), dma((2, 3)), *([dma((3,))] * 2), *([dma((3,))] * 2), *([dma((3,))] * 10),
        ],
        compiler_params=pltpu.CompilerParams(
            collective_id=1, has_side_effects=True, vmem_limit_bytes=62 * 1024 * 1024,
        ),
        name="layer",
    )(xn, q, k, v, wq, wk, wv, wo, cot)


def hand_over(*refs):
    into = [pltpu.make_async_copy(refs[n], refs[6 + n], refs[9].at[n]) for n in range(3)]
    out = [pltpu.make_async_copy(refs[6 + n], refs[3 + n], refs[9].at[3 + n]) for n in range(3)]
    for c in into:
        c.start()
    for n in range(3):
        into[n].wait()
        out[n].start()
    for c in out:
        c.wait()


def local(*args):
    results = layer(*args)
    hbm = tuple(pl.BlockSpec(memory_space=pl.ANY) for _ in range(3))
    grad_input, grad_wvalue, grad_woutput = pl.pallas_call(
        hand_over,
        out_shape=tuple(jax.ShapeDtypeStruct(a.shape, a.dtype) for a in results),
        in_specs=hbm,
        out_specs=hbm,
        scratch_shapes=[pltpu.VMEM(a.shape, a.dtype) for a in results] + [pltpu.SemaphoreType.DMA((6,))],
        name="hand_over",
    )(*results)
    return grad_input.T, grad_wvalue, grad_woutput.T


def solution(mesh):
    seq, both, cols, rows = P("seq", None), P("seq", "head"), P(None, "head"), P("head", None)
    return jax.shard_map(
        local,
        mesh=mesh,
        in_specs=(seq, both, both, both, cols, cols, cols, rows, seq),
        out_specs=(both, both, P("head", "seq")),
        check_vma=False,
    )
```

```python
import functools
import math

import jax
import jax.numpy as jnp
from jax import lax
from jax.experimental import pallas as pl
from jax.experimental.pallas import tpu as pltpu
from jax.sharding import PartitionSpec as P

MESH = pl.DeviceIdType.MESH
F32 = jnp.float32
BF16 = jnp.bfloat16
LOGIT_SCALE = 1.0 / 12.0
EXP2_SCALE = LOGIT_SCALE * math.log2(math.e)
NEG = -1e30
T = 128
D = 128
SLOTS = 9
ROWS = 1024
WIN = 640
COLS = 576
KEYS = 256
NT = (((1,), (1,)), ((), ()))


def dot(a, b):
    return jnp.dot(a, b, preferred_element_type=F32)


def place():
    i = lax.axis_index("seq")
    h = lax.axis_index("head")
    x = lax.div(i, 16)
    y = lax.rem(lax.div(i, 4), 4)
    z = lax.rem(i, 4)
    return i, h, x, y, z


def layer_kernel(
    x_hbm, q_hbm, k_hbm, v_hbm, wq_hbm, wk_hbm, wv_hbm, wo_hbm, cot_hbm,
    gi_h, gwv_h, gwo_h, gi_o, gwv_o, gwo_o, res_s,
    attn_o, gq_o, gk_o, gv_o, wq, wk, wv, win, winT, ag, gvg, po, pv, yo, yv, zso, zsv, zpo, zpv, zio, ziv, tb, hin,
    tq, facc, kv, qg, dog, og, cot, wo, q2, do2, qT, doT, sbuf, dpbuf, pb_s, ds_s, ms, st, st_in, fin,
    oT, dqT, osend, oin, dqsend, dqin, dkv, rbuf, csend, cin, finkv, pin,
    lsem, pair_s, pair_r, q_s, q_r, do_s, do_r, kvx_s, kvy_s, kv_r, st_s, st_r, o_s, o_r, dq_s, dq_r,
    rb_s, rb_r, c_s, c_r, f_s, f_r,
    xw_s, fx_s, fx_r, w_s, w_r, ag_s, ag_r, gg_s, gg_r, yo_s, yo_r, yv_s, yv_r, zo_s, zo_r, zv_s, zv_r, h_s, h_r,
):
    i, h, x, y, z = place()
    e, f = lax.rem(z, 2), lax.div(z, 2)
    S = x * 4 + y

    def dev(x_, y_, z_):
        return (x_ * 16 + y_ * 4 + z_, h)

    def wrap(a):
        return lax.rem(a + 4, 4)

    def remote(src, dst, s, r, to):
        return pltpu.make_async_remote_copy(
            src_ref=src, dst_ref=dst, send_sem=s, recv_sem=r, device_id=to, device_id_type=MESH
        )

    erow = pl.multiple_of(e * T, T)
    prow = pl.multiple_of((1 - e) * T, T)
    ecol2 = pl.multiple_of(e * 256, 256)
    c_wo = pltpu.make_async_copy(wo_hbm, wo, lsem.at[0])
    c_cot = pltpu.make_async_copy(cot_hbm, cot, lsem.at[1])
    c_k = pltpu.make_async_copy(k_hbm.at[:, pl.ds(erow, D)], kv.at[0, 0, pl.ds(erow, T), :], lsem.at[2])
    c_v = pltpu.make_async_copy(v_hbm.at[:, pl.ds(erow, D)], kv.at[0, 1, pl.ds(erow, T), :], lsem.at[3])
    c_q = pltpu.make_async_copy(q_hbm.at[:, pl.ds(ecol2, 256)], qg.at[z], lsem.at[4])
    for c in (c_wo, c_cot, c_k, c_v, c_q):
        c.start()

    def window(xt):
        return pl.ds(pl.multiple_of(lax.div(9 * xt, 2) * 128, 128), WIN)

    c_win = [
        pltpu.make_async_copy(src.at[:, window(x)], win.at[n, x], lsem.at[5 + n]) for n, src in ((0, x_hbm), (1, cot_hbm))
    ]
    c_w = [pltpu.make_async_copy(src, dst, lsem.at[7 + n]) for n, (src, dst) in enumerate(((wq_hbm, wq), (wk_hbm, wk), (wv_hbm, wv)))]

    bar = pltpu.get_barrier_semaphore()
    for r in (1, 2, 3):
        for to in (dev(x, y, wrap(z + r)), dev(x, wrap(y + r), z), dev(wrap(x + r), y, z)):
            pl.semaphore_signal(bar, inc=1, device_id=to, device_id_type=MESH)
    hc = h + 1 - 2 * lax.rem(h, 2)
    hz = lax.rem(h + 2, 4)
    for to in ((i, hc), (i, hz)):
        pl.semaphore_signal(bar, inc=1, device_id=to, device_id_type=MESH)
    zp = z + 1 - 2 * e
    for r in (1, 2, 3):
        pl.semaphore_signal(bar, inc=1, device_id=dev(wrap(x + r), y, zp), device_id_type=MESH)
    pl.semaphore_wait(bar, 14)

    pair = [
        remote(src.at[:, pl.ds(prow, D)], kv.at[0, n, pl.ds(erow, T), :], pair_s.at[n], pair_r.at[n], dev(x, y, zp))
        for n, src in ((0, k_hbm), (1, v_hbm))
    ]
    for c in pair:
        c.start()

    first = [
        remote(src.at[:, pl.ds(col, D)], kv.at[4, n, pl.ds(erow, T), :], fx_s.at[m + n], fx_r.at[m + n], dev(wrap(x + 1), y, zt))
        for m, col, zt in ((0, erow, z), (2, prow, zp))
        for n, src in ((0, k_hbm), (1, v_hbm))
    ]

    @pl.when(x < 3)
    def _():
        for c in first:
            c.start()

    def gathered(src_of, buf, s, r_):
        copies = []
        for r in (1, 2, 3):
            zt = wrap(z + r)
            copies.append(remote(src_of(zt), buf.at[z], s.at[r - 1], r_.at[r - 1], dev(x, y, zt)))
        return copies

    qcopies = gathered(
        lambda zt: q_hbm.at[:, pl.ds(pl.multiple_of(lax.rem(zt, 2) * 256, 256), 256)], qg, q_s, q_r
    )
    for c in qcopies:
        c.start()

    c_wo.wait()
    c_cot.wait()
    grad = lax.dot_general(cot[...], wo[...], NT, preferred_element_type=F32).astype(BF16)
    og[0] = grad[:, :256]
    og[1] = grad[:, 256:]
    docopies = gathered(lambda zt: og.at[lax.rem(zt, 2)], dog, do_s, do_r)
    for c in docopies:
        c.start()
    dog[z] = og[e]

    c_k.wait()
    c_v.wait()
    for c in pair:
        c.wait_recv()

    def fwd_x(src, dst):
        return remote(kv.at[src], kv.at[dst], kvx_s.at[dst // 8], kv_r.at[dst], dev(wrap(x + 1), y, z))

    def fwd_y(r, kind):
        yt = wrap(y + r)
        up = yt > y
        if kind == 0:
            src, dst = 4, 4 + yt - y
        else:
            src, dst = jnp.where(up, 0, 8), jnp.where(up, yt - y, 8 + yt - y)
        return remote(kv.at[src], kv.at[dst], kvy_s.at[kind * 3 + r - 1], kv_r.at[dst], dev(x, yt, z))

    for r in (1, 2, 3):
        @pl.when(y + r < 4)
        def _():
            fwd_y(r, 1).start()

    def recv_slot(d):
        remote(kv.at[d], kv.at[d], kvx_s.at[0], kv_r.at[d], dev(wrap(x + 1), y, z)).wait_recv()

    @pl.when(x >= 1)
    def _():
        for c in first:
            c.wait_recv()
        for r in (1, 2, 3):
            fwd_y(r, 0).start()

    @pl.when((x >= 1) & (x < 3))
    def _():
        fwd_x(4, 8).start()

    wcopies = []
    for r in (1, 2, 3):
        xt = wrap(x + r)
        for n, src in ((0, x_hbm), (1, cot_hbm)):
            wcopies.append(
                remote(src.at[:, window(xt)], win.at[n, x], w_s.at[n, r - 1], w_r.at[n, r - 1], dev(xt, y, z))
            )

    c_q.wait()
    @pl.when(x >= 2)
    def _():
        recv_slot(8)

        @pl.when(y >= 1)
        def _():
            fwd_y(3, 1).start()

    for c in qcopies:
        c.wait_recv()

    @pl.loop(0, 4)
    def _(zz):
        for j in range(2):
            rows = pl.ds(pl.multiple_of(j * 512 + zz * T, T), T)
            qb = qg[zz, :, j * D : (j + 1) * D]
            q2[rows, :] = qb
            qT[:, rows] = qb.T

    st[...] = jnp.concatenate([jnp.full((1, ROWS), NEG, F32), jnp.zeros((7, ROWS), F32)], axis=0)
    oT[...] = jnp.zeros_like(oT)
    dqT[...] = jnp.zeros_like(dqT)

    def slot_of(kind, r):
        if kind == 0:
            return 4 + jnp.where(r <= y, r, r - 4)
        return jnp.where(r <= y, r, r + 4)

    quarters = [slice(c * 256, (c + 1) * 256) for c in range(4)]

    def scores(d, edge):
        kd = kv[d, 0]
        low = jnp.where(d == 0, 0, -100000)
        high = jnp.where(d == 8, 0, 100000)
        for c, cs in enumerate(quarters):
            s = dot(kd, qT[:, cs])
            if edge:
                gap = (
                    lax.broadcasted_iota(jnp.int32, (KEYS, 256), 1)
                    - lax.broadcasted_iota(jnp.int32, (KEYS, 256), 0)
                    + ((c % 2) * 256 - f * 256)
                )
                s = jnp.where((gap >= low) & (gap < high), s, NEG)
            sbuf[d, :, cs] = s
            ms[d, 0:1, cs] = jnp.max(s, axis=0, keepdims=True)

    def probabilities(d):
        vd = kv[d, 1]
        vt = vd.T
        for cs in quarters:
            dpbuf[d, :, cs] = dot(vd, doT[:, cs])
        for cs in quarters:
            before = st[0:1, cs]
            top = jnp.maximum(before, ms[d, 0:1, cs])
            p = jnp.exp2((sbuf[d, :, cs] - top) * EXP2_SCALE)
            keep = jnp.exp2((before - top) * EXP2_SCALE)
            st[0:1, cs] = top
            st[1:2, cs] = st[1:2, cs] * keep + jnp.sum(p, axis=0, keepdims=True)
            st[2:3, cs] = st[2:3, cs] * keep + jnp.sum(p * dpbuf[d, :, cs], axis=0, keepdims=True)
            ms[d, 0:1, cs] = top
            sbuf[d, :, cs] = p
            pb_s[:, cs] = p.astype(BF16)
            oT[:, cs] = oT[:, cs] * keep + dot(vt, pb_s[:, cs])

    def order(t):
        kind = (t >= 5) & (t < 8)
        r = jnp.where(t < 4, t, jnp.where(t < 8, t - 4, t - 8))
        d = jnp.where(r == 0, t, jnp.where(kind, slot_of(0, r), slot_of(1, r)))
        fits = (S >= d) & ((r == 0) | kind | jnp.where(t < 4, r <= y, r > y))
        return d, r, fits

    def pass_on(r, d):
        return remote(kv.at[d], kv.at[r + 4], xw_s.at[r - 1], kv_r.at[r + 4], dev(wrap(x + 1), y, z))

    def score_step(t):
        d, r, fits = order(t)

        @pl.when(fits & ((t == 0) | (t == 8)))
        def _():
            scores(d, True)

        @pl.when(fits & (t != 0) & (t != 8))
        def _():
            @pl.when(r > 0)
            def _():
                recv_slot(d)

            @pl.when((t >= 5) & (t < 7) & (r > y) & (x < 3))
            def _():
                pass_on(r, d).start()

            scores(d, False)

    def prob_step(t):
        d, r, fits = order(t)

        @pl.when(fits)
        def _():
            probabilities(d)

    pl.loop(0, 8)(score_step)

    for c in docopies:
        c.wait_recv()
    for c in c_win + c_w:
        c.start()

    @pl.when(x >= 2)
    def _():
        for c in wcopies:
            c.start()


    @pl.loop(0, 4)
    def _(zz):
        for j in range(2):
            rows = pl.ds(pl.multiple_of(j * 512 + zz * T, T), T)
            db = dog[zz, :, j * D : (j + 1) * D]
            do2[rows, :] = db
            doT[:, rows] = db.T

    pl.loop(0, 8)(prob_step)

    @pl.loop(8, 12)
    def _(t):
        score_step(t)
        prob_step(t)

    stat = remote(st, st_in, st_s, st_r, dev(x, y, wrap(z + 2)))
    stat.start()
    stat.wait()

    @pl.when(x < 2)
    def _():
        for c in wcopies:
            c.start()

    top = jnp.maximum(st[0:1, :], st_in[0:1, :])
    mine = jnp.exp2((st[0:1, :] - top) * EXP2_SCALE)
    other = jnp.exp2((st_in[0:1, :] - top) * EXP2_SCALE)
    inv = 1.0 / (st[1:2, :] * mine + st_in[1:2, :] * other)
    fin[0:1, :] = top
    fin[1:2, :] = inv
    fin[2:3, :] = (st[2:3, :] * mine + st_in[2:3, :] * other) * inv
    oT[...] = oT[...] * (mine * inv)

    def spread(srcT, factor, sendbuf, inbuf, s, r_):
        for j in range(2):
            for zz in range(4):
                piece = srcT[:, j * 512 + zz * T : j * 512 + (zz + 1) * T]
                sendbuf[zz, :, j * D : (j + 1) * D] = (piece * factor).T.astype(BF16)
        copies = []
        for r in (1, 2, 3):
            zt = wrap(z + r)
            copies.append(remote(sendbuf.at[zt], inbuf.at[z], s.at[r - 1], r_.at[r - 1], dev(x, y, zt)))
        for c in copies:
            c.start()
        inbuf[z] = sendbuf[z]
        return copies

    ocopies = spread(oT, 1.0, osend, oin, o_s, o_r)

    def grad_slot(d):
        w = jnp.exp2((ms[d, 0:1, :] - fin[0:1, :]) * EXP2_SCALE) * fin[1:2, :]
        kt = kv[d, 0].T
        for c in range(4):
            cs = slice(c * 256, (c + 1) * 256)
            p = sbuf[d, :, cs] * w[:, cs]
            pb_s[:, cs] = p.astype(BF16)
            ds = (p * (dpbuf[d, :, cs] - fin[2:3, cs])).astype(BF16)
            ds_s[:, cs] = ds
            dqT[:, cs] += dot(kt, ds)
        dkv[d, 0] = (LOGIT_SCALE * dot(ds_s[...], q2[...])).astype(BF16)
        dkv[d, 1] = dot(pb_s[...], do2[...]).astype(BF16)

    def back_y(kind, r):
        d = slot_of(kind, r)
        n = kind * 3 + r - 1
        return remote(dkv.at[d], rbuf.at[n], rb_s.at[n], rb_r.at[n], dev(x, wrap(y - r), z))

    def grad_step(t):
        kind = (t >= 4) & (t < 7)
        r = jnp.where(t < 3, t + 1, jnp.where(kind, t - 3, jnp.where((t >= 8) & (t < 11), t - 7, 0)))
        d = jnp.where(r == 0, jnp.where(t == 3, 8, jnp.where(t == 7, 4, 0)), jnp.where(kind, slot_of(0, r), slot_of(1, r)))
        fits = (r == 0) | kind | jnp.where(t < 3, r > y, r <= y)

        @pl.when((S >= d) & fits)
        def _():
            grad_slot(d)

            @pl.when(r > 0)
            def _():
                n = jnp.where(kind, r - 1, r + 2)
                remote(dkv.at[d], rbuf.at[n], rb_s.at[n], rb_r.at[n], dev(x, wrap(y - r), z)).start()

    pl.loop(0, 12)(grad_step)

    dqcopies = spread(dqT, LOGIT_SCALE, dqsend, dqin, dq_s, dq_r)

    def over_x(src, dst, s, r_):
        return [remote(src, dst, s.at[r - 1], r_.at[r - 1], dev(wrap(x + r), y, z)) for r in (1, 2, 3)]

    for c in ocopies:
        c.wait_recv()
    for n in range(2):
        attn_o[n] = (oin[n].astype(F32) + oin[n + 2].astype(F32)).astype(BF16)
    agcopies = over_x(attn_o, ag.at[:, x], ag_s, ag_r)
    for c in agcopies:
        c.start()
    ag[:, x] = attn_o[...]


    def recv_back(n):
        remote(rbuf.at[n], rbuf.at[n], rb_s.at[n], rb_r.at[n], dev(x, wrap(y + 1), z)).wait_recv()

    chain8, chain4 = (
        [
            remote(
                csend.at[m, :, pl.ds(row, T), :], cin.at[m, part], c_s.at[m, part], c_r.at[m, part], dev(wrap(x - 2 + m), y, zt)
            )
            for part, row, zt in ((0, erow, z), (1, prow, zp))
        ]
        for m in range(2)
    )

    @pl.when(x >= 2)
    def _():
        facc[...] = dkv[8].astype(F32)
        for r in (1, 2, 3):
            @pl.when(y + r >= 4)
            def _():
                recv_back(3 + r - 1)
                facc[...] += rbuf[3 + r - 1].astype(F32)

        csend[0] = facc[...].astype(BF16)
        for c in chain8:
            c.start()

    @pl.when(x >= 1)
    def _():
        facc[...] = dkv[4].astype(F32)
        for r in (1, 2, 3):
            recv_back(r - 1)
            facc[...] += rbuf[r - 1].astype(F32)
        csend[1] = facc[...].astype(BF16)
        for c in chain4:
            c.start()

    off = pl.multiple_of(64 * lax.rem(x, 2), 16)

    def over_y(src, buf, s, r_):
        copies = []
        for r in (1, 2, 3):
            yt = wrap(y + r)
            rows = pl.ds(pl.multiple_of(off + 144 * yt, 16), 144)
            copies.append(remote(src.at[rows, :], buf.at[r - 1], s.at[r - 1], r_.at[r - 1], dev(x, yt, z)))
        return copies

    facc[...] = dkv[0].astype(F32)
    for r in (1, 2, 3):
        @pl.when(y + r < 4)
        def _():
            recv_back(3 + r - 1)
            facc[...] += rbuf[3 + r - 1].astype(F32)

    finkv[...] = facc[:, pl.ds(prow, T), :].astype(BF16)
    swap = [remote(finkv, pin, f_s, f_r, dev(x, y, zp))]
    swap[0].start()

    for c in dqcopies:
        c.wait_recv()
    for n in range(2):
        gq_o[n] = (dqin[n].astype(F32) + dqin[n + 2].astype(F32)).astype(BF16)
    for c in c_w:
        c.wait()

    def wrows(hh):
        return pl.ds(pl.multiple_of(COLS * hh, 16), COLS)

    @pl.loop(0, 4)
    def _(hh):
        tq[hh] = sum(
            lax.dot_general(wq[wrows(hh), n * 256 : (n + 1) * 256], gq_o[n], NT, preferred_element_type=F32)
            for n in range(2)
        )

    for c in c_win:
        c.wait()
    for c in wcopies:
        c.wait_recv()

    @pl.loop(0, 4)
    def _(xx):
        for n in range(2):
            for b in range(WIN // 128):
                cols = slice(b * 128, (b + 1) * 128)
                winT[n, cols, pl.ds(pl.multiple_of(xx * T, T), T)] = win[n, xx, :, cols].T

    for c in agcopies:
        c.wait_recv()
    for n in range(2):
        po[:, n * 256 : (n + 1) * 256] = dot(winT[1], ag[n].reshape(4 * T, 256)).astype(BF16)
    yocopies = over_y(po, yo, yo_s, yo_r)
    for c in yocopies:
        c.start()

    swap[0].wait_recv()
    ggcopies = over_x(gv_o, gvg.at[:, x], gg_s, gg_r)
    for m, chain in enumerate((chain8, chain4)):
        @pl.when(x < 2 + m)
        def _():
            for c in chain:
                c.wait_recv()

    for n, out in ((1, gv_o), (0, gk_o)):
        parts = [facc[n, pl.ds(erow, T), :], pin[n].astype(F32)]
        for m in (0, 1):
            parts = [a + jnp.where(x < 2 + m, cin[m, part, n].astype(F32), 0.0) for part, a in enumerate(parts)]
        out[e] = parts[0].astype(BF16)
        out[1 - e] = parts[1].astype(BF16)
        if n == 1:
            for c in ggcopies:
                c.start()
    gvg[:, x] = gv_o[...]

    def terms(hh):
        acc = tq[hh]
        for n in range(2):
            acc = acc + lax.dot_general(wk[wrows(hh), n * D : (n + 1) * D], gk_o[n], NT, preferred_element_type=F32)
            acc = acc + lax.dot_general(wv[wrows(hh), n * D : (n + 1) * D], gv_o[n], NT, preferred_element_type=F32)
        return acc

    hzc = lax.rem(hc + 2, 4)
    tb[0] = terms(hzc).astype(BF16)
    far = remote(tb.at[0], hin.at[0], h_s.at[0], h_r.at[0], (i, hc))
    far.start()
    mine_far = terms(hz)
    far.wait_recv()
    tb[1] = (mine_far + hin[0].astype(F32)).astype(BF16)
    across = remote(tb.at[1], hin.at[1], h_s.at[1], h_r.at[1], (i, hz))
    across.start()
    for c in ggcopies:
        c.wait_recv()
    for n in range(2):
        pv[:, n * D : (n + 1) * D] = dot(winT[0], gvg[n].reshape(4 * T, D)).astype(BF16)
    yvcopies = over_y(pv, yv, yv_s, yv_r)
    for c in yvcopies:
        c.start()

    tb[2] = terms(hc).astype(BF16)
    near = remote(tb.at[2], hin.at[2], h_s.at[2], h_r.at[2], (i, hc))
    near.start()

    def over_z(copies, own, buf, total_s, piece_s, in_s, s, r_):
        for c in copies:
            c.wait_recv()
        acc = own[pl.ds(pl.multiple_of(off + 144 * y, 16), 144), :].astype(F32)
        for r in range(3):
            acc = acc + buf[r].astype(F32)
        total_s[...] = acc
        for zz in range(4):
            piece_s[zz] = total_s[36 * zz : 36 * (zz + 1), :].astype(piece_s.dtype)
        out = []
        for r in (1, 2, 3):
            zt = wrap(z + r)
            out.append(remote(piece_s.at[zt], in_s.at[r - 1], s.at[r - 1], r_.at[r - 1], dev(x, y, zt)))
        for c in out:
            c.start()
        return out

    zocopies = over_z(yocopies, po, yo, zso, zpo, zio, zo_s, zo_r)
    mine_near = terms(h)
    zvcopies = over_z(yvcopies, pv, yv, zsv, zpv, ziv, zv_s, zv_r)

    for c in zocopies:
        c.wait_recv()
    acc = zpo[z].astype(F32)
    for r in range(3):
        acc = acc + zio[r].astype(F32)
    gwo_o[...] = acc
    results = [
        pltpu.make_async_copy(src, dst, res_s.at[n])
        for n, (src, dst) in enumerate(((gi_o, gi_h), (gwv_o, gwv_h), (gwo_o, gwo_h)))
    ]
    results[2].start()
    near.wait_recv()
    across.wait_recv()
    gi_o[...] = (mine_near + hin[2].astype(F32) + hin[1].astype(F32)).astype(BF16)
    results[0].start()
    for c in zvcopies:
        c.wait_recv()
    acc = zpv[z].astype(F32)
    for r in range(3):
        acc = acc + ziv[r].astype(F32)
    gwv_o[...] = acc

    results[1].start()
    for c in results:
        c.wait()

    for c in (
        pair + qcopies + docopies + ocopies + dqcopies + swap + wcopies + agcopies + ggcopies
        + yocopies + yvcopies + zocopies + zvcopies + [far, across, near]
    ):
        c.wait_send()

    @pl.when(x < 3)
    def _():
        for c in first:
            c.wait_send()

    @pl.when((x >= 1) & (x < 3))
    def _():
        fwd_x(4, 8).wait_send()

    for r in (1, 2, 3):
        @pl.when((y + r < 4) | ((x >= 2) & (r == 3)))
        def _():
            fwd_y(r, 1).wait_send()

        if r < 3:
            @pl.when((r > y) & (x >= 1) & (x < 3))
            def _():
                pass_on(r, slot_of(0, r)).wait_send()

        @pl.when(x >= 1)
        def _():
            fwd_y(r, 0).wait_send()
            back_y(0, r).wait_send()

        @pl.when((r <= y) | (x >= 2))
        def _():
            back_y(1, r).wait_send()

    @pl.when(x >= 2)
    def _():
        for c in chain8:
            c.wait_send()

    @pl.when(x >= 1)
    def _():
        for c in chain4:
            c.wait_send()


def layer(xn, q, k, v, wq, wk, wv, wo, cot):
    dma = pltpu.SemaphoreType.DMA
    vm = pltpu.VMEM
    return pl.pallas_call(
        layer_kernel,
        out_shape=(
            jax.ShapeDtypeStruct((COLS, T), BF16),
            jax.ShapeDtypeStruct((36, 256), F32),
            jax.ShapeDtypeStruct((36, 512), F32),
        ),
        in_specs=[pl.BlockSpec(memory_space=pl.ANY)] * 9,
        out_specs=tuple(pl.BlockSpec(memory_space=pl.ANY) for _ in range(3)),
        scratch_shapes=[
            vm((COLS, T), BF16),
            vm((36, 256), F32),
            vm((36, 512), F32),
            dma((3,)),
            vm((2, T, 256), BF16),
            vm((2, T, 256), BF16),
            vm((2, T, D), BF16),
            vm((2, T, D), BF16),
            vm(wq.shape, BF16),
            vm(wk.shape, BF16),
            vm(wv.shape, BF16),
            vm((2, 4, T, WIN), BF16),
            vm((2, WIN, 4 * T), BF16),
            vm((2, 4, T, 256), BF16),
            vm((2, 4, T, D), BF16),
            vm((WIN, 512), BF16),
            vm((WIN, 256), BF16),
            vm((3, 144, 512), BF16),
            vm((3, 144, 256), BF16),
            vm((144, 512), F32),
            vm((144, 256), F32),
            vm((4, 36, 512), BF16),
            vm((4, 36, 256), BF16),
            vm((3, 36, 512), BF16),
            vm((3, 36, 256), BF16),
            vm((3, COLS, T), BF16),
            vm((3, COLS, T), BF16),
            vm((4, COLS, T), F32),
            vm((2, KEYS, D), F32),
            vm((SLOTS, 2, KEYS, D), BF16),
            vm((4, T, 256), BF16),
            vm((4, T, 256), BF16),
            vm((2, T, 256), BF16),
            vm(cot.shape, BF16),
            vm(wo.shape, BF16),
            vm((ROWS, D), BF16),
            vm((ROWS, D), BF16),
            vm((D, ROWS), BF16),
            vm((D, ROWS), BF16),
            vm((SLOTS, KEYS, ROWS), F32),
            vm((SLOTS, KEYS, ROWS), F32),
            vm((KEYS, ROWS), BF16),
            vm((KEYS, ROWS), BF16),
            vm((SLOTS, 8, ROWS), F32),
            vm((8, ROWS), F32),
            vm((8, ROWS), F32),
            vm((8, ROWS), F32),
            vm((D, ROWS), F32),
            vm((D, ROWS), F32),
            vm((4, T, 256), BF16),
            vm((4, T, 256), BF16),
            vm((4, T, 256), BF16),
            vm((4, T, 256), BF16),
            vm((SLOTS, 2, KEYS, D), BF16),
            vm((6, 2, KEYS, D), BF16),
            vm((2, 2, KEYS, D), BF16),
            vm((2, 2, 2, T, D), BF16),
            vm((2, T, D), BF16),
            vm((2, T, D), BF16),
            dma((10,)), dma((2,)), dma((2,)), dma((3,)), dma((3,)), dma((3,)), dma((3,)),
            dma((2,)), dma((6,)), dma((SLOTS,)), dma, dma, dma((3,)), dma((3,)), dma((3,)), dma((3,)),
            dma((6,)), dma((6,)), dma((2, 2)), dma((2, 2)), dma, dma,
            dma((2,)), dma((4,)), dma((4,)), dma((2, 3)), dma((2, 3)), *([dma((3,))] * 2), *([dma((3,))] * 2), *([dma((3,))] * 10),
        ],
        compiler_params=pltpu.CompilerParams(
            collective_id=1, has_side_effects=True, vmem_limit_bytes=62 * 1024 * 1024,
        ),
        name="layer",
    )(xn, q, k, v, wq, wk, wv, wo, cot)


def hand_over(*refs):
    into = [pltpu.make_async_copy(refs[n], refs[6 + n], refs[9].at[n]) for n in range(3)]
    out = [pltpu.make_async_copy(refs[6 + n], refs[3 + n], refs[9].at[3 + n]) for n in range(3)]
    for c in into:
        c.start()
    for n in range(3):
        into[n].wait()
        out[n].start()
    for c in out:
        c.wait()


def local(*args):
    results = layer(*args)
    hbm = tuple(pl.BlockSpec(memory_space=pl.ANY) for _ in range(3))
    grad_input, grad_wvalue, grad_woutput = pl.pallas_call(
        hand_over,
        out_shape=tuple(jax.ShapeDtypeStruct(a.shape, a.dtype) for a in results),
        in_specs=hbm,
        out_specs=hbm,
        scratch_shapes=[pltpu.VMEM(a.shape, a.dtype) for a in results] + [pltpu.SemaphoreType.DMA((6,))],
        name="hand_over",
    )(*results)
    return grad_input.T, grad_wvalue, grad_woutput.T


def solution(mesh):
    seq, both, cols, rows = P("seq", None), P("seq", "head"), P(None, "head"), P("head", None)
    return jax.shard_map(
        local,
        mesh=mesh,
        in_specs=(seq, both, both, both, cols, cols, cols, rows, seq),
        out_specs=(both, both, P("head", "seq")),
        check_vma=False,
    )
```

```python
import functools
import math

import jax
import jax.numpy as jnp
from jax import lax
from jax.experimental import pallas as pl
from jax.experimental.pallas import tpu as pltpu
from jax.sharding import PartitionSpec as P

MESH = pl.DeviceIdType.MESH
F32 = jnp.float32
BF16 = jnp.bfloat16
LOGIT_SCALE = 1.0 / 12.0
EXP2_SCALE = LOGIT_SCALE * math.log2(math.e)
NEG = -1e30
T = 128
D = 128
SLOTS = 9
ROWS = 1024
WIN = 640
COLS = 576
KEYS = 256
NT = (((1,), (1,)), ((), ()))


def dot(a, b):
    return jnp.dot(a, b, preferred_element_type=F32)


def place():
    i = lax.axis_index("seq")
    h = lax.axis_index("head")
    x = lax.div(i, 16)
    y = lax.rem(lax.div(i, 4), 4)
    z = lax.rem(i, 4)
    return i, h, x, y, z


def layer_kernel(
    x_hbm, q_hbm, k_hbm, v_hbm, wq_hbm, wk_hbm, wv_hbm, wo_hbm, cot_hbm,
    gi_h, gwv_h, gwo_h, gi_o, gwv_o, gwo_o, res_s,
    attn_o, gq_o, gk_o, gv_o, wq, wk, wv, win, winT, ag, gvg, po, pv, yo, yv, zso, zsv, zpo, zpv, zio, ziv, tb, hin,
    tq, facc, kv, qg, dog, og, cot, wo, q2, do2, qT, doT, sbuf, dpbuf, pb_s, ds_s, ms, st, st_in, fin,
    oT, dqT, osend, oin, dqsend, dqin, dkv, rbuf, csend, cin, finkv, pin,
    lsem, pair_s, pair_r, q_s, q_r, do_s, do_r, kvx_s, kvy_s, kv_r, st_s, st_r, o_s, o_r, dq_s, dq_r,
    rb_s, rb_r, c_s, c_r, f_s, f_r,
    xw_s, fx_s, fx_r, w_s, w_r, ag_s, ag_r, gg_s, gg_r, yo_s, yo_r, yv_s, yv_r, zo_s, zo_r, zv_s, zv_r, h_s, h_r,
):
    i, h, x, y, z = place()
    e, f = lax.rem(z, 2), lax.div(z, 2)
    S = x * 4 + y

    def dev(x_, y_, z_):
        return (x_ * 16 + y_ * 4 + z_, h)

    def wrap(a):
        return lax.rem(a + 4, 4)

    def remote(src, dst, s, r, to):
        return pltpu.make_async_remote_copy(
            src_ref=src, dst_ref=dst, send_sem=s, recv_sem=r, device_id=to, device_id_type=MESH
        )

    erow = pl.multiple_of(e * T, T)
    prow = pl.multiple_of((1 - e) * T, T)
    ecol2 = pl.multiple_of(e * 256, 256)
    c_wo = pltpu.make_async_copy(wo_hbm, wo, lsem.at[0])
    c_cot = pltpu.make_async_copy(cot_hbm, cot, lsem.at[1])
    c_k = pltpu.make_async_copy(k_hbm.at[:, pl.ds(erow, D)], kv.at[0, 0, pl.ds(erow, T), :], lsem.at[2])
    c_v = pltpu.make_async_copy(v_hbm.at[:, pl.ds(erow, D)], kv.at[0, 1, pl.ds(erow, T), :], lsem.at[3])
    c_q = pltpu.make_async_copy(q_hbm.at[:, pl.ds(ecol2, 256)], qg.at[z], lsem.at[4])
    for c in (c_wo, c_cot, c_k, c_v, c_q):
        c.start()

    def window(xt):
        return pl.ds(pl.multiple_of(lax.div(9 * xt, 2) * 128, 128), WIN)

    c_win = [
        pltpu.make_async_copy(src.at[:, window(x)], win.at[n, x], lsem.at[5 + n]) for n, src in ((0, x_hbm), (1, cot_hbm))
    ]
    c_w = [pltpu.make_async_copy(src, dst, lsem.at[7 + n]) for n, (src, dst) in enumerate(((wq_hbm, wq), (wk_hbm, wk), (wv_hbm, wv)))]

    bar = pltpu.get_barrier_semaphore()
    for r in (1, 2, 3):
        for to in (dev(x, y, wrap(z + r)), dev(x, wrap(y + r), z), dev(wrap(x + r), y, z)):
            pl.semaphore_signal(bar, inc=1, device_id=to, device_id_type=MESH)
    hc = h + 1 - 2 * lax.rem(h, 2)
    hz = lax.rem(h + 2, 4)
    for to in ((i, hc), (i, hz)):
        pl.semaphore_signal(bar, inc=1, device_id=to, device_id_type=MESH)
    zp = z + 1 - 2 * e
    for r in (1, 2, 3):
        pl.semaphore_signal(bar, inc=1, device_id=dev(wrap(x + r), y, zp), device_id_type=MESH)
    pl.semaphore_wait(bar, 14)

    pair = [
        remote(src.at[:, pl.ds(prow, D)], kv.at[0, n, pl.ds(erow, T), :], pair_s.at[n], pair_r.at[n], dev(x, y, zp))
        for n, src in ((0, k_hbm), (1, v_hbm))
    ]
    for c in pair:
        c.start()

    first = [
        remote(src.at[:, pl.ds(col, D)], kv.at[4, n, pl.ds(erow, T), :], fx_s.at[m + n], fx_r.at[m + n], dev(wrap(x + 1), y, zt))
        for m, col, zt in ((0, erow, z), (2, prow, zp))
        for n, src in ((0, k_hbm), (1, v_hbm))
    ]

    @pl.when(x < 3)
    def _():
        for c in first:
            c.start()

    def gathered(src_of, buf, s, r_):
        copies = []
        for r in (1, 2, 3):
            zt = wrap(z + r)
            copies.append(remote(src_of(zt), buf.at[z], s.at[r - 1], r_.at[r - 1], dev(x, y, zt)))
        return copies

    qcopies = gathered(
        lambda zt: q_hbm.at[:, pl.ds(pl.multiple_of(lax.rem(zt, 2) * 256, 256), 256)], qg, q_s, q_r
    )
    for c in qcopies:
        c.start()

    c_wo.wait()
    c_cot.wait()
    grad = lax.dot_general(cot[...], wo[...], NT, preferred_element_type=F32).astype(BF16)
    og[0] = grad[:, :256]
    og[1] = grad[:, 256:]
    docopies = gathered(lambda zt: og.at[lax.rem(zt, 2)], dog, do_s, do_r)
    for c in docopies:
        c.start()
    dog[z] = og[e]

    c_k.wait()
    c_v.wait()
    for c in pair:
        c.wait_recv()

    def fwd_x(src, dst):
        return remote(kv.at[src], kv.at[dst], kvx_s.at[dst // 8], kv_r.at[dst], dev(wrap(x + 1), y, z))

    def fwd_y(r, kind):
        yt = wrap(y + r)
        up = yt > y
        if kind == 0:
            src, dst = 4, 4 + yt - y
        else:
            src, dst = jnp.where(up, 0, 8), jnp.where(up, yt - y, 8 + yt - y)
        return remote(kv.at[src], kv.at[dst], kvy_s.at[kind * 3 + r - 1], kv_r.at[dst], dev(x, yt, z))

    for r in (1, 2, 3):
        @pl.when(y + r < 4)
        def _():
            fwd_y(r, 1).start()

    def recv_slot(d):
        remote(kv.at[d], kv.at[d], kvx_s.at[0], kv_r.at[d], dev(wrap(x + 1), y, z)).wait_recv()

    @pl.when(x >= 1)
    def _():
        for c in first:
            c.wait_recv()
        for r in (1, 2, 3):
            fwd_y(r, 0).start()

    @pl.when((x >= 1) & (x < 3))
    def _():
        fwd_x(4, 8).start()

    xcopies, ccopies = (
        [
            remote(src.at[:, window(wrap(x + r))], win.at[n, x], w_s.at[n, r - 1], w_r.at[n, r - 1], dev(wrap(x + r), y, z))
            for r in (1, 2, 3)
        ]
        for n, src in ((0, x_hbm), (1, cot_hbm))
    )

    c_q.wait()
    @pl.when(x >= 2)
    def _():
        recv_slot(8)

        @pl.when(y >= 1)
        def _():
            fwd_y(3, 1).start()

    for c in qcopies:
        c.wait_recv()

    @pl.loop(0, 4)
    def _(zz):
        for j in range(2):
            rows = pl.ds(pl.multiple_of(j * 512 + zz * T, T), T)
            qb = qg[zz, :, j * D : (j + 1) * D]
            q2[rows, :] = qb
            qT[:, rows] = qb.T

    st[...] = jnp.concatenate([jnp.full((1, ROWS), NEG, F32), jnp.zeros((7, ROWS), F32)], axis=0)
    oT[...] = jnp.zeros_like(oT)
    dqT[...] = jnp.zeros_like(dqT)

    def slot_of(kind, r):
        if kind == 0:
            return 4 + jnp.where(r <= y, r, r - 4)
        return jnp.where(r <= y, r, r + 4)

    quarters = [slice(c * 256, (c + 1) * 256) for c in range(4)]

    def scores(d, edge):
        kd = kv[d, 0]
        low = jnp.where(d == 0, 0, -100000)
        high = jnp.where(d == 8, 0, 100000)
        for c, cs in enumerate(quarters):
            s = dot(kd, qT[:, cs])
            if edge:
                gap = (
                    lax.broadcasted_iota(jnp.int32, (KEYS, 256), 1)
                    - lax.broadcasted_iota(jnp.int32, (KEYS, 256), 0)
                    + ((c % 2) * 256 - f * 256)
                )
                s = jnp.where((gap >= low) & (gap < high), s, NEG)
            sbuf[d, :, cs] = s
            ms[d, 0:1, cs] = jnp.max(s, axis=0, keepdims=True)

    def probabilities(d):
        vd = kv[d, 1]
        vt = vd.T
        for cs in quarters:
            dpbuf[d, :, cs] = dot(vd, doT[:, cs])
        for cs in quarters:
            before = st[0:1, cs]
            top = jnp.maximum(before, ms[d, 0:1, cs])
            p = jnp.exp2((sbuf[d, :, cs] - top) * EXP2_SCALE)
            keep = jnp.exp2((before - top) * EXP2_SCALE)
            st[0:1, cs] = top
            st[1:2, cs] = st[1:2, cs] * keep + jnp.sum(p, axis=0, keepdims=True)
            st[2:3, cs] = st[2:3, cs] * keep + jnp.sum(p * dpbuf[d, :, cs], axis=0, keepdims=True)
            ms[d, 0:1, cs] = top
            sbuf[d, :, cs] = p
            pb_s[:, cs] = p.astype(BF16)
            oT[:, cs] = oT[:, cs] * keep + dot(vt, pb_s[:, cs])

    def order(t):
        kind = (t >= 5) & (t < 8)
        r = jnp.where(t < 4, t, jnp.where(t < 8, t - 4, t - 8))
        d = jnp.where(r == 0, t, jnp.where(kind, slot_of(0, r), slot_of(1, r)))
        fits = (S >= d) & ((r == 0) | kind | jnp.where(t < 4, r <= y, r > y))
        return d, r, fits

    def pass_on(r, d):
        return remote(kv.at[d], kv.at[r + 4], xw_s.at[r - 1], kv_r.at[r + 4], dev(wrap(x + 1), y, z))

    def score_step(t):
        d, r, fits = order(t)

        @pl.when(fits & ((t == 0) | (t == 8)))
        def _():
            scores(d, True)

        @pl.when(fits & (t != 0) & (t != 8))
        def _():
            @pl.when(r > 0)
            def _():
                recv_slot(d)

            @pl.when((t >= 5) & (t < 7) & (r > y) & (x < 3))
            def _():
                pass_on(r, d).start()

            scores(d, False)

    def prob_step(t):
        d, r, fits = order(t)

        @pl.when(fits)
        def _():
            probabilities(d)

    pl.loop(0, 8)(score_step)

    for c in docopies:
        c.wait_recv()
    for c in c_win + c_w:
        c.start()

    @pl.when(x >= 2)
    def _():
        for c in ccopies:
            c.start()


    @pl.loop(0, 4)
    def _(zz):
        for j in range(2):
            rows = pl.ds(pl.multiple_of(j * 512 + zz * T, T), T)
            db = dog[zz, :, j * D : (j + 1) * D]
            do2[rows, :] = db
            doT[:, rows] = db.T

    pl.loop(0, 8)(prob_step)

    @pl.loop(8, 12)
    def _(t):
        score_step(t)
        prob_step(t)

    stat = remote(st, st_in, st_s, st_r, dev(x, y, wrap(z + 2)))
    stat.start()
    stat.wait()

    @pl.when(x < 2)
    def _():
        for c in ccopies:
            c.start()

    for c in xcopies:
        c.start()

    top = jnp.maximum(st[0:1, :], st_in[0:1, :])
    mine = jnp.exp2((st[0:1, :] - top) * EXP2_SCALE)
    other = jnp.exp2((st_in[0:1, :] - top) * EXP2_SCALE)
    inv = 1.0 / (st[1:2, :] * mine + st_in[1:2, :] * other)
    fin[0:1, :] = top
    fin[1:2, :] = inv
    fin[2:3, :] = (st[2:3, :] * mine + st_in[2:3, :] * other) * inv
    oT[...] = oT[...] * (mine * inv)

    def spread(srcT, factor, sendbuf, inbuf, s, r_):
        for j in range(2):
            for zz in range(4):
                piece = srcT[:, j * 512 + zz * T : j * 512 + (zz + 1) * T]
                sendbuf[zz, :, j * D : (j + 1) * D] = (piece * factor).T.astype(BF16)
        copies = []
        for r in (1, 2, 3):
            zt = wrap(z + r)
            copies.append(remote(sendbuf.at[zt], inbuf.at[z], s.at[r - 1], r_.at[r - 1], dev(x, y, zt)))
        for c in copies:
            c.start()
        inbuf[z] = sendbuf[z]
        return copies

    ocopies = spread(oT, 1.0, osend, oin, o_s, o_r)

    def grad_slot(d):
        w = jnp.exp2((ms[d, 0:1, :] - fin[0:1, :]) * EXP2_SCALE) * fin[1:2, :]
        kt = kv[d, 0].T
        for c in range(4):
            cs = slice(c * 256, (c + 1) * 256)
            p = sbuf[d, :, cs] * w[:, cs]
            pb_s[:, cs] = p.astype(BF16)
            ds = (p * (dpbuf[d, :, cs] - fin[2:3, cs])).astype(BF16)
            ds_s[:, cs] = ds
            dqT[:, cs] += dot(kt, ds)
        dkv[d, 0] = (LOGIT_SCALE * dot(ds_s[...], q2[...])).astype(BF16)
        dkv[d, 1] = dot(pb_s[...], do2[...]).astype(BF16)

    def back_y(kind, r):
        d = slot_of(kind, r)
        n = kind * 3 + r - 1
        return remote(dkv.at[d], rbuf.at[n], rb_s.at[n], rb_r.at[n], dev(x, wrap(y - r), z))

    def grad_step(t):
        kind = (t >= 4) & (t < 7)
        r = jnp.where(t < 3, t + 1, jnp.where(kind, t - 3, jnp.where((t >= 8) & (t < 11), t - 7, 0)))
        d = jnp.where(r == 0, jnp.where(t == 3, 8, jnp.where(t == 7, 4, 0)), jnp.where(kind, slot_of(0, r), slot_of(1, r)))
        fits = (r == 0) | kind | jnp.where(t < 3, r > y, r <= y)

        @pl.when((S >= d) & fits)
        def _():
            grad_slot(d)

            @pl.when(r > 0)
            def _():
                n = jnp.where(kind, r - 1, r + 2)
                remote(dkv.at[d], rbuf.at[n], rb_s.at[n], rb_r.at[n], dev(x, wrap(y - r), z)).start()

    pl.loop(0, 12)(grad_step)

    dqcopies = spread(dqT, LOGIT_SCALE, dqsend, dqin, dq_s, dq_r)

    def over_x(src, dst, s, r_):
        return [remote(src, dst, s.at[r - 1], r_.at[r - 1], dev(wrap(x + r), y, z)) for r in (1, 2, 3)]

    for c in ocopies:
        c.wait_recv()
    for n in range(2):
        attn_o[n] = (oin[n].astype(F32) + oin[n + 2].astype(F32)).astype(BF16)
    agcopies = over_x(attn_o, ag.at[:, x], ag_s, ag_r)
    for c in agcopies:
        c.start()
    ag[:, x] = attn_o[...]


    def recv_back(n):
        remote(rbuf.at[n], rbuf.at[n], rb_s.at[n], rb_r.at[n], dev(x, wrap(y + 1), z)).wait_recv()

    chain8, chain4 = (
        [
            remote(
                csend.at[m, :, pl.ds(row, T), :], cin.at[m, part], c_s.at[m, part], c_r.at[m, part], dev(wrap(x - 2 + m), y, zt)
            )
            for part, row, zt in ((0, erow, z), (1, prow, zp))
        ]
        for m in range(2)
    )

    @pl.when(x >= 2)
    def _():
        facc[...] = dkv[8].astype(F32)
        for r in (1, 2, 3):
            @pl.when(y + r >= 4)
            def _():
                recv_back(3 + r - 1)
                facc[...] += rbuf[3 + r - 1].astype(F32)

        csend[0] = facc[...].astype(BF16)
        for c in chain8:
            c.start()

    @pl.when(x >= 1)
    def _():
        facc[...] = dkv[4].astype(F32)
        for r in (1, 2, 3):
            recv_back(r - 1)
            facc[...] += rbuf[r - 1].astype(F32)
        csend[1] = facc[...].astype(BF16)
        for c in chain4:
            c.start()

    off = pl.multiple_of(64 * lax.rem(x, 2), 16)

    def over_y(src, buf, s, r_):
        copies = []
        for r in (1, 2, 3):
            yt = wrap(y + r)
            rows = pl.ds(pl.multiple_of(off + 144 * yt, 16), 144)
            copies.append(remote(src.at[rows, :], buf.at[r - 1], s.at[r - 1], r_.at[r - 1], dev(x, yt, z)))
        return copies

    facc[...] = dkv[0].astype(F32)
    for r in (1, 2, 3):
        @pl.when(y + r < 4)
        def _():
            recv_back(3 + r - 1)
            facc[...] += rbuf[3 + r - 1].astype(F32)

    finkv[...] = facc[:, pl.ds(prow, T), :].astype(BF16)
    swap = [remote(finkv, pin, f_s, f_r, dev(x, y, zp))]
    swap[0].start()

    for c in dqcopies:
        c.wait_recv()
    for n in range(2):
        gq_o[n] = (dqin[n].astype(F32) + dqin[n + 2].astype(F32)).astype(BF16)
    for c in c_w:
        c.wait()

    def wrows(hh):
        return pl.ds(pl.multiple_of(COLS * hh, 16), COLS)

    @pl.loop(0, 4)
    def _(hh):
        tq[hh] = sum(
            lax.dot_general(wq[wrows(hh), n * 256 : (n + 1) * 256], gq_o[n], NT, preferred_element_type=F32)
            for n in range(2)
        )

    swap[0].wait_recv()
    ggcopies = over_x(gv_o, gvg.at[:, x], gg_s, gg_r)
    for m, chain in enumerate((chain8, chain4)):
        @pl.when(x < 2 + m)
        def _():
            for c in chain:
                c.wait_recv()

    for n, out in ((1, gv_o), (0, gk_o)):
        parts = [facc[n, pl.ds(erow, T), :], pin[n].astype(F32)]
        for m in (0, 1):
            parts = [a + jnp.where(x < 2 + m, cin[m, part, n].astype(F32), 0.0) for part, a in enumerate(parts)]
        out[e] = parts[0].astype(BF16)
        out[1 - e] = parts[1].astype(BF16)
        if n == 1:
            for c in ggcopies:
                c.start()
    gvg[:, x] = gv_o[...]

    def terms(hh):
        acc = tq[hh]
        for n in range(2):
            acc = acc + lax.dot_general(wk[wrows(hh), n * D : (n + 1) * D], gk_o[n], NT, preferred_element_type=F32)
            acc = acc + lax.dot_general(wv[wrows(hh), n * D : (n + 1) * D], gv_o[n], NT, preferred_element_type=F32)
        return acc

    hzc = lax.rem(hc + 2, 4)
    tb[0] = terms(hzc).astype(BF16)
    far = remote(tb.at[0], hin.at[0], h_s.at[0], h_r.at[0], (i, hc))
    far.start()

    def turn(n, copies):
        c_win[n].wait()
        for c in copies:
            c.wait_recv()

        @pl.loop(0, 4)
        def _(xx):
            for b in range(WIN // 128):
                cols = slice(b * 128, (b + 1) * 128)
                winT[n, cols, pl.ds(pl.multiple_of(xx * T, T), T)] = win[n, xx, :, cols].T

    turn(1, ccopies)
    for c in agcopies:
        c.wait_recv()
    for n in range(2):
        po[:, n * 256 : (n + 1) * 256] = dot(winT[1], ag[n].reshape(4 * T, 256)).astype(BF16)
    yocopies = over_y(po, yo, yo_s, yo_r)
    for c in yocopies:
        c.start()

    mine_far = terms(hz)
    far.wait_recv()
    tb[1] = (mine_far + hin[0].astype(F32)).astype(BF16)
    across = remote(tb.at[1], hin.at[1], h_s.at[1], h_r.at[1], (i, hz))
    across.start()
    turn(0, xcopies)
    for c in ggcopies:
        c.wait_recv()
    for n in range(2):
        pv[:, n * D : (n + 1) * D] = dot(winT[0], gvg[n].reshape(4 * T, D)).astype(BF16)
    yvcopies = over_y(pv, yv, yv_s, yv_r)
    for c in yvcopies:
        c.start()

    tb[2] = terms(hc).astype(BF16)
    near = remote(tb.at[2], hin.at[2], h_s.at[2], h_r.at[2], (i, hc))
    near.start()

    def over_z(copies, own, buf, total_s, piece_s, in_s, s, r_):
        for c in copies:
            c.wait_recv()
        acc = own[pl.ds(pl.multiple_of(off + 144 * y, 16), 144), :].astype(F32)
        for r in range(3):
            acc = acc + buf[r].astype(F32)
        total_s[...] = acc
        for zz in range(4):
            piece_s[zz] = total_s[36 * zz : 36 * (zz + 1), :].astype(piece_s.dtype)
        out = []
        for r in (1, 2, 3):
            zt = wrap(z + r)
            out.append(remote(piece_s.at[zt], in_s.at[r - 1], s.at[r - 1], r_.at[r - 1], dev(x, y, zt)))
        for c in out:
            c.start()
        return out

    zocopies = over_z(yocopies, po, yo, zso, zpo, zio, zo_s, zo_r)
    mine_near = terms(h)
    zvcopies = over_z(yvcopies, pv, yv, zsv, zpv, ziv, zv_s, zv_r)

    for c in zocopies:
        c.wait_recv()
    acc = zpo[z].astype(F32)
    for r in range(3):
        acc = acc + zio[r].astype(F32)
    gwo_o[...] = acc
    results = [
        pltpu.make_async_copy(src, dst, res_s.at[n])
        for n, (src, dst) in enumerate(((gi_o, gi_h), (gwv_o, gwv_h), (gwo_o, gwo_h)))
    ]
    results[2].start()
    near.wait_recv()
    across.wait_recv()
    gi_o[...] = (mine_near + hin[2].astype(F32) + hin[1].astype(F32)).astype(BF16)
    results[0].start()
    for c in zvcopies:
        c.wait_recv()
    acc = zpv[z].astype(F32)
    for r in range(3):
        acc = acc + ziv[r].astype(F32)
    gwv_o[...] = acc

    results[1].start()
    for c in results:
        c.wait()

    for c in (
        pair + qcopies + docopies + ocopies + dqcopies + swap + xcopies + ccopies + agcopies + ggcopies
        + yocopies + yvcopies + zocopies + zvcopies + [far, across, near]
    ):
        c.wait_send()

    @pl.when(x < 3)
    def _():
        for c in first:
            c.wait_send()

    @pl.when((x >= 1) & (x < 3))
    def _():
        fwd_x(4, 8).wait_send()

    for r in (1, 2, 3):
        @pl.when((y + r < 4) | ((x >= 2) & (r == 3)))
        def _():
            fwd_y(r, 1).wait_send()

        if r < 3:
            @pl.when((r > y) & (x >= 1) & (x < 3))
            def _():
                pass_on(r, slot_of(0, r)).wait_send()

        @pl.when(x >= 1)
        def _():
            fwd_y(r, 0).wait_send()
            back_y(0, r).wait_send()

        @pl.when((r <= y) | (x >= 2))
        def _():
            back_y(1, r).wait_send()

    @pl.when(x >= 2)
    def _():
        for c in chain8:
            c.wait_send()

    @pl.when(x >= 1)
    def _():
        for c in chain4:
            c.wait_send()


def layer(xn, q, k, v, wq, wk, wv, wo, cot):
    dma = pltpu.SemaphoreType.DMA
    vm = pltpu.VMEM
    return pl.pallas_call(
        layer_kernel,
        out_shape=(
            jax.ShapeDtypeStruct((COLS, T), BF16),
            jax.ShapeDtypeStruct((36, 256), F32),
            jax.ShapeDtypeStruct((36, 512), F32),
        ),
        in_specs=[pl.BlockSpec(memory_space=pl.ANY)] * 9,
        out_specs=tuple(pl.BlockSpec(memory_space=pl.ANY) for _ in range(3)),
        scratch_shapes=[
            vm((COLS, T), BF16),
            vm((36, 256), F32),
            vm((36, 512), F32),
            dma((3,)),
            vm((2, T, 256), BF16),
            vm((2, T, 256), BF16),
            vm((2, T, D), BF16),
            vm((2, T, D), BF16),
            vm(wq.shape, BF16),
            vm(wk.shape, BF16),
            vm(wv.shape, BF16),
            vm((2, 4, T, WIN), BF16),
            vm((2, WIN, 4 * T), BF16),
            vm((2, 4, T, 256), BF16),
            vm((2, 4, T, D), BF16),
            vm((WIN, 512), BF16),
            vm((WIN, 256), BF16),
            vm((3, 144, 512), BF16),
            vm((3, 144, 256), BF16),
            vm((144, 512), F32),
            vm((144, 256), F32),
            vm((4, 36, 512), BF16),
            vm((4, 36, 256), BF16),
            vm((3, 36, 512), BF16),
            vm((3, 36, 256), BF16),
            vm((3, COLS, T), BF16),
            vm((3, COLS, T), BF16),
            vm((4, COLS, T), F32),
            vm((2, KEYS, D), F32),
            vm((SLOTS, 2, KEYS, D), BF16),
            vm((4, T, 256), BF16),
            vm((4, T, 256), BF16),
            vm((2, T, 256), BF16),
            vm(cot.shape, BF16),
            vm(wo.shape, BF16),
            vm((ROWS, D), BF16),
            vm((ROWS, D), BF16),
            vm((D, ROWS), BF16),
            vm((D, ROWS), BF16),
            vm((SLOTS, KEYS, ROWS), F32),
            vm((SLOTS, KEYS, ROWS), F32),
            vm((KEYS, ROWS), BF16),
            vm((KEYS, ROWS), BF16),
            vm((SLOTS, 8, ROWS), F32),
            vm((8, ROWS), F32),
            vm((8, ROWS), F32),
            vm((8, ROWS), F32),
            vm((D, ROWS), F32),
            vm((D, ROWS), F32),
            vm((4, T, 256), BF16),
            vm((4, T, 256), BF16),
            vm((4, T, 256), BF16),
            vm((4, T, 256), BF16),
            vm((SLOTS, 2, KEYS, D), BF16),
            vm((6, 2, KEYS, D), BF16),
            vm((2, 2, KEYS, D), BF16),
            vm((2, 2, 2, T, D), BF16),
            vm((2, T, D), BF16),
            vm((2, T, D), BF16),
            dma((10,)), dma((2,)), dma((2,)), dma((3,)), dma((3,)), dma((3,)), dma((3,)),
            dma((2,)), dma((6,)), dma((SLOTS,)), dma, dma, dma((3,)), dma((3,)), dma((3,)), dma((3,)),
            dma((6,)), dma((6,)), dma((2, 2)), dma((2, 2)), dma, dma,
            dma((2,)), dma((4,)), dma((4,)), dma((2, 3)), dma((2, 3)), *([dma((3,))] * 2), *([dma((3,))] * 2), *([dma((3,))] * 10),
        ],
        compiler_params=pltpu.CompilerParams(
            collective_id=1, has_side_effects=True, vmem_limit_bytes=62 * 1024 * 1024,
        ),
        name="layer",
    )(xn, q, k, v, wq, wk, wv, wo, cot)


def hand_over(*refs):
    into = [pltpu.make_async_copy(refs[n], refs[6 + n], refs[9].at[n]) for n in range(3)]
    out = [pltpu.make_async_copy(refs[6 + n], refs[3 + n], refs[9].at[3 + n]) for n in range(3)]
    for c in into:
        c.start()
    for n in range(3):
        into[n].wait()
        out[n].start()
    for c in out:
        c.wait()


def local(*args):
    results = layer(*args)
    hbm = tuple(pl.BlockSpec(memory_space=pl.ANY) for _ in range(3))
    grad_input, grad_wvalue, grad_woutput = pl.pallas_call(
        hand_over,
        out_shape=tuple(jax.ShapeDtypeStruct(a.shape, a.dtype) for a in results),
        in_specs=hbm,
        out_specs=hbm,
        scratch_shapes=[pltpu.VMEM(a.shape, a.dtype) for a in results] + [pltpu.SemaphoreType.DMA((6,))],
        name="hand_over",
    )(*results)
    return grad_input.T, grad_wvalue, grad_woutput.T


def solution(mesh):
    seq, both, cols, rows = P("seq", None), P("seq", "head"), P(None, "head"), P("head", None)
    return jax.shard_map(
        local,
        mesh=mesh,
        in_specs=(seq, both, both, both, cols, cols, cols, rows, seq),
        out_specs=(both, both, P("head", "seq")),
        check_vma=False,
    )
```

```python
import functools
import math

import jax
import jax.numpy as jnp
from jax import lax
from jax.experimental import pallas as pl
from jax.experimental.pallas import tpu as pltpu
from jax.sharding import PartitionSpec as P

MESH = pl.DeviceIdType.MESH
F32 = jnp.float32
BF16 = jnp.bfloat16
LOGIT_SCALE = 1.0 / 12.0
EXP2_SCALE = LOGIT_SCALE * math.log2(math.e)
NEG = -1e30
T = 128
D = 128
SLOTS = 9
ROWS = 1024
WIN = 640
COLS = 576
KEYS = 256
NT = (((1,), (1,)), ((), ()))


def dot(a, b):
    return jnp.dot(a, b, preferred_element_type=F32)


def place():
    i = lax.axis_index("seq")
    h = lax.axis_index("head")
    x = lax.div(i, 16)
    y = lax.rem(lax.div(i, 4), 4)
    z = lax.rem(i, 4)
    return i, h, x, y, z


def layer_kernel(
    x_hbm, q_hbm, k_hbm, v_hbm, wq_hbm, wk_hbm, wv_hbm, wo_hbm, cot_hbm,
    gi_h, gwv_h, gwo_h, gi_o, gwv_o, gwo_o, res_s,
    attn_o, gq_o, gk_o, gv_o, wq, wk, wv, win, winT, ag, gvg, po, pv, yo, yv, zso, zsv, zpo, zpv, zio, ziv, tb, hin,
    tq, facc, kv, qg, dog, og, cot, wo, q2, do2, qT, doT, sbuf, dpbuf, pb_s, ds_s, ms, st, st_in, fin,
    oT, dqT, osend, oin, dqsend, dqin, dkv, rbuf, csend, cin, finkv, pin,
    lsem, pair_s, pair_r, q_s, q_r, do_s, do_r, kvx_s, kvy_s, kv_r, st_s, st_r, o_s, o_r, dq_s, dq_r,
    rb_s, rb_r, c_s, c_r, f_s, f_r,
    xw_s, fx_s, fx_r, w_s, w_r, ag_s, ag_r, gg_s, gg_r, yo_s, yo_r, yv_s, yv_r, zo_s, zo_r, zv_s, zv_r, h_s, h_r,
):
    i, h, x, y, z = place()
    e, f = lax.rem(z, 2), lax.div(z, 2)
    S = x * 4 + y

    def dev(x_, y_, z_):
        return (x_ * 16 + y_ * 4 + z_, h)

    def wrap(a):
        return lax.rem(a + 4, 4)

    def remote(src, dst, s, r, to):
        return pltpu.make_async_remote_copy(
            src_ref=src, dst_ref=dst, send_sem=s, recv_sem=r, device_id=to, device_id_type=MESH
        )

    erow = pl.multiple_of(e * T, T)
    prow = pl.multiple_of((1 - e) * T, T)
    ecol2 = pl.multiple_of(e * 256, 256)
    c_wo = pltpu.make_async_copy(wo_hbm, wo, lsem.at[0])
    c_cot = pltpu.make_async_copy(cot_hbm, cot, lsem.at[1])
    c_k = pltpu.make_async_copy(k_hbm.at[:, pl.ds(erow, D)], kv.at[0, 0, pl.ds(erow, T), :], lsem.at[2])
    c_v = pltpu.make_async_copy(v_hbm.at[:, pl.ds(erow, D)], kv.at[0, 1, pl.ds(erow, T), :], lsem.at[3])
    c_q = pltpu.make_async_copy(q_hbm.at[:, pl.ds(ecol2, 256)], qg.at[z], lsem.at[4])
    for c in (c_wo, c_cot, c_k, c_v, c_q):
        c.start()

    def window(xt):
        return pl.ds(pl.multiple_of(lax.div(9 * xt, 2) * 128, 128), WIN)

    c_win = [
        pltpu.make_async_copy(src.at[:, window(x)], win.at[n, x], lsem.at[5 + n]) for n, src in ((0, x_hbm), (1, cot_hbm))
    ]
    c_w = [pltpu.make_async_copy(src, dst, lsem.at[7 + n]) for n, (src, dst) in enumerate(((wq_hbm, wq), (wk_hbm, wk), (wv_hbm, wv)))]

    bar = pltpu.get_barrier_semaphore()
    for r in (1, 2, 3):
        for to in (dev(x, y, wrap(z + r)), dev(x, wrap(y + r), z), dev(wrap(x + r), y, z)):
            pl.semaphore_signal(bar, inc=1, device_id=to, device_id_type=MESH)
    hc = h + 1 - 2 * lax.rem(h, 2)
    hz = lax.rem(h + 2, 4)
    for to in ((i, hc), (i, hz)):
        pl.semaphore_signal(bar, inc=1, device_id=to, device_id_type=MESH)
    zp = z + 1 - 2 * e
    for r in (1, 2, 3):
        pl.semaphore_signal(bar, inc=1, device_id=dev(wrap(x + r), y, zp), device_id_type=MESH)
    pl.semaphore_wait(bar, 14)

    pair = [
        remote(src.at[:, pl.ds(prow, D)], kv.at[0, n, pl.ds(erow, T), :], pair_s.at[n], pair_r.at[n], dev(x, y, zp))
        for n, src in ((0, k_hbm), (1, v_hbm))
    ]
    for c in pair:
        c.start()

    first = [
        remote(src.at[:, pl.ds(col, D)], kv.at[4, n, pl.ds(erow, T), :], fx_s.at[m + n], fx_r.at[m + n], dev(wrap(x + 1), y, zt))
        for m, col, zt in ((0, erow, z), (2, prow, zp))
        for n, src in ((0, k_hbm), (1, v_hbm))
    ]

    @pl.when(x < 3)
    def _():
        for c in first:
            c.start()

    def gathered(src_of, buf, s, r_):
        copies = []
        for r in (1, 2, 3):
            zt = wrap(z + r)
            copies.append(remote(src_of(zt), buf.at[z], s.at[r - 1], r_.at[r - 1], dev(x, y, zt)))
        return copies

    qcopies = gathered(
        lambda zt: q_hbm.at[:, pl.ds(pl.multiple_of(lax.rem(zt, 2) * 256, 256), 256)], qg, q_s, q_r
    )
    for c in qcopies:
        c.start()

    c_wo.wait()
    c_cot.wait()
    grad = lax.dot_general(cot[...], wo[...], NT, preferred_element_type=F32).astype(BF16)
    og[0] = grad[:, :256]
    og[1] = grad[:, 256:]
    docopies = gathered(lambda zt: og.at[lax.rem(zt, 2)], dog, do_s, do_r)
    for c in docopies:
        c.start()
    dog[z] = og[e]

    c_k.wait()
    c_v.wait()
    for c in pair:
        c.wait_recv()

    def fwd_x(src, dst):
        return remote(kv.at[src], kv.at[dst], kvx_s.at[dst // 8], kv_r.at[dst], dev(wrap(x + 1), y, z))

    def fwd_y(r, kind):
        yt = wrap(y + r)
        up = yt > y
        if kind == 0:
            src, dst = 4, 4 + yt - y
        else:
            src, dst = jnp.where(up, 0, 8), jnp.where(up, yt - y, 8 + yt - y)
        return remote(kv.at[src], kv.at[dst], kvy_s.at[kind * 3 + r - 1], kv_r.at[dst], dev(x, yt, z))

    for r in (1, 2, 3):
        @pl.when(y + r < 4)
        def _():
            fwd_y(r, 1).start()

    def recv_slot(d):
        remote(kv.at[d], kv.at[d], kvx_s.at[0], kv_r.at[d], dev(wrap(x + 1), y, z)).wait_recv()

    @pl.when(x >= 1)
    def _():
        for c in first:
            c.wait_recv()
        for r in (1, 2, 3):
            fwd_y(r, 0).start()

    @pl.when((x >= 1) & (x < 3))
    def _():
        fwd_x(4, 8).start()

    xcopies, ccopies = (
        [
            remote(src.at[:, window(wrap(x + r))], win.at[n, x], w_s.at[n, r - 1], w_r.at[n, r - 1], dev(wrap(x + r), y, z))
            for r in (1, 2, 3)
        ]
        for n, src in ((0, x_hbm), (1, cot_hbm))
    )

    c_q.wait()
    @pl.when(x >= 2)
    def _():
        recv_slot(8)

        @pl.when(y >= 1)
        def _():
            fwd_y(3, 1).start()

    for c in qcopies:
        c.wait_recv()

    @pl.loop(0, 4)
    def _(zz):
        for j in range(2):
            rows = pl.ds(pl.multiple_of(j * 512 + zz * T, T), T)
            qb = qg[zz, :, j * D : (j + 1) * D]
            q2[rows, :] = qb
            qT[:, rows] = qb.T

    st[...] = jnp.concatenate([jnp.full((1, ROWS), NEG, F32), jnp.zeros((7, ROWS), F32)], axis=0)
    oT[...] = jnp.zeros_like(oT)
    dqT[...] = jnp.zeros_like(dqT)

    def slot_of(kind, r):
        if kind == 0:
            return 4 + jnp.where(r <= y, r, r - 4)
        return jnp.where(r <= y, r, r + 4)

    quarters = [slice(c * 256, (c + 1) * 256) for c in range(4)]

    def scores(d, edge):
        kd = kv[d, 0]
        low = jnp.where(d == 0, 0, -100000)
        high = jnp.where(d == 8, 0, 100000)
        for c, cs in enumerate(quarters):
            s = dot(kd, qT[:, cs])
            if edge:
                gap = (
                    lax.broadcasted_iota(jnp.int32, (KEYS, 256), 1)
                    - lax.broadcasted_iota(jnp.int32, (KEYS, 256), 0)
                    + ((c % 2) * 256 - f * 256)
                )
                s = jnp.where((gap >= low) & (gap < high), s, NEG)
            sbuf[d, :, cs] = s
            ms[d, 0:1, cs] = jnp.max(s, axis=0, keepdims=True)

    def probabilities(d):
        vd = kv[d, 1]
        vt = vd.T
        for cs in quarters:
            dpbuf[d, :, cs] = dot(vd, doT[:, cs])
        for cs in quarters:
            before = st[0:1, cs]
            top = jnp.maximum(before, ms[d, 0:1, cs])
            p = jnp.exp2((sbuf[d, :, cs] - top) * EXP2_SCALE)
            keep = jnp.exp2((before - top) * EXP2_SCALE)
            st[0:1, cs] = top
            st[1:2, cs] = st[1:2, cs] * keep + jnp.sum(p, axis=0, keepdims=True)
            st[2:3, cs] = st[2:3, cs] * keep + jnp.sum(p * dpbuf[d, :, cs], axis=0, keepdims=True)
            ms[d, 0:1, cs] = top
            sbuf[d, :, cs] = p
            pb_s[:, cs] = p.astype(BF16)
            oT[:, cs] = oT[:, cs] * keep + dot(vt, pb_s[:, cs])

    def order(t):
        kind = (t >= 5) & (t < 8)
        r = jnp.where(t < 4, t, jnp.where(t < 8, t - 4, t - 8))
        d = jnp.where(r == 0, t, jnp.where(kind, slot_of(0, r), slot_of(1, r)))
        fits = (S >= d) & ((r == 0) | kind | jnp.where(t < 4, r <= y, r > y))
        return d, r, fits

    def pass_on(r, d):
        return remote(kv.at[d], kv.at[r + 4], xw_s.at[r - 1], kv_r.at[r + 4], dev(wrap(x + 1), y, z))

    def score_step(t):
        d, r, fits = order(t)

        @pl.when(fits & ((t == 0) | (t == 8)))
        def _():
            scores(d, True)

        @pl.when(fits & (t != 0) & (t != 8))
        def _():
            @pl.when(r > 0)
            def _():
                recv_slot(d)

            @pl.when((t >= 5) & (t < 7) & (r > y) & (x < 3))
            def _():
                pass_on(r, d).start()

            scores(d, False)

    def prob_step(t):
        d, r, fits = order(t)

        @pl.when(fits)
        def _():
            probabilities(d)

    pl.loop(0, 8)(score_step)

    for c in docopies:
        c.wait_recv()
    for c in c_win + c_w:
        c.start()

    @pl.when(x >= 2)
    def _():
        for c in ccopies + xcopies:
            c.start()


    @pl.loop(0, 4)
    def _(zz):
        for j in range(2):
            rows = pl.ds(pl.multiple_of(j * 512 + zz * T, T), T)
            db = dog[zz, :, j * D : (j + 1) * D]
            do2[rows, :] = db
            doT[:, rows] = db.T

    pl.loop(0, 8)(prob_step)

    @pl.loop(8, 12)
    def _(t):
        score_step(t)
        prob_step(t)

    stat = remote(st, st_in, st_s, st_r, dev(x, y, wrap(z + 2)))
    stat.start()
    stat.wait()

    @pl.when(x < 2)
    def _():
        for c in ccopies + xcopies:
            c.start()

    top = jnp.maximum(st[0:1, :], st_in[0:1, :])
    mine = jnp.exp2((st[0:1, :] - top) * EXP2_SCALE)
    other = jnp.exp2((st_in[0:1, :] - top) * EXP2_SCALE)
    inv = 1.0 / (st[1:2, :] * mine + st_in[1:2, :] * other)
    fin[0:1, :] = top
    fin[1:2, :] = inv
    fin[2:3, :] = (st[2:3, :] * mine + st_in[2:3, :] * other) * inv
    oT[...] = oT[...] * (mine * inv)

    def spread(srcT, factor, sendbuf, inbuf, s, r_):
        for j in range(2):
            for zz in range(4):
                piece = srcT[:, j * 512 + zz * T : j * 512 + (zz + 1) * T]
                sendbuf[zz, :, j * D : (j + 1) * D] = (piece * factor).T.astype(BF16)
        copies = []
        for r in (1, 2, 3):
            zt = wrap(z + r)
            copies.append(remote(sendbuf.at[zt], inbuf.at[z], s.at[r - 1], r_.at[r - 1], dev(x, y, zt)))
        for c in copies:
            c.start()
        inbuf[z] = sendbuf[z]
        return copies

    ocopies = spread(oT, 1.0, osend, oin, o_s, o_r)

    def grad_slot(d):
        w = jnp.exp2((ms[d, 0:1, :] - fin[0:1, :]) * EXP2_SCALE) * fin[1:2, :]
        kt = kv[d, 0].T
        for c in range(4):
            cs = slice(c * 256, (c + 1) * 256)
            p = sbuf[d, :, cs] * w[:, cs]
            pb_s[:, cs] = p.astype(BF16)
            ds = (p * (dpbuf[d, :, cs] - fin[2:3, cs])).astype(BF16)
            ds_s[:, cs] = ds
            dqT[:, cs] += dot(kt, ds)
        dkv[d, 0] = (LOGIT_SCALE * dot(ds_s[...], q2[...])).astype(BF16)
        dkv[d, 1] = dot(pb_s[...], do2[...]).astype(BF16)

    def back_y(kind, r):
        d = slot_of(kind, r)
        n = kind * 3 + r - 1
        return remote(dkv.at[d], rbuf.at[n], rb_s.at[n], rb_r.at[n], dev(x, wrap(y - r), z))

    def grad_step(t):
        kind = (t >= 4) & (t < 7)
        r = jnp.where(t < 3, t + 1, jnp.where(kind, t - 3, jnp.where((t >= 8) & (t < 11), t - 7, 0)))
        d = jnp.where(r == 0, jnp.where(t == 3, 8, jnp.where(t == 7, 4, 0)), jnp.where(kind, slot_of(0, r), slot_of(1, r)))
        fits = (r == 0) | kind | jnp.where(t < 3, r > y, r <= y)

        @pl.when((S >= d) & fits)
        def _():
            grad_slot(d)

            @pl.when(r > 0)
            def _():
                n = jnp.where(kind, r - 1, r + 2)
                remote(dkv.at[d], rbuf.at[n], rb_s.at[n], rb_r.at[n], dev(x, wrap(y - r), z)).start()

    pl.loop(0, 12)(grad_step)

    dqcopies = spread(dqT, LOGIT_SCALE, dqsend, dqin, dq_s, dq_r)

    def over_x(src, dst, s, r_):
        return [remote(src, dst, s.at[r - 1], r_.at[r - 1], dev(wrap(x + r), y, z)) for r in (1, 2, 3)]

    for c in ocopies:
        c.wait_recv()
    for n in range(2):
        attn_o[n] = (oin[n].astype(F32) + oin[n + 2].astype(F32)).astype(BF16)
    agcopies = over_x(attn_o, ag.at[:, x], ag_s, ag_r)
    for c in agcopies:
        c.start()
    ag[:, x] = attn_o[...]


    def recv_back(n):
        remote(rbuf.at[n], rbuf.at[n], rb_s.at[n], rb_r.at[n], dev(x, wrap(y + 1), z)).wait_recv()

    chain8, chain4 = (
        [
            remote(
                csend.at[m, :, pl.ds(row, T), :], cin.at[m, part], c_s.at[m, part], c_r.at[m, part], dev(wrap(x - 2 + m), y, zt)
            )
            for part, row, zt in ((0, erow, z), (1, prow, zp))
        ]
        for m in range(2)
    )

    @pl.when(x >= 2)
    def _():
        facc[...] = dkv[8].astype(F32)
        for r in (1, 2, 3):
            @pl.when(y + r >= 4)
            def _():
                recv_back(3 + r - 1)
                facc[...] += rbuf[3 + r - 1].astype(F32)

        csend[0] = facc[...].astype(BF16)
        for c in chain8:
            c.start()

    @pl.when(x >= 1)
    def _():
        facc[...] = dkv[4].astype(F32)
        for r in (1, 2, 3):
            recv_back(r - 1)
            facc[...] += rbuf[r - 1].astype(F32)
        csend[1] = facc[...].astype(BF16)
        for c in chain4:
            c.start()

    off = pl.multiple_of(64 * lax.rem(x, 2), 16)

    def over_y(src, buf, s, r_):
        copies = []
        for r in (1, 2, 3):
            yt = wrap(y + r)
            rows = pl.ds(pl.multiple_of(off + 144 * yt, 16), 144)
            copies.append(remote(src.at[rows, :], buf.at[r - 1], s.at[r - 1], r_.at[r - 1], dev(x, yt, z)))
        return copies

    facc[...] = dkv[0].astype(F32)
    for r in (1, 2, 3):
        @pl.when(y + r < 4)
        def _():
            recv_back(3 + r - 1)
            facc[...] += rbuf[3 + r - 1].astype(F32)

    finkv[...] = facc[:, pl.ds(prow, T), :].astype(BF16)
    swap = [remote(finkv, pin, f_s, f_r, dev(x, y, zp))]
    swap[0].start()

    for c in dqcopies:
        c.wait_recv()
    for n in range(2):
        gq_o[n] = (dqin[n].astype(F32) + dqin[n + 2].astype(F32)).astype(BF16)
    for c in c_w:
        c.wait()

    def wrows(hh):
        return pl.ds(pl.multiple_of(COLS * hh, 16), COLS)

    @pl.loop(0, 4)
    def _(hh):
        tq[hh] = sum(
            lax.dot_general(wq[wrows(hh), n * 256 : (n + 1) * 256], gq_o[n], NT, preferred_element_type=F32)
            for n in range(2)
        )

    def turn(n, copies):
        c_win[n].wait()
        for c in copies:
            c.wait_recv()

        @pl.loop(0, 4)
        def _(xx):
            for b in range(WIN // 128):
                cols = slice(b * 128, (b + 1) * 128)
                winT[n, cols, pl.ds(pl.multiple_of(xx * T, T), T)] = win[n, xx, :, cols].T

    turn(1, ccopies)
    for c in agcopies:
        c.wait_recv()
    for n in range(2):
        po[:, n * 256 : (n + 1) * 256] = dot(winT[1], ag[n].reshape(4 * T, 256)).astype(BF16)
    yocopies = over_y(po, yo, yo_s, yo_r)
    for c in yocopies:
        c.start()

    swap[0].wait_recv()
    ggcopies = over_x(gv_o, gvg.at[:, x], gg_s, gg_r)
    for m, chain in enumerate((chain8, chain4)):
        @pl.when(x < 2 + m)
        def _():
            for c in chain:
                c.wait_recv()

    for n, out in ((1, gv_o), (0, gk_o)):
        parts = [facc[n, pl.ds(erow, T), :], pin[n].astype(F32)]
        for m in (0, 1):
            parts = [a + jnp.where(x < 2 + m, cin[m, part, n].astype(F32), 0.0) for part, a in enumerate(parts)]
        out[e] = parts[0].astype(BF16)
        out[1 - e] = parts[1].astype(BF16)
        if n == 1:
            for c in ggcopies:
                c.start()
    gvg[:, x] = gv_o[...]

    def terms(hh):
        acc = tq[hh]
        for n in range(2):
            acc = acc + lax.dot_general(wk[wrows(hh), n * D : (n + 1) * D], gk_o[n], NT, preferred_element_type=F32)
            acc = acc + lax.dot_general(wv[wrows(hh), n * D : (n + 1) * D], gv_o[n], NT, preferred_element_type=F32)
        return acc

    hzc = lax.rem(hc + 2, 4)
    tb[0] = terms(hzc).astype(BF16)
    far = remote(tb.at[0], hin.at[0], h_s.at[0], h_r.at[0], (i, hc))
    far.start()

    mine_far = terms(hz)
    far.wait_recv()
    tb[1] = (mine_far + hin[0].astype(F32)).astype(BF16)
    across = remote(tb.at[1], hin.at[1], h_s.at[1], h_r.at[1], (i, hz))
    across.start()
    turn(0, xcopies)
    for c in ggcopies:
        c.wait_recv()
    for n in range(2):
        pv[:, n * D : (n + 1) * D] = dot(winT[0], gvg[n].reshape(4 * T, D)).astype(BF16)
    yvcopies = over_y(pv, yv, yv_s, yv_r)
    for c in yvcopies:
        c.start()

    tb[2] = terms(hc).astype(BF16)
    near = remote(tb.at[2], hin.at[2], h_s.at[2], h_r.at[2], (i, hc))
    near.start()

    def over_z(copies, own, buf, total_s, piece_s, in_s, s, r_):
        for c in copies:
            c.wait_recv()
        acc = own[pl.ds(pl.multiple_of(off + 144 * y, 16), 144), :].astype(F32)
        for r in range(3):
            acc = acc + buf[r].astype(F32)
        total_s[...] = acc
        for zz in range(4):
            piece_s[zz] = total_s[36 * zz : 36 * (zz + 1), :].astype(piece_s.dtype)
        out = []
        for r in (1, 2, 3):
            zt = wrap(z + r)
            out.append(remote(piece_s.at[zt], in_s.at[r - 1], s.at[r - 1], r_.at[r - 1], dev(x, y, zt)))
        for c in out:
            c.start()
        return out

    zocopies = over_z(yocopies, po, yo, zso, zpo, zio, zo_s, zo_r)
    mine_near = terms(h)
    zvcopies = over_z(yvcopies, pv, yv, zsv, zpv, ziv, zv_s, zv_r)

    for c in zocopies:
        c.wait_recv()
    acc = zpo[z].astype(F32)
    for r in range(3):
        acc = acc + zio[r].astype(F32)
    gwo_o[...] = acc
    results = [
        pltpu.make_async_copy(src, dst, res_s.at[n])
        for n, (src, dst) in enumerate(((gi_o, gi_h), (gwv_o, gwv_h), (gwo_o, gwo_h)))
    ]
    results[2].start()
    near.wait_recv()
    across.wait_recv()
    gi_o[...] = (mine_near + hin[2].astype(F32) + hin[1].astype(F32)).astype(BF16)
    results[0].start()
    for c in zvcopies:
        c.wait_recv()
    acc = zpv[z].astype(F32)
    for r in range(3):
        acc = acc + ziv[r].astype(F32)
    gwv_o[...] = acc

    results[1].start()
    for c in results:
        c.wait()

    for c in (
        pair + qcopies + docopies + ocopies + dqcopies + swap + xcopies + ccopies + agcopies + ggcopies
        + yocopies + yvcopies + zocopies + zvcopies + [far, across, near]
    ):
        c.wait_send()

    @pl.when(x < 3)
    def _():
        for c in first:
            c.wait_send()

    @pl.when((x >= 1) & (x < 3))
    def _():
        fwd_x(4, 8).wait_send()

    for r in (1, 2, 3):
        @pl.when((y + r < 4) | ((x >= 2) & (r == 3)))
        def _():
            fwd_y(r, 1).wait_send()

        if r < 3:
            @pl.when((r > y) & (x >= 1) & (x < 3))
            def _():
                pass_on(r, slot_of(0, r)).wait_send()

        @pl.when(x >= 1)
        def _():
            fwd_y(r, 0).wait_send()
            back_y(0, r).wait_send()

        @pl.when((r <= y) | (x >= 2))
        def _():
            back_y(1, r).wait_send()

    @pl.when(x >= 2)
    def _():
        for c in chain8:
            c.wait_send()

    @pl.when(x >= 1)
    def _():
        for c in chain4:
            c.wait_send()


def layer(xn, q, k, v, wq, wk, wv, wo, cot):
    dma = pltpu.SemaphoreType.DMA
    vm = pltpu.VMEM
    return pl.pallas_call(
        layer_kernel,
        out_shape=(
            jax.ShapeDtypeStruct((COLS, T), BF16),
            jax.ShapeDtypeStruct((36, 256), F32),
            jax.ShapeDtypeStruct((36, 512), F32),
        ),
        in_specs=[pl.BlockSpec(memory_space=pl.ANY)] * 9,
        out_specs=tuple(pl.BlockSpec(memory_space=pl.ANY) for _ in range(3)),
        scratch_shapes=[
            vm((COLS, T), BF16),
            vm((36, 256), F32),
            vm((36, 512), F32),
            dma((3,)),
            vm((2, T, 256), BF16),
            vm((2, T, 256), BF16),
            vm((2, T, D), BF16),
            vm((2, T, D), BF16),
            vm(wq.shape, BF16),
            vm(wk.shape, BF16),
            vm(wv.shape, BF16),
            vm((2, 4, T, WIN), BF16),
            vm((2, WIN, 4 * T), BF16),
            vm((2, 4, T, 256), BF16),
            vm((2, 4, T, D), BF16),
            vm((WIN, 512), BF16),
            vm((WIN, 256), BF16),
            vm((3, 144, 512), BF16),
            vm((3, 144, 256), BF16),
            vm((144, 512), F32),
            vm((144, 256), F32),
            vm((4, 36, 512), BF16),
            vm((4, 36, 256), BF16),
            vm((3, 36, 512), BF16),
            vm((3, 36, 256), BF16),
            vm((3, COLS, T), BF16),
            vm((3, COLS, T), BF16),
            vm((4, COLS, T), F32),
            vm((2, KEYS, D), F32),
            vm((SLOTS, 2, KEYS, D), BF16),
            vm((4, T, 256), BF16),
            vm((4, T, 256), BF16),
            vm((2, T, 256), BF16),
            vm(cot.shape, BF16),
            vm(wo.shape, BF16),
            vm((ROWS, D), BF16),
            vm((ROWS, D), BF16),
            vm((D, ROWS), BF16),
            vm((D, ROWS), BF16),
            vm((SLOTS, KEYS, ROWS), F32),
            vm((SLOTS, KEYS, ROWS), F32),
            vm((KEYS, ROWS), BF16),
            vm((KEYS, ROWS), BF16),
            vm((SLOTS, 8, ROWS), F32),
            vm((8, ROWS), F32),
            vm((8, ROWS), F32),
            vm((8, ROWS), F32),
            vm((D, ROWS), F32),
            vm((D, ROWS), F32),
            vm((4, T, 256), BF16),
            vm((4, T, 256), BF16),
            vm((4, T, 256), BF16),
            vm((4, T, 256), BF16),
            vm((SLOTS, 2, KEYS, D), BF16),
            vm((6, 2, KEYS, D), BF16),
            vm((2, 2, KEYS, D), BF16),
            vm((2, 2, 2, T, D), BF16),
            vm((2, T, D), BF16),
            vm((2, T, D), BF16),
            dma((10,)), dma((2,)), dma((2,)), dma((3,)), dma((3,)), dma((3,)), dma((3,)),
            dma((2,)), dma((6,)), dma((SLOTS,)), dma, dma, dma((3,)), dma((3,)), dma((3,)), dma((3,)),
            dma((6,)), dma((6,)), dma((2, 2)), dma((2, 2)), dma, dma,
            dma((2,)), dma((4,)), dma((4,)), dma((2, 3)), dma((2, 3)), *([dma((3,))] * 2), *([dma((3,))] * 2), *([dma((3,))] * 10),
        ],
        compiler_params=pltpu.CompilerParams(
            collective_id=1, has_side_effects=True, vmem_limit_bytes=62 * 1024 * 1024,
        ),
        name="layer",
    )(xn, q, k, v, wq, wk, wv, wo, cot)


def hand_over(*refs):
    into = [pltpu.make_async_copy(refs[n], refs[6 + n], refs[9].at[n]) for n in range(3)]
    out = [pltpu.make_async_copy(refs[6 + n], refs[3 + n], refs[9].at[3 + n]) for n in range(3)]
    for c in into:
        c.start()
    for n in range(3):
        into[n].wait()
        out[n].start()
    for c in out:
        c.wait()


def local(*args):
    results = layer(*args)
    hbm = tuple(pl.BlockSpec(memory_space=pl.ANY) for _ in range(3))
    grad_input, grad_wvalue, grad_woutput = pl.pallas_call(
        hand_over,
        out_shape=tuple(jax.ShapeDtypeStruct(a.shape, a.dtype) for a in results),
        in_specs=hbm,
        out_specs=hbm,
        scratch_shapes=[pltpu.VMEM(a.shape, a.dtype) for a in results] + [pltpu.SemaphoreType.DMA((6,))],
        name="hand_over",
    )(*results)
    return grad_input.T, grad_wvalue, grad_woutput.T


def solution(mesh):
    seq, both, cols, rows = P("seq", None), P("seq", "head"), P(None, "head"), P("head", None)
    return jax.shard_map(
        local,
        mesh=mesh,
        in_specs=(seq, both, both, both, cols, cols, cols, rows, seq),
        out_specs=(both, both, P("head", "seq")),
        check_vma=False,
    )
```
